32 devices in a mesh: gx: 4 (over z), gy: 4 (over y, core), gz: 2 (over x).
Axes of the slice: x: 2, y: 2, z: 4, core: 2. Of those that a mesh axis runs over, the one named last changes fastest.
Arguments:
- charges: float32 [64, 64, 256], P('gx', 'gy', 'gz'), may hold values from -6 to 6
- exponents: float32 [2, 4], replicated, may hold values from 0.01 to 1
- amplitudes: float32 [2, 4], replicated, may hold values from 0.25 to 1
- top_x: float32 [4, 4], replicated, may hold values from -1.5 to 1.5
- top_y: float32 [4, 4], replicated, may hold values from -1.5 to 1.5
- top_z: float32 [16, 16], replicated, may hold values from -0.75 to 0.75
Outputs:
- potential: float32 [64, 64, 256], P('gx', 'gy', 'gz')
The draws below stay inside these ranges and needn't reach their ends.
All inputs are finite; a program needn't handle non-finite values.
Results may differ from the reference program's by a relative error of at most 0.0003.
Values sent between devices are 32-bit elements; how exact they have to be, the bound alone decides.
No kernel may reach another device: no remote copies, remote signals or barrier semaphores. Data moves between devices by JAX's collectives and lax.ppermute only.
A program may use at most 64 MiB of HBM per device.

```python
import math
import jax
import jax.numpy as jnp
from jax import lax

GAUSSIANS = 4
REACH = 8
NX = 64
NY = 64
NZ = 256
TX = 4
TY = 4
TZ = 16


def steps_of(stream_key, extent, cuts, smallest, largest):
    level, own = 1.0, jax.random.fold_in(stream_key, 6)
    for axis_at, blocks in cuts:
        steps = jnp.exp(jax.random.uniform(jax.random.fold_in(own, axis_at), (blocks,), jnp.float32, smallest / len(cuts), largest / len(cuts)))
        level = level * jnp.repeat(steps, extent[axis_at] // blocks).reshape([-1 if axis == axis_at else 1 for axis in range(len(extent))])
    return level


def normal_values(key, dims, spread, limit, cuts=(), kind=jnp.bfloat16):
    drawn = jax.random.normal(key, dims, jnp.float32) * spread
    if len(cuts) > 0:
        drawn = steps_of(key, dims, cuts, -0.22, 0.18) * drawn
    return jnp.clip(drawn, min=-limit, max=limit).astype(kind)


def setup_inputs(seed: int = 0) -> dict:
    keys = jax.random.split(jax.random.key(seed), 7)
    return {
        "charges": normal_values(keys[0], (NX, NY, NZ), 1.0, 6.0, ((0, 4), (1, 4), (2, 2)), jnp.float32),
        "exponents": jnp.clip(jnp.exp(jax.random.uniform(keys[1], (2, GAUSSIANS), jnp.float32, math.log(0.01), math.log(1.0))), 0.01, 1.0),
        "amplitudes": jnp.clip(jnp.exp(jax.random.uniform(keys[2], (2, GAUSSIANS), jnp.float32, math.log(0.25), math.log(1.0))), 0.25, 1.0),
        "top_x": normal_values(keys[3], (TX, TX), (4 * TX) ** -0.5, 1.5, (), jnp.float32),
        "top_y": normal_values(keys[4], (TY, TY), (4 * TY) ** -0.5, 1.5, (), jnp.float32),
        "top_z": normal_values(keys[5], (TZ, TZ), (4 * TZ) ** -0.5, 0.75, (), jnp.float32),
    }


HIGHEST = lax.Precision.HIGHEST


def gauss_taps(exponents):
    offsets = jnp.arange(-REACH, REACH + 1).astype(jnp.float32)
    weights = jnp.exp(-exponents[..., None] * offsets * offsets)
    return weights / jnp.sum(weights, axis=-1, keepdims=True)


def smooth_axis(field, tap_row, axis):
    summed = jnp.zeros_like(field)
    for offset in range(2 * REACH + 1):
        summed = summed + tap_row[offset] * jnp.roll(field, REACH - offset, axis)
    return summed


def gauss_term(field, tap_table, weights):
    summed = jnp.zeros_like(field)
    for term in range(GAUSSIANS):
        smoothed = smooth_axis(field, tap_table[term], 2)
        smoothed = smooth_axis(smoothed, tap_table[term], 1)
        smoothed = smooth_axis(smoothed, tap_table[term], 0)
        summed = summed + weights[term] * smoothed
    return summed


def restrict_axis(field, axis):
    length = field.shape[axis]
    summed = (jnp.roll(field, 1, axis) + 3.0 * field + 3.0 * jnp.roll(field, -1, axis) + jnp.roll(field, -2, axis)) * 0.25
    return lax.slice_in_dim(summed, 0, length, 2, axis)


def restrict_three(field):
    return restrict_axis(restrict_axis(restrict_axis(field, 0), 1), 2)


def prolong_axis(coarse, axis):
    even_cells = 0.75 * coarse + 0.25 * jnp.roll(coarse, 1, axis)
    odd_cells = 0.75 * coarse + 0.25 * jnp.roll(coarse, -1, axis)
    stacked = jnp.stack([even_cells, odd_cells], axis=axis + 1)
    sizes = list(coarse.shape)
    sizes[axis] = sizes[axis] * 2
    return stacked.reshape(sizes)


def prolong_three(field):
    return prolong_axis(prolong_axis(prolong_axis(field, 0), 1), 2)


def reference(charges, exponents, amplitudes, top_x, top_y, top_z):
    tap_table = gauss_taps(exponents)
    level_one = restrict_three(charges)
    level_two = restrict_three(level_one)
    level_three = restrict_three(level_two)
    level_four = restrict_three(level_three)
    phi_four = jnp.einsum('ia,abc->ibc', top_x, level_four, precision=HIGHEST)
    phi_four = jnp.einsum('jb,ibc->ijc', top_y, phi_four, precision=HIGHEST)
    phi_four = jnp.einsum('kc,ijc->ijk', top_z, phi_four, precision=HIGHEST)
    phi_two = prolong_three(prolong_three(phi_four))
    phi_one = gauss_term(level_one, tap_table[1], amplitudes[1]) + prolong_three(phi_two)
    return gauss_term(charges, tap_table[0], amplitudes[0]) + prolong_three(phi_one)
```

```python
import functools

import jax
import jax.numpy as jnp
import numpy as np
from jax import lax
from jax.experimental import pallas as pl
from jax.experimental.pallas import tpu as pltpu
from jax.sharding import PartitionSpec as P

REACH = 8


HIGHEST = lax.Precision.HIGHEST


def with_halo(cells, sides, width):
    for axis, dim in sides:
        count = lax.axis_size(axis)
        head = lax.slice_in_dim(cells, 0, width, axis=dim)
        tail = lax.slice_in_dim(cells, cells.shape[dim] - width, cells.shape[dim], axis=dim)
        cells = jnp.concatenate(
            [
                lax.ppermute(tail, axis, [(i, (i + 1) % count) for i in range(count)]),
                cells,
                lax.ppermute(head, axis, [((i + 1) % count, i) for i in range(count)]),
            ],
            axis=dim,
        )
    return cells


def gauss_taps(exponents):
    offsets = jnp.arange(-REACH, REACH + 1).astype(jnp.float32)
    weights = jnp.exp(-exponents[..., None] * offsets * offsets)
    return weights / jnp.sum(weights, axis=-1, keepdims=True)


def spline(offsets):
    inner_weight = jnp.where((offsets == 1) | (offsets == 2), 0.75, 0.0)
    return jnp.where((offsets == 0) | (offsets == 3), 0.25, inner_weight).astype(jnp.float32)


def band_gauss(tap_table, length):
    rows = jnp.arange(length + 2 * REACH)[:, None]
    cols = jnp.arange(length)[None, :]
    offsets = rows - cols
    onehot = (offsets[:, :, None] == jnp.arange(2 * REACH + 1)[None, None, :]).astype(jnp.float32)
    return jnp.einsum("gk,pok->gpo", tap_table, onehot, precision=HIGHEST)


def band_restrict(length):
    rows = jnp.arange(length + 2)[:, None]
    cols = jnp.arange(length // 2)[None, :]
    return spline(rows - 2 * cols)


def band_prolong(length):
    rows = jnp.arange(length + 2)[:, None]
    cols = jnp.arange(2 * length)[None, :]
    return spline(cols - 2 * rows + 3)


def apply_three(field, band_x, band_y, band_z):
    field = jnp.einsum("xyz,zc->xyc", field, band_z, precision=HIGHEST)
    field = jnp.einsum("xyz,yb->xbz", field, band_y, precision=HIGHEST)
    return jnp.einsum("xyz,xa->ayz", field, band_x, precision=HIGHEST)


def rim_cells(field):
    return with_halo(field, (("gx", 0), ("gy", 1), ("gz", 2)), 1)


def restrict_local(padded):
    sizes = padded.shape
    return apply_three(
        padded,
        band_restrict(sizes[0] - 2),
        band_restrict(sizes[1] - 2),
        band_restrict(sizes[2] - 2),
    )


def prolong_local(field):
    sizes = field.shape
    return apply_three(
        rim_cells(field), band_prolong(sizes[0]), band_prolong(sizes[1]), band_prolong(sizes[2])
    )


def prolong_from_whole(whole_grid, brick):
    padded = jnp.pad(whole_grid, 1, mode="wrap")
    starts = (
        lax.axis_index("gx") * brick[0],
        lax.axis_index("gy") * brick[1],
        lax.axis_index("gz") * brick[2],
    )
    piece_cells = lax.dynamic_slice(padded, starts, (brick[0] + 2, brick[1] + 2, brick[2] + 2))
    return apply_three(
        piece_cells, band_prolong(brick[0]), band_prolong(brick[1]), band_prolong(brick[2])
    )


def assemble(gathered, brick):
    count_x = lax.axis_size("gx")
    count_y = lax.axis_size("gy")
    count_z = lax.axis_size("gz")
    blocks = gathered.reshape(count_x, count_y, count_z, brick[0], brick[1], brick[2])
    blocks = jnp.transpose(blocks, (0, 3, 1, 4, 2, 5))
    return blocks.reshape(count_x * brick[0], count_y * brick[1], count_z * brick[2])


def top_level(field, top_x, top_y, top_z):
    field = jnp.einsum("ia,abc->ibc", top_x, field, precision=HIGHEST)
    field = jnp.einsum("jb,ibc->ijc", top_y, field, precision=HIGHEST)
    return jnp.einsum("kc,ijc->ijk", top_z, field, precision=HIGHEST)


def gauss_and_restrict(field, tap_table, weights):
    size_x, size_y, size_z = field.shape
    band_z = band_gauss(tap_table, size_z)
    band_y = band_gauss(tap_table, size_y)
    band_x = band_gauss(tap_table, size_x) * weights[:, None, None]
    padded = with_halo(field, (("gx", 0), ("gy", 1), ("gz", 2)), REACH)
    along_z = jnp.einsum("xyp,gpo->xygo", padded, band_z, precision=HIGHEST)
    along_y = jnp.einsum("xpgz,gpw->xgwz", along_z, band_y, precision=HIGHEST)
    result = jnp.einsum("pgwz,gpv->vwz", along_y, band_x, precision=HIGHEST)
    inner_cells = padded[
        REACH - 1 : size_x + REACH + 1,
        REACH - 1 : size_y + REACH + 1,
        REACH - 1 : size_z + REACH + 1,
    ]
    coarse = restrict_local(inner_cells)
    return (result, coarse)


def local_any(charges, exponents, amplitudes, top_x, top_y, top_z):
    tap_table = gauss_taps(exponents)
    term_zero, level_one = gauss_and_restrict(charges, tap_table[0], amplitudes[0])
    term_one, level_two = gauss_and_restrict(level_one, tap_table[1], amplitudes[1])
    level_three = restrict_local(rim_cells(level_two))
    level_four = restrict_local(rim_cells(level_three))
    brick_four = level_four.shape
    gathered = lax.all_gather(level_four.reshape(1, -1), ("gx", "gy", "gz"), axis=0, tiled=True)
    phi_four = top_level(assemble(gathered, brick_four), top_x, top_y, top_z)
    phi_three = prolong_from_whole(phi_four, brick_four)
    phi_two = prolong_local(phi_three)
    phi_one = term_one + prolong_local(phi_two)
    return term_zero + prolong_local(phi_one)


F32 = jnp.float32
BF16 = jnp.bfloat16
LANES = 128
FAR = 1.0e9
GAUSSIAN_RIM = REACH + 1


def up8(count):
    return -(-count // 8) * 8


def restrict_weights(fine, coarse):
    offsets = np.asarray(fine)[None, :] - 2 * np.asarray(coarse)[:, None] + 1
    inner = np.where((offsets == 1) | (offsets == 2), 0.75, 0.0)
    return np.where((offsets == 0) | (offsets == 3), 0.25, inner).astype(np.float32)


def reach_four(length):
    total, cells = np.eye(length, dtype=np.float32), np.arange(length)
    for level in range(1, 5):
        coarse = np.arange(-1, length // 2**level + 1)
        total = restrict_weights(cells, coarse) @ total
        cells = coarse
    return total


def prolong_three_whole(count):
    total = np.eye(count, dtype=np.float32)
    for level in range(3):
        size = count * 2**level
        step = np.zeros((2 * size, size), np.float32)
        for cell in range(size):
            for offset, weight in ((-1, 0.25), (0, 0.75), (1, 0.75), (2, 0.25)):
                step[(2 * cell + offset) % (2 * size), cell] += weight
        total = step @ total
    return total


def padded(table, rows, cols):
    out = np.zeros((rows, cols), np.float32)
    out[: table.shape[0], : table.shape[1]] = table
    return out


class Plan:
    def __init__(self, brick, counts):
        self.brick, self.counts = brick, counts
        bx, by, bz = brick
        self.half = by // 2
        self.rim = up8(2 * GAUSSIAN_RIM + 1)
        self.fine_rows = bz + 2 * REACH
        self.cx, self.cy = bx // 2 + 2, by // 2 + 2
        self.window = bz // 2 + 2 * GAUSSIAN_RIM
        self.window_rows = up8(self.window)
        self.out_z = bz // 2 + 2
        self.out_rows = up8(self.out_z)
        self.top_rows = 2 * up8(bz // 16 + 2)
        self.top_z = bz // 16 + 2
        self.top_x, self.top_y = bx // 16 + 2, by // 16 + 2
        self.group = 16
        x_of, y_of = self.own_cells()
        rz = reach_four(bz)
        self.top_left = padded(rz, self.top_rows // 2, bz)
        rx, ry = reach_four(bx), reach_four(by)
        self.top_right, self.rest_right = [], []
        sx = restrict_weights(np.arange(bx), np.arange(-1, bx // 2 + 1))
        sy = restrict_weights(np.arange(by), np.arange(-1, by // 2 + 1))
        for part in range(2):
            y = y_of + part * self.half
            table = rx[:, x_of][:, None, :] * ry[:, y][None, :, :]
            self.top_right.append(padded(table.reshape(-1, LANES).T, LANES, LANES))
            table = sx[:, x_of][:, None, :] * sy[:, y][None, :, :]
            self.rest_right.append(padded(table.reshape(-1, LANES).T, LANES, LANES))
        z_in = np.concatenate([np.arange(bz), bz + np.arange(self.rim), np.arange(-self.rim, 0)])
        z_out = np.arange(-GAUSSIAN_RIM, bz // 2 + GAUSSIAN_RIM)
        self.rest_left = padded(restrict_weights(z_in, z_out), self.window_rows, z_in.size)
        spread = restrict_weights(np.arange(bz), np.arange(-1, bz // 2 + 1)).T
        self.back_left = padded(spread, bz, self.out_rows)
        cols = []
        for part in range(2):
            y = y_of + part * self.half
            table = sx[:, x_of][:, None, :] * sy[:, y][None, :, :]
            cols.append(padded(table.reshape(-1, LANES), LANES, LANES))
        self.back_right = np.concatenate(cols, axis=1)
        self.message = self.fine_rows + self.window_rows + self.top_rows

    def own_cells(self):
        lane = np.arange(LANES)
        return lane // self.half, lane % self.half


def fits(brick, counts):
    bx, by, bz = brick
    return (
        counts == (4, 4, 2)
        and bx * (by // 2) == LANES
        and by % 16 == 0
        and bx % 16 == 0
        and bz == LANES
        and bx // 2 >= REACH
        and (bx // 2 + 4) * (by // 2 + 2) <= LANES
        and (bx // 16 + 2) * (by // 16 + 2) <= 16
    )


def split(value):
    high = value.astype(BF16)
    return high, (value - high.astype(F32)).astype(BF16)


def split_wide(value):
    high = lax.reduce_precision(value, 8, 7)
    return high.astype(BF16), (value - high).astype(BF16)


def dot(left, right):
    return jnp.dot(left, right, preferred_element_type=F32)


def dot_left(exact, value):
    high, low = split(value)
    return dot(exact, high) + dot(exact, low)


def dot_right(value, exact):
    high, low = split(value)
    return dot(high, exact) + dot(low, exact)


def dot_split(left, right):
    return dot(left[0], right[0]) + dot(left[1], right[0]) + dot(left[0], right[1])


def lanes_of(rows):
    return lax.broadcasted_iota(jnp.int32, (rows, LANES), 1)


def halves(first, second):
    low = lanes_of(first.shape[0]) < LANES // 2
    return (
        jnp.where(low, first, pltpu.roll(second, LANES // 2, 1)),
        jnp.where(low, pltpu.roll(first, LANES // 2, 1), second),
    )


def start_kernel(plan, charges_ref, left_ref, left_low_ref, right_ref, right_low_ref, own_ref, out_ref):
    bx, by, bz = plan.brick
    rim, half = plan.rim, plan.half
    top = None
    for part in range(2):
        cells = charges_ref[:, part * half : (part + 1) * half, :].reshape(LANES, bz).T
        own_ref[part] = cells
        out_ref[2 * rim * part : 2 * rim * part + rim] = cells[:rim]
        out_ref[2 * rim * part + rim : 2 * rim * (part + 1)] = cells[bz - rim :]
        rows = dot_split((left_ref[...], left_low_ref[...]), split(cells))
        rows = dot_split(split(rows), (right_ref[part], right_low_ref[part]))
        top = rows if top is None else top + rows
    out_ref[4 * rim :] = top


def spread_kernel(plan, place_ref, own_ref, sent_ref, got_ref, left_ref, right_ref, fine_ref, out_ref):
    bx, by, bz = plan.brick
    rim, rows = plan.rim, plan.fine_rows
    coarse = None
    for part in range(2):
        cells = own_ref[part]
        far = got_ref[2 * rim * part : 2 * rim * (part + 1)]
        fine_ref[part, :bz] = cells
        fine_ref[part, bz : bz + REACH] = far[2 * rim - REACH :]
        fine_ref[part, bz + REACH :] = far[:REACH]
        summed = dot_left(left_ref[...], jnp.concatenate([cells, far], axis=0))
        summed = dot_right(summed, right_ref[part])
        coarse = summed if coarse is None else coarse + summed
    low, high = halves(fine_ref[0], fine_ref[1])
    even = place_ref[0] % 2 == 0
    out_ref[:rows] = jnp.where(even, high, low)
    out_ref[rows : rows + plan.window_rows] = coarse
    top = rows + plan.window_rows
    out_ref[top : top + plan.top_rows // 2] = sent_ref[4 * rim :]
    out_ref[top + plan.top_rows // 2 :] = got_ref[4 * rim :]


def pass_kernel(plan, place_ref, fine_ref, sent_ref, got_ref, out_ref):
    rows = plan.fine_rows
    even = place_ref[0] % 2 == 0
    low, high = halves(fine_ref[0], fine_ref[1])
    out_ref[:rows] = jnp.where(even, low, high)
    own = sent_ref[rows : rows + plan.window_rows]
    far = got_ref[rows : rows + plan.window_rows]
    lane = lanes_of(plan.window_rows)
    edge, all_lanes = 2 * plan.cy, plan.cx * plan.cy
    last = all_lanes - edge
    right = own + jnp.where((lane >= last) & (lane < all_lanes), pltpu.roll(far, last, 1), 0.0)
    right = right + jnp.where((lane >= all_lanes) & (lane < all_lanes + edge), pltpu.roll(far, edge, 1), 0.0)
    left = own + jnp.where(lane < edge, pltpu.roll(far, LANES - last, 1), 0.0)
    left = left + jnp.where((lane >= all_lanes) & (lane < all_lanes + edge), pltpu.roll(far, all_lanes, 1), 0.0)
    out_ref[rows : rows + plan.window_rows] = jnp.where(even, right, left)
    top = rows + plan.window_rows
    out_ref[top:] = sent_ref[top:] + pltpu.roll(got_ref[top:], plan.group, 1)


def stack_kernel(plan, place_ref, fine_ref, first_sent_ref, sent_ref, first_ref, second_ref, cells_ref, out_ref):
    rows, window = plan.fine_rows, plan.window_rows
    low, high = halves(first_ref[:rows], second_ref[:rows])
    for part, other in ((0, low), (1, high)):
        cells_ref[part, :rows] = fine_ref[part]
        cells_ref[part, rows:] = other
    even = place_ref[1] % 2 == 0
    out_ref[: 2 * rows] = jnp.where(even, cells_ref[0], cells_ref[1])
    at = 2 * rows
    for source in (first_sent_ref, first_ref, second_ref):
        out_ref[at : at + window] = source[rows : rows + window]
        at = at + window
    out_ref[at:] = sent_ref[rows + window :] + pltpu.roll(second_ref[rows + window :], 2 * plan.group, 1)


def share_kernel(plan, place_ref, cells_ref, sent_ref, got_ref, out_ref):
    rows, window = plan.fine_rows, plan.window_rows
    even = place_ref[1] % 2 == 0
    out_ref[: 2 * rows] = jnp.where(even, cells_ref[1], cells_ref[0])
    at, size = 2 * rows, 3 * window
    out_ref[at : at + size] = sent_ref[at : at + size]
    out_ref[at + size : at + 2 * size] = got_ref[at : at + size]
    out_ref[at + 2 * size :] = sent_ref[at + size :] + pltpu.roll(got_ref[at + size :], 4 * plan.group, 1)


def add_fine(plan, total, cells, left, right_refs, at, terms):
    bz = plan.brick[2]
    for block in range(2):
        along_z = dot_split(left, split(cells[block]))
        for term in range(terms):
            piece = split(along_z[term * bz : (term + 1) * bz])
            rows = pl.ds((2 * at + block) * LANES, LANES)
            total = total + dot_split(piece, (right_refs[0][term, rows], right_refs[1][term, rows]))
    return total


def add_coarse(plan, total, cells, left, right_refs, at, terms):
    along_z = dot_split(left, split(cells))
    rows = pl.ds(at * LANES, LANES)
    for term in range(terms):
        piece = split(along_z[term * plan.out_rows : (term + 1) * plan.out_rows])
        total = total + dot_split(piece, (right_refs[0][term, rows], right_refs[1][term, rows]))
    return total


def near_kernel(plan, terms, cells_ref, sent_ref, zl_ref, zl_low_ref, kl_ref, kl_low_ref, z1_ref, z1_low_ref,
                k1_ref, k1_low_ref, fine_ref, coarse_ref):
    rows, window = plan.fine_rows, plan.window_rows
    total = jnp.zeros((plan.brick[2], 2 * LANES), F32)
    left = (zl_ref[...], zl_low_ref[...])
    for part in range(2):
        blocks = (cells_ref[part, :rows], cells_ref[part, rows:])
        total = add_fine(plan, total, blocks, left, (kl_ref, kl_low_ref), part, terms)
    fine_ref[...] = total
    coarse = jnp.zeros((plan.out_rows, LANES), F32)
    left = (z1_ref[...], z1_low_ref[...])
    for part in range(3):
        at = 2 * rows + part * window
        coarse = add_coarse(plan, coarse, sent_ref[at : at + window], left, (k1_ref, k1_low_ref), part, terms)
    coarse_ref[...] = coarse


def far_kernel(plan, terms, fine_ref, coarse_ref, first_ref, sent_ref, second_ref, zl_ref, zl_low_ref, kl_ref,
               kl_low_ref, z1_ref, z1_low_ref, k1_ref, k1_low_ref, zc_ref, zc_low_ref, kc_ref, kc_low_ref, back_ref,
               back_right_ref, out_ref):
    rows, window, bz = plan.fine_rows, plan.window_rows, plan.brick[2]
    total = fine_ref[...]
    left = (zl_ref[...], zl_low_ref[...])
    for part, source in ((2, first_ref), (3, second_ref)):
        blocks = (source[:rows], source[rows : 2 * rows])
        total = add_fine(plan, total, blocks, left, (kl_ref, kl_low_ref), part, terms)
    coarse = coarse_ref[...]
    left = (z1_ref[...], z1_low_ref[...])
    for part in range(9):
        source, place = (first_ref, part) if part < 3 else (second_ref, part - 3)
        at = 2 * rows + place * window
        coarse = add_coarse(plan, coarse, source[at : at + window], left, (k1_ref, k1_low_ref), part + 3, terms)
    at = 2 * rows + 6 * window
    for part, source in ((0, sent_ref), (1, second_ref)):
        along_z = dot_split((zc_ref[...], zc_low_ref[...]), split(source[at : at + plan.top_rows]))
        place = pl.ds(part * LANES, LANES)
        coarse = coarse + dot_split(split(along_z), (kc_ref[place], kc_low_ref[place]))
    total = total + dot_right(dot_left(back_ref[...], coarse), back_right_ref[...])
    half = plan.half
    for part in range(2):
        cells = total[:, part * LANES : (part + 1) * LANES].T
        out_ref[:, part * half : (part + 1) * half, :] = cells.reshape(plan.brick[0], half, bz)


def norms(exponents):
    offsets = jnp.arange(-REACH, REACH + 1).astype(F32)
    return 1.0 / jnp.sum(jnp.exp(-exponents[..., None] * offsets * offsets), axis=-1)


def gauss_of(exponents, scales, squared):
    return scales[:, None, None] * jnp.exp(-exponents[:, None, None] * squared[None])


def squares(difference):
    return jnp.where(jnp.abs(difference) <= REACH, (difference * difference).astype(F32), FAR)


def wrapped(difference, count):
    return (difference + count // 2 + 2 * count) % count - count // 2


def fine_weights(plan, exponents, amplitudes, even_x, even_y):
    bx, by, bz = plan.brick
    half = plan.half
    scale = norms(exponents)
    z_in = np.concatenate([np.arange(bz), np.arange(-REACH, 0), bz + np.arange(REACH)])
    left = gauss_of(exponents, scale, squares(jnp.asarray(z_in[None, :] - np.arange(bz)[:, None])))
    row = jnp.arange(8 * LANES)[:, None]
    col = jnp.arange(2 * LANES)[None, :]
    lane, block, group = row % LANES, (row // LANES) % 2, row // (2 * LANES)
    strip = lane // (LANES // 2)
    to_right = (strip == 0) == even_x
    x_far = jnp.where(to_right, bx, -REACH) + (lane % (LANES // 2)) // half
    x_in = jnp.where(block == 0, lane // half, x_far)
    y_far = jnp.where((group == 3) == even_y, by, -half)
    y_in = jnp.where(group < 2, group * half, y_far) + lane % half
    x_out, y_out = (col % LANES) // half, (col // LANES) * half + col % half
    right = gauss_of(exponents, amplitudes * scale * scale, squares(x_in - x_out) + squares(y_in - y_out))
    return split_wide(left.reshape(-1, plan.fine_rows)), split_wide(right)


def coarse_weights(plan, exponents, amplitudes, even_x, even_y):
    bx, by, bz = (size // 2 for size in plan.brick)
    scale = norms(exponents)
    z_in = np.arange(plan.window_rows) - GAUSSIAN_RIM
    z_out = np.arange(plan.out_rows) - 1
    distance = np.where((np.arange(plan.window_rows) < plan.window)[None, :], z_in[None, :] - z_out[:, None], 2 * REACH)
    distance = np.where((np.arange(plan.out_rows) < plan.out_z)[:, None], distance, 2 * REACH)
    left = gauss_of(exponents, scale, squares(jnp.asarray(distance)))
    row = jnp.arange(12 * LANES)[:, None]
    col = jnp.arange(LANES)[None, :]
    lane, slot, group = row % LANES, (row // LANES) % 3, row // (3 * LANES)
    cell = lane // plan.cy
    to_right = (slot == 1) == even_x
    toward = jnp.where(to_right, bx, -bx)
    x_in = jnp.where(slot == 0, 0, toward) + cell - 1
    extra = jnp.where(to_right, 2 * bx + bx - 1, -2 * bx - 1) + cell - plan.cx
    x_in = jnp.where(cell >= plan.cx, extra, x_in)
    used = cell < jnp.where(slot == 2, plan.cx + 2, plan.cx)
    toward = jnp.where((group == 2) == even_y, by, -by)
    y_in = jnp.where(group == 0, 0, jnp.where(group == 3, 2 * by, toward)) + lane % plan.cy - 1
    x_out, y_out = col // plan.cy - 1, col % plan.cy - 1
    squared = squares(wrapped(x_in - x_out, bx * plan.counts[0])) + squares(wrapped(y_in - y_out, by * plan.counts[1]))
    squared = jnp.where(used & (col < plan.cx * plan.cy), squared, FAR)
    right = gauss_of(exponents, amplitudes * scale * scale, squared)
    return split_wide(left.reshape(-1, plan.window_rows)), split_wide(right)


def top_weights(plan, place, top_x, top_y, top_z):
    bx, by, bz = plan.brick
    nx, ny, nz = plan.counts
    four = (bx // 16, by // 16, bz // 16)

    def spread(kernel, axis, rows):
        whole = prolong_three_whole(kernel.shape[0])
        size = plan.brick[axis] // 2
        wide = np.concatenate([whole[-1:], whole, whole[: size + 8]], axis=0)
        mine = lax.dynamic_slice(jnp.asarray(wide), (place[axis] * size, 0), (rows, kernel.shape[0]))
        return jnp.dot(mine, kernel, precision=HIGHEST)

    def pick(index, used, count):
        return jnp.where((index[:, None] % count == jnp.arange(count)[None, :]) & used[:, None], 1.0, 0.0)

    row = jnp.arange(plan.top_rows)
    side, cell = row // (plan.top_rows // 2), row % (plan.top_rows // 2)
    z_in = jnp.where(side == 0, place[2], nz - 1 - place[2]) * four[2] + cell - 1 + nz * four[2]
    left = jnp.dot(
        spread(top_z, 2, plan.out_rows), pick(z_in, cell < plan.top_z, nz * four[2]).T, precision=HIGHEST
    )
    row = jnp.arange(2 * LANES)
    lane, partner = row % LANES, row // LANES
    group, cell = lane // plan.group, lane % plan.group
    used = cell < plan.top_x * plan.top_y
    x_dev = place[0] ^ (group % 2) ^ (3 * ((group // 2) % 2))
    y_dev = place[1] ^ partner ^ (3 * (group // 4))
    x_in = x_dev * four[0] + cell // plan.top_y - 1 + nx * four[0]
    y_in = y_dev * four[1] + cell % plan.top_y - 1 + ny * four[1]
    along_x = jnp.dot(pick(x_in, used, nx * four[0]), spread(top_x, 0, plan.cx).T, precision=HIGHEST)
    along_y = jnp.dot(pick(y_in, used, ny * four[1]), spread(top_y, 1, plan.cy).T, precision=HIGHEST)
    col = np.arange(LANES)
    cols_x = (np.arange(plan.cx)[:, None] == col[None, :] // plan.cy).astype(np.float32)
    cols_y = (np.arange(plan.cy)[:, None] == col[None, :] % plan.cy).astype(np.float32)
    right = jnp.dot(along_x, cols_x, precision=HIGHEST) * jnp.dot(along_y, cols_y, precision=HIGHEST)
    return split_wide(left), split_wide(right)


def call(body, shapes, *operands, scalars=0):
    specs = [pl.BlockSpec(memory_space=pltpu.SMEM)] * scalars
    specs += [pl.BlockSpec(memory_space=pltpu.VMEM)] * (len(operands) - scalars)
    out = pl.pallas_call(
        body,
        out_shape=[jax.ShapeDtypeStruct(shape, F32) for shape in shapes],
        in_specs=specs,
        out_specs=[pl.BlockSpec(memory_space=pltpu.VMEM)] * len(shapes),
    )(*operands)
    return out


def pair(value, axis, bits):
    count = lax.axis_size(axis)
    return lax.ppermute(value, axis, [(i, i ^ bits) for i in range(count)])


def local_short(plan, charges, exponents, amplitudes, top_x, top_y, top_z):
    place = [lax.axis_index(axis) for axis in ("gx", "gy", "gz")]
    where = jnp.stack(place).astype(jnp.int32)
    even_x, even_y = place[0] % 2 == 0, place[1] % 2 == 0
    terms = exponents.shape[1]
    bx, by, bz = plan.brick
    bind = functools.partial

    own, sent_z = call(
        bind(start_kernel, plan),
        [(2, bz, LANES), (4 * plan.rim + plan.top_rows // 2, LANES)],
        charges,
        *np_split(plan.top_left),
        *np_split(np.stack(plan.top_right)),
    )
    got_z = pair(sent_z, "gz", 1)
    fine_left, fine_right = fine_weights(plan, exponents[0], amplitudes[0], even_x, even_y)
    coarse_left, coarse_right = coarse_weights(plan, exponents[1], amplitudes[1], even_x, even_y)
    top_left, top_right = top_weights(plan, place, top_x, top_y, top_z)

    fine, sent_a = call(
        bind(spread_kernel, plan),
        [(2, plan.fine_rows, LANES), (plan.message, LANES)],
        where,
        own,
        sent_z,
        got_z,
        jnp.asarray(plan.rest_left, BF16),
        jnp.asarray(np.stack(plan.rest_right), BF16),
        scalars=1,
    )
    got_a = pair(sent_a, "gx", 1)
    (sent_b,) = call(bind(pass_kernel, plan), [(plan.message, LANES)], where, fine, sent_a, got_a, scalars=1)
    got_b = pair(sent_b, "gx", 3)
    size = 2 * plan.fine_rows + 3 * plan.window_rows + plan.top_rows
    cells, sent_c = call(
        bind(stack_kernel, plan),
        [(2, 2 * plan.fine_rows, LANES), (size, LANES)],
        where,
        fine,
        sent_a,
        sent_b,
        got_a,
        got_b,
        scalars=1,
    )
    got_c = pair(sent_c, "gy", 3)
    weights = (*fine_left, *fine_right, *coarse_left, *coarse_right)
    near_fine, near_coarse = call(
        bind(near_kernel, plan, terms), [(bz, 2 * LANES), (plan.out_rows, LANES)], cells, sent_c, *weights
    )
    (sent_d,) = call(
        bind(share_kernel, plan), [(size + 3 * plan.window_rows, LANES)], where, cells, sent_c, got_c, scalars=1
    )
    got_d = pair(sent_d, "gy", 1)
    (out,) = call(
        bind(far_kernel, plan, terms),
        [(bx, by, bz)],
        near_fine,
        near_coarse,
        got_c,
        sent_d,
        got_d,
        *weights,
        *top_left,
        *top_right,
        jnp.asarray(plan.back_left, BF16),
        jnp.asarray(plan.back_right, BF16),
    )
    return out


def np_split(table):
    high = table.astype(BF16)
    return jnp.asarray(high), jnp.asarray((table - high.astype(np.float32)).astype(BF16))


def local(*arguments):
    counts = tuple(lax.axis_size(axis) for axis in ("gx", "gy", "gz"))
    brick = arguments[0].shape
    if fits(brick, counts):
        return local_short(Plan(brick, counts), *arguments)
    return local_any(*arguments)


def solution(mesh):
    in_specs = (P("gx", "gy", "gz"), P(), P(), P(), P(), P())
    out_specs = P("gx", "gy", "gz")
    return jax.shard_map(local, mesh=mesh, in_specs=in_specs, out_specs=out_specs, check_vma=False)
```

```python
import functools

import jax
import jax.numpy as jnp
import numpy as np
from jax import lax
from jax.experimental import pallas as pl
from jax.experimental.pallas import tpu as pltpu
from jax.sharding import PartitionSpec as P

REACH = 8


HIGHEST = lax.Precision.HIGHEST


def with_halo(cells, sides, width):
    for axis, dim in sides:
        count = lax.axis_size(axis)
        head = lax.slice_in_dim(cells, 0, width, axis=dim)
        tail = lax.slice_in_dim(cells, cells.shape[dim] - width, cells.shape[dim], axis=dim)
        cells = jnp.concatenate(
            [
                lax.ppermute(tail, axis, [(i, (i + 1) % count) for i in range(count)]),
                cells,
                lax.ppermute(head, axis, [((i + 1) % count, i) for i in range(count)]),
            ],
            axis=dim,
        )
    return cells


def gauss_taps(exponents):
    offsets = jnp.arange(-REACH, REACH + 1).astype(jnp.float32)
    weights = jnp.exp(-exponents[..., None] * offsets * offsets)
    return weights / jnp.sum(weights, axis=-1, keepdims=True)


def spline(offsets):
    inner_weight = jnp.where((offsets == 1) | (offsets == 2), 0.75, 0.0)
    return jnp.where((offsets == 0) | (offsets == 3), 0.25, inner_weight).astype(jnp.float32)


def band_gauss(tap_table, length):
    rows = jnp.arange(length + 2 * REACH)[:, None]
    cols = jnp.arange(length)[None, :]
    offsets = rows - cols
    onehot = (offsets[:, :, None] == jnp.arange(2 * REACH + 1)[None, None, :]).astype(jnp.float32)
    return jnp.einsum("gk,pok->gpo", tap_table, onehot, precision=HIGHEST)


def band_restrict(length):
    rows = jnp.arange(length + 2)[:, None]
    cols = jnp.arange(length // 2)[None, :]
    return spline(rows - 2 * cols)


def band_prolong(length):
    rows = jnp.arange(length + 2)[:, None]
    cols = jnp.arange(2 * length)[None, :]
    return spline(cols - 2 * rows + 3)


def apply_three(field, band_x, band_y, band_z):
    field = jnp.einsum("xyz,zc->xyc", field, band_z, precision=HIGHEST)
    field = jnp.einsum("xyz,yb->xbz", field, band_y, precision=HIGHEST)
    return jnp.einsum("xyz,xa->ayz", field, band_x, precision=HIGHEST)


def rim_cells(field):
    return with_halo(field, (("gx", 0), ("gy", 1), ("gz", 2)), 1)


def restrict_local(padded):
    sizes = padded.shape
    return apply_three(
        padded,
        band_restrict(sizes[0] - 2),
        band_restrict(sizes[1] - 2),
        band_restrict(sizes[2] - 2),
    )


def prolong_local(field):
    sizes = field.shape
    return apply_three(
        rim_cells(field), band_prolong(sizes[0]), band_prolong(sizes[1]), band_prolong(sizes[2])
    )


def prolong_from_whole(whole_grid, brick):
    padded = jnp.pad(whole_grid, 1, mode="wrap")
    starts = (
        lax.axis_index("gx") * brick[0],
        lax.axis_index("gy") * brick[1],
        lax.axis_index("gz") * brick[2],
    )
    piece_cells = lax.dynamic_slice(padded, starts, (brick[0] + 2, brick[1] + 2, brick[2] + 2))
    return apply_three(
        piece_cells, band_prolong(brick[0]), band_prolong(brick[1]), band_prolong(brick[2])
    )


def assemble(gathered, brick):
    count_x = lax.axis_size("gx")
    count_y = lax.axis_size("gy")
    count_z = lax.axis_size("gz")
    blocks = gathered.reshape(count_x, count_y, count_z, brick[0], brick[1], brick[2])
    blocks = jnp.transpose(blocks, (0, 3, 1, 4, 2, 5))
    return blocks.reshape(count_x * brick[0], count_y * brick[1], count_z * brick[2])


def top_level(field, top_x, top_y, top_z):
    field = jnp.einsum("ia,abc->ibc", top_x, field, precision=HIGHEST)
    field = jnp.einsum("jb,ibc->ijc", top_y, field, precision=HIGHEST)
    return jnp.einsum("kc,ijc->ijk", top_z, field, precision=HIGHEST)


def gauss_and_restrict(field, tap_table, weights):
    size_x, size_y, size_z = field.shape
    band_z = band_gauss(tap_table, size_z)
    band_y = band_gauss(tap_table, size_y)
    band_x = band_gauss(tap_table, size_x) * weights[:, None, None]
    padded = with_halo(field, (("gx", 0), ("gy", 1), ("gz", 2)), REACH)
    along_z = jnp.einsum("xyp,gpo->xygo", padded, band_z, precision=HIGHEST)
    along_y = jnp.einsum("xpgz,gpw->xgwz", along_z, band_y, precision=HIGHEST)
    result = jnp.einsum("pgwz,gpv->vwz", along_y, band_x, precision=HIGHEST)
    inner_cells = padded[
        REACH - 1 : size_x + REACH + 1,
        REACH - 1 : size_y + REACH + 1,
        REACH - 1 : size_z + REACH + 1,
    ]
    coarse = restrict_local(inner_cells)
    return (result, coarse)


def local_any(charges, exponents, amplitudes, top_x, top_y, top_z):
    tap_table = gauss_taps(exponents)
    term_zero, level_one = gauss_and_restrict(charges, tap_table[0], amplitudes[0])
    term_one, level_two = gauss_and_restrict(level_one, tap_table[1], amplitudes[1])
    level_three = restrict_local(rim_cells(level_two))
    level_four = restrict_local(rim_cells(level_three))
    brick_four = level_four.shape
    gathered = lax.all_gather(level_four.reshape(1, -1), ("gx", "gy", "gz"), axis=0, tiled=True)
    phi_four = top_level(assemble(gathered, brick_four), top_x, top_y, top_z)
    phi_three = prolong_from_whole(phi_four, brick_four)
    phi_two = prolong_local(phi_three)
    phi_one = term_one + prolong_local(phi_two)
    return term_zero + prolong_local(phi_one)


F32 = jnp.float32
BF16 = jnp.bfloat16
LANES = 128
FAR = 1.0e9
GAUSSIAN_RIM = REACH + 1


def up8(count):
    return -(-count // 8) * 8


def restrict_weights(fine, coarse):
    offsets = np.asarray(fine)[None, :] - 2 * np.asarray(coarse)[:, None] + 1
    inner = np.where((offsets == 1) | (offsets == 2), 0.75, 0.0)
    return np.where((offsets == 0) | (offsets == 3), 0.25, inner).astype(np.float32)


def reach_four(length):
    total, cells = np.eye(length, dtype=np.float32), np.arange(length)
    for level in range(1, 5):
        coarse = np.arange(-1, length // 2**level + 1)
        total = restrict_weights(cells, coarse) @ total
        cells = coarse
    return total


def prolong_three_whole(count):
    total = np.eye(count, dtype=np.float32)
    for level in range(3):
        size = count * 2**level
        step = np.zeros((2 * size, size), np.float32)
        for cell in range(size):
            for offset, weight in ((-1, 0.25), (0, 0.75), (1, 0.75), (2, 0.25)):
                step[(2 * cell + offset) % (2 * size), cell] += weight
        total = step @ total
    return total


def padded(table, rows, cols):
    out = np.zeros((rows, cols), np.float32)
    out[: table.shape[0], : table.shape[1]] = table
    return out


class Plan:
    def __init__(self, brick, counts):
        self.brick, self.counts = brick, counts
        bx, by, bz = brick
        self.half = by // 2
        self.rim = up8(2 * GAUSSIAN_RIM + 1)
        self.fine_rows = bz + 2 * REACH
        self.cx, self.cy = bx // 2 + 2, by // 2 + 2
        self.window = bz // 2 + 2 * GAUSSIAN_RIM
        self.window_rows = up8(self.window)
        self.out_z = bz // 2 + 2
        self.out_rows = up8(self.out_z)
        self.top_rows = 2 * up8(bz // 16 + 2)
        self.top_z = bz // 16 + 2
        self.top_x, self.top_y = bx // 16 + 2, by // 16 + 2
        self.group = 16
        x_of, y_of = self.own_cells()
        rz = reach_four(bz)
        self.top_left = padded(rz, self.top_rows // 2, bz)
        rx, ry = reach_four(bx), reach_four(by)
        self.top_right, self.rest_right = [], []
        sx = restrict_weights(np.arange(bx), np.arange(-1, bx // 2 + 1))
        sy = restrict_weights(np.arange(by), np.arange(-1, by // 2 + 1))
        for part in range(2):
            y = y_of + part * self.half
            table = rx[:, x_of][:, None, :] * ry[:, y][None, :, :]
            self.top_right.append(padded(table.reshape(-1, LANES).T, LANES, LANES))
            table = sx[:, x_of][:, None, :] * sy[:, y][None, :, :]
            self.rest_right.append(padded(table.reshape(-1, LANES).T, LANES, LANES))
        z_in = np.concatenate([np.arange(bz), bz + np.arange(self.rim), np.arange(-self.rim, 0)])
        z_out = np.arange(-GAUSSIAN_RIM, bz // 2 + GAUSSIAN_RIM)
        self.rest_left = padded(restrict_weights(z_in, z_out), self.window_rows, z_in.size)
        spread = restrict_weights(np.arange(bz), np.arange(-1, bz // 2 + 1)).T
        self.back_left = padded(spread.T, LANES, bz)
        cols = []
        for part in range(2):
            y = y_of + part * self.half
            table = sx[:, x_of][:, None, :] * sy[:, y][None, :, :]
            cols.append(padded(table.reshape(-1, LANES), LANES, LANES))
        self.out_cells = -(-self.cx * self.cy // 16) * 16
        self.back_right = np.concatenate(cols, axis=1).T[:, : self.out_cells]
        self.message = self.fine_rows + self.window_rows + self.top_rows

    def constants(self, kernels):
        rest = self.rest_left
        fine_cells, fine_dz = self.fine_tables()
        coarse_cells, out_cells, coarse_dz = self.coarse_tables()
        spread_x, pick_x, spread_y, pick_y, spread_z, pick_z, lift_x, lift_y = self.top_tables(kernels)
        named = {
            "rest_left": rest[:, :LANES],
            "rest_far": rest[:, LANES:],
            "rest_right": np.concatenate(self.rest_right),
            "fine_cells": fine_cells,
            "fine_dz": fine_dz,
            "coarse_cells": coarse_cells,
            "out_cells": out_cells.reshape(-1, LANES),
            "coarse_dz": coarse_dz,
            "back": self.back_left,
            "back_right": self.back_right,
            "spread_x": spread_x.reshape(-1, 16),
            "pick_x": pick_x.transpose(0, 2, 1, 3).reshape(-1, LANES),
            "spread_y": spread_y.reshape(-1, 16),
            "pick_y": pick_y.transpose(0, 2, 1, 3).reshape(-1, LANES),
            "spread_z": spread_z.reshape(-1, 16),
            "pick_z": pick_z.reshape(-1, self.top_rows),
            "lift_x": lift_x,
            "lift_y": lift_y,
        }
        at, starts, pieces = 0, {}, []
        for name, table in named.items():
            rows = -(-table.shape[0] // 16) * 16
            starts[name] = at
            pieces.append(padded(table, rows, LANES))
            at += rows
        self.starts = starts
        return np.concatenate(pieces)

    def fine_tables(self):
        bx, by, bz = self.brick
        x_of, y_of = self.own_cells()
        strip, x_far = np.arange(LANES) // (LANES // 2), x_of % (LANES // 2 // self.half)
        right, left = bx + x_far, x_far - REACH
        cells = np.stack([x_of, y_of, np.where(strip == 0, right, left), np.where(strip == 0, left, right)])
        z_in = np.concatenate([np.arange(bz), np.arange(-REACH, 0), bz + np.arange(REACH)])
        distance = z_in[:, None] - np.arange(bz)[None, :]
        squared = np.where(np.abs(distance) <= REACH, distance * distance, FAR)
        return padded(cells, 8, LANES), squared.astype(np.float32)

    def coarse_tables(self):
        bx, by, bz = (size // 2 for size in self.brick)
        lane = np.arange(LANES)
        cell, count = lane // self.cy, self.cx * self.cy
        own = cell - 1
        extra = cell >= self.cx
        far_right = np.where(extra, 3 * bx - 1 + cell - self.cx, bx + own)
        far_left = np.where(extra, -2 * bx - 1 + cell - self.cx, own - bx)
        cells = [own, own, own + bx, own - bx, far_left, far_right, lane % self.cy - 1]
        cells += [np.where(lane < count, 0.0, FAR), np.where(cell < self.cx + 2, 0.0, FAR)]
        row = np.arange(self.out_cells)[:, None] + np.zeros((1, LANES))
        outs = np.stack([row // self.cy - 1, row % self.cy - 1, np.where(row < count, 0.0, FAR)])
        z_in, z_out = np.arange(self.window_rows) - GAUSSIAN_RIM, np.arange(LANES) - 1
        distance = z_in[:, None] - z_out[None, :]
        near = (np.abs(distance) <= REACH) & (np.arange(LANES) < self.out_z)[None, :]
        near = near & (np.arange(self.window_rows) < self.window)[:, None]
        squared = np.where(near, distance * distance, FAR)
        return padded(np.stack(cells), 16, LANES), outs.astype(np.float32), squared.astype(np.float32)

    def top_tables(self, kernels):
        four = [size // 16 for size in self.brick]
        lane = np.arange(2 * LANES)
        group, cell, partner = (lane % LANES) // self.group, lane % self.group, lane // LANES
        used = cell < self.top_x * self.top_y
        tables = []
        for axis in range(3):
            count, size = kernels[axis].shape[0], self.brick[axis] // 2
            whole = prolong_three_whole(count)
            outs = (self.cx, self.cy, self.out_z)[axis]
            spread, pick = [], []
            for place in range(self.counts[axis]):
                index = (place * size - 1 + np.arange(outs)) % (8 * count)
                spread.append(padded(whole[index], 16 if axis < 2 else LANES, 16))
                if axis == 0:
                    cells = (place ^ (group % 2) ^ (3 * ((group // 2) % 2))) * four[0] + cell // self.top_y - 1
                    valid = used
                elif axis == 1:
                    cells = (place ^ partner ^ (3 * (group // 4))) * four[1] + cell % self.top_y - 1
                    valid = used
                else:
                    row = np.arange(self.top_rows)
                    side, at = row // (self.top_rows // 2), row % (self.top_rows // 2)
                    cells = (place ^ side) * four[2] + at - 1
                    valid = at < self.top_z
                hot = (np.arange(count)[:, None] == (cells % count)[None, :]) & valid[None, :]
                hot = padded(hot, 16, cells.size)
                pick.append(hot if axis == 2 else hot.reshape(16, 2, LANES))
            tables += [np.stack(spread), np.stack(pick)]
        out = np.arange(self.out_cells)
        tables.append((out[:, None] // self.cy == np.arange(16)[None, :]).astype(np.float32))
        tables.append((out[:, None] % self.cy == np.arange(16)[None, :]).astype(np.float32))
        return tables

    def own_cells(self):
        lane = np.arange(LANES)
        return lane // self.half, lane % self.half


def fits(brick, counts, tops):
    bx, by, bz = brick
    return (
        counts == (4, 4, 2)
        and bx * (by // 2) == LANES
        and by % 16 == 0
        and bx % 16 == 0
        and bz == LANES
        and bx // 2 == REACH
        and by // 2 == REACH
        and (bx // 2 + 4) * (by // 2 + 2) <= LANES
        and (bx // 16 + 2) * (by // 16 + 2) <= 16
        and max(top.shape[0] for top in tops) <= 16
    )


def split(value):
    high = value.astype(BF16)
    return high, (value - high.astype(F32)).astype(BF16)


def dot(left, right):
    return jnp.dot(left, right, preferred_element_type=F32)


def dot_left(exact, value):
    high, low = split(value)
    return dot(exact, high) + dot(exact, low)


def dot_right(value, exact):
    high, low = split(value)
    return dot(high, exact) + dot(low, exact)


def dot_split(left, right):
    return dot(left[0], right[0]) + dot(left[1], right[0]) + dot(left[0], right[1])


def exact_tables(plan, ref):
    def read(name, rows, at=0):
        start = plan.starts[name] + at * rows
        return ref[start : start + rows].astype(BF16)

    return read


def lanes_of(rows):
    return lax.broadcasted_iota(jnp.int32, (rows, LANES), 1)


def halves(first, second):
    low = lanes_of(first.shape[0]) < LANES // 2
    return (
        jnp.where(low, first, pltpu.roll(second, LANES // 2, 1)),
        jnp.where(low, pltpu.roll(first, LANES // 2, 1), second),
    )


def start_kernel(plan, charges_ref, left_ref, left_low_ref, right_ref, right_low_ref, own_ref, out_ref):
    bx, by, bz = plan.brick
    rim, half = plan.rim, plan.half
    top = None
    for part in range(2):
        cells = charges_ref[:, part * half : (part + 1) * half, :].reshape(LANES, bz).T
        own_ref[part] = cells
        out_ref[2 * rim * part : 2 * rim * part + rim] = cells[:rim]
        out_ref[2 * rim * part + rim : 2 * rim * (part + 1)] = cells[bz - rim :]
        rows = dot_split((left_ref[...], left_low_ref[...]), split(cells))
        rows = dot_split(split(rows), (right_ref[part], right_low_ref[part]))
        top = rows if top is None else top + rows
    out_ref[4 * rim :] = top


def setup_kernel(plan, terms, exponents_ref, amplitudes_ref, tops_x_ref, tops_y_ref, tops_z_ref, table_ref, kept_ref,
                 params_ref, semaphore):
    copy = pltpu.make_async_copy(table_ref, kept_ref, semaphore)
    copy.start()
    offsets = lax.broadcasted_iota(jnp.int32, (1, LANES), 1).astype(F32) - REACH
    squared = jnp.where(offsets <= REACH, offsets * offsets, FAR)
    for level in range(2):
        for term in range(terms):
            exponent = exponents_ref[level, term]
            scale = 1.0 / jnp.sum(jnp.exp(squared * -exponent), axis=1, keepdims=True)
            scale = jnp.broadcast_to(scale, (1, LANES))
            row = 3 * terms * level + term
            params_ref[row : row + 1] = jnp.zeros((1, LANES), F32) + exponent
            row = row + terms
            params_ref[row : row + 1] = scale * scale * amplitudes_ref[level, term]
            row = row + terms
            params_ref[row : row + 1] = scale
    params_ref[6 * terms :] = jnp.zeros((3 * 16, LANES), F32)
    for axis, source in enumerate((tops_x_ref, tops_y_ref, tops_z_ref)):
        at, count = 6 * terms + 16 * axis, source.shape[0]
        params_ref[at : at + count, :count] = source[...]
    copy.wait()


def spread_kernel(plan, place_ref, own_ref, sent_ref, got_ref, table_ref, fine_ref, out_ref):
    bx, by, bz = plan.brick
    rim, rows = plan.rim, plan.fine_rows
    table = exact_tables(plan, table_ref)
    coarse = None
    for part in range(2):
        cells = own_ref[part]
        far = got_ref[2 * rim * part : 2 * rim * (part + 1)]
        fine_ref[part, :bz] = cells
        fine_ref[part, bz : bz + REACH] = far[2 * rim - REACH :]
        fine_ref[part, bz + REACH :] = far[:REACH]
        summed = dot_left(table("rest_left", plan.window_rows), cells)
        summed = summed + dot_left(table("rest_far", plan.window_rows)[:, : 2 * rim], far)
        summed = dot_right(summed, table("rest_right", LANES, part))
        coarse = summed if coarse is None else coarse + summed
    low, high = halves(fine_ref[0], fine_ref[1])
    even = place_ref[0] % 2 == 0
    out_ref[:rows] = jnp.where(even, high, low)
    out_ref[rows : rows + plan.window_rows] = coarse
    top = rows + plan.window_rows
    out_ref[top : top + plan.top_rows // 2] = sent_ref[4 * rim :]
    out_ref[top + plan.top_rows // 2 :] = got_ref[4 * rim :]


def pass_kernel(plan, place_ref, fine_ref, sent_ref, got_ref, out_ref):
    rows = plan.fine_rows
    even = place_ref[0] % 2 == 0
    low, high = halves(fine_ref[0], fine_ref[1])
    out_ref[:rows] = jnp.where(even, low, high)
    own = sent_ref[rows : rows + plan.window_rows]
    far = got_ref[rows : rows + plan.window_rows]
    lane = lanes_of(plan.window_rows)
    edge, all_lanes = 2 * plan.cy, plan.cx * plan.cy
    last = all_lanes - edge
    right = own + jnp.where((lane >= last) & (lane < all_lanes), pltpu.roll(far, last, 1), 0.0)
    right = right + jnp.where((lane >= all_lanes) & (lane < all_lanes + edge), pltpu.roll(far, edge, 1), 0.0)
    left = own + jnp.where(lane < edge, pltpu.roll(far, LANES - last, 1), 0.0)
    left = left + jnp.where((lane >= all_lanes) & (lane < all_lanes + edge), pltpu.roll(far, all_lanes, 1), 0.0)
    out_ref[rows : rows + plan.window_rows] = jnp.where(even, right, left)
    top = rows + plan.window_rows
    out_ref[top:] = sent_ref[top:] + pltpu.roll(got_ref[top:], plan.group, 1)


def stack_kernel(plan, place_ref, fine_ref, first_sent_ref, sent_ref, first_ref, second_ref, cells_ref, out_ref):
    rows, window = plan.fine_rows, plan.window_rows
    low, high = halves(first_ref[:rows], second_ref[:rows])
    for part, other in ((0, low), (1, high)):
        cells_ref[part, :rows] = fine_ref[part]
        cells_ref[part, rows:] = other
    even = place_ref[1] % 2 == 0
    out_ref[: 2 * rows] = jnp.where(even, cells_ref[0], cells_ref[1])
    at = 2 * rows
    for source in (first_sent_ref, first_ref, second_ref):
        out_ref[at : at + window] = source[rows : rows + window]
        at = at + window
    out_ref[at:] = sent_ref[rows + window :] + pltpu.roll(second_ref[rows + window :], 2 * plan.group, 1)


def share_kernel(plan, place_ref, cells_ref, sent_ref, got_ref, out_ref):
    rows, window = plan.fine_rows, plan.window_rows
    even = place_ref[1] % 2 == 0
    out_ref[: 2 * rows] = jnp.where(even, cells_ref[1], cells_ref[0])
    at, size = 2 * rows, 3 * window
    out_ref[at : at + size] = sent_ref[at : at + size]
    out_ref[at + size : at + 2 * size] = got_ref[at : at + size]
    out_ref[at + 2 * size :] = sent_ref[at + size :] + pltpu.roll(got_ref[at + size :], 4 * plan.group, 1)


def dot_turned(left, right):
    def product(first, second):
        return lax.dot_general(first, second, (((1,), (1,)), ((), ())), preferred_element_type=F32)

    return product(left[0], right[0]) + product(left[1], right[0]) + product(left[0], right[1])


def fine_weights_kernel(plan, terms, place_ref, params_ref, table_ref, kf_ref, kf_low_ref, zf_ref, zf_low_ref):
    bx, by, bz = plan.brick
    cells_ref = table_ref.at[pl.ds(plan.starts["fine_cells"], 8)]
    dz_ref = table_ref.at[pl.ds(plan.starts["fine_dz"], plan.fine_rows)]
    half = plan.half
    even_x, even_y = place_ref[0] % 2 == 0, place_ref[1] % 2 == 0
    own_x, own_y = cells_ref[0:1], cells_ref[1:2]
    far_x = jnp.where(even_x, cells_ref[2:3], cells_ref[3:4])
    x_out = lax.broadcasted_iota(jnp.int32, (bx, LANES), 0).astype(F32)
    y_out = lax.broadcasted_iota(jnp.int32, (half, LANES), 0).astype(F32)
    y_low, y_high = F32(-half), F32(by)
    y_far = jnp.where(even_y, y_low, y_high), jnp.where(even_y, y_high, y_low)

    def decay(exponent, distance):
        return jnp.where(jnp.abs(distance) <= REACH, jnp.exp(-exponent * distance * distance), 0.0)

    for term in range(terms):
        exponent = params_ref[term : term + 1]
        scale = params_ref[terms + term : terms + term + 1]
        along_x = [decay(exponent, x_in - x_out)[:, None, :] for x_in in (own_x, far_x)]
        for group in range(4):
            y_in = own_y + (F32(group * half) if group < 2 else y_far[group - 2])
            for part in range(2):
                along_y = decay(exponent, y_in - (y_out + part * half)) * scale
                for block in range(2):
                    high, low = split((along_x[block] * along_y[None]).reshape(bx * half, LANES))
                    rows, cols = pl.ds(part * LANES, LANES), pl.ds((2 * group + block) * LANES, LANES)
                    kf_ref[term, rows, cols] = high
                    kf_low_ref[term, rows, cols] = low
        zf_ref[term], zf_low_ref[term] = split(
            jnp.exp(-exponent * dz_ref[...]) * params_ref[2 * terms + term : 2 * terms + term + 1]
        )


def coarse_weights_kernel(plan, terms, place_ref, params_ref, table_ref, k1_ref, k1_low_ref, z1_ref, z1_low_ref,
                          zc_ref, kc_ref):
    cells_ref = table_ref.at[pl.ds(plan.starts["coarse_cells"], 16)]
    at, count = plan.starts["out_cells"], plan.out_cells
    out_cells_ref = [table_ref[at + count * part : at + count * (part + 1)] for part in range(3)]
    dz_ref = table_ref.at[pl.ds(plan.starts["coarse_dz"], plan.window_rows)]
    zc_ref[...], kc_ref[...] = top_weights(plan, terms, place_ref, params_ref, table_ref)
    bx, by = plan.brick[0] // 2, plan.brick[1] // 2
    even_x, even_y = place_ref[0] % 2 == 0, place_ref[1] % 2 == 0
    base = 3 * terms

    def squared(distance, count):
        distance = distance - count * jnp.floor((distance + count // 2) * (1.0 / count))
        return jnp.where(jnp.abs(distance) <= REACH, distance * distance, FAR)

    x_out, y_out = out_cells_ref[0], out_cells_ref[1]
    squares_x = []
    for slot in range(3):
        x_in = jnp.where(even_x, cells_ref[2 * slot : 2 * slot + 1], cells_ref[2 * slot + 1 : 2 * slot + 2])
        used = cells_ref[7:8] if slot < 2 else cells_ref[8:9]
        squares_x.append(squared(x_in - x_out, bx * plan.counts[0]) + used)
    toward = jnp.where(even_y, F32(by), F32(-by))
    for group, offset in enumerate((F32(0), -toward, toward, F32(2 * by))):
        square_y = squared(cells_ref[6:7] + offset - y_out, by * plan.counts[1]) + out_cells_ref[2]
        for slot in range(3):
            total = squares_x[slot] + square_y
            cols = pl.ds((3 * group + slot) * LANES, LANES)
            for term in range(terms):
                exponent = params_ref[base + term : base + term + 1]
                scale = params_ref[base + terms + term : base + terms + term + 1]
                high, low = split(jnp.exp(-exponent * total) * scale)
                rows = pl.ds(term * plan.out_cells, plan.out_cells)
                k1_ref[rows, cols] = high
                k1_low_ref[rows, cols] = low
    for term in range(terms):
        exponent = params_ref[base + term : base + term + 1]
        scale = params_ref[base + 2 * terms + term : base + 2 * terms + term + 1]
        z1_ref[term], z1_low_ref[term] = split(jnp.exp(-exponent * dz_ref[...]) * scale)


def top_weights(plan, terms, place_ref, params_ref, table_ref):
    def chain(*factors):
        value = factors[0]
        for factor in factors[1:]:
            value = dot_split(split(value), split(factor))
        return value

    def read(name, rows, at=0):
        return table_ref[pl.ds(pl.multiple_of(plan.starts[name] + at * rows, 8), rows)]

    size = 16
    along = []
    for axis, (spread, pick) in enumerate((("spread_x", "pick_x"), ("spread_y", "pick_y"))):
        top = params_ref[6 * terms + size * axis : 6 * terms + size * (axis + 1)]
        picked = read(pick, 2 * size, place_ref[axis])
        picked = jnp.concatenate([picked[:size], picked[size:]], axis=1)
        value = chain(read(spread, size, place_ref[axis])[:, :size], top)[:, :size]
        along.append(chain(value, picked))
    top = params_ref[6 * terms + 2 * size : 6 * terms + 3 * size]
    value = chain(read("spread_z", LANES, place_ref[2])[:, :size], top)[:, :size]
    left = chain(value, read("pick_z", size, place_ref[2])[:, : plan.top_rows])
    lift_x, lift_y = (read(name, plan.out_cells)[:, :size] for name in ("lift_x", "lift_y"))
    return left, chain(lift_x, along[0]) * chain(lift_y, along[1])


def side_by_side(source, start, rows, count):
    return jnp.concatenate([source[start + rows * at : start + rows * (at + 1)] for at in range(count)], axis=1)


def gather_part(plan, terms, blocks, near, kf_refs, k1_refs, fine_at, coarse_at, before):
    cells, near = split(blocks), split(near)
    fine_cols = pl.ds(fine_at * LANES, blocks.shape[1])
    fine = []
    for term in range(terms):
        value = dot_turned((kf_refs[0][term, :, fine_cols], kf_refs[1][term, :, fine_cols]), cells)
        fine.append(value if before is None else before[0][term] + value)
    cols = pl.ds(coarse_at * LANES, near[0].shape[1])
    coarse = dot_turned((k1_refs[0][:, cols], k1_refs[1][:, cols]), near)
    return fine, coarse if before is None else before[1][...] + coarse


def near_kernel(plan, terms, cells_ref, sent_ref, kf_ref, kf_low_ref, k1_ref, k1_low_ref, fine_ref, coarse_ref):
    rows, window = plan.fine_rows, plan.window_rows
    blocks = [cells_ref[part, at : at + rows] for part in range(2) for at in (0, rows)]
    near = side_by_side(sent_ref, 2 * rows, window, 3)
    fine, coarse = gather_part(plan, terms, jnp.concatenate(blocks, axis=1), near, (kf_ref, kf_low_ref),
                               (k1_ref, k1_low_ref), 0, 0, None)
    for term in range(terms):
        fine_ref[term] = fine[term]
    coarse_ref[...] = coarse


def middle_kernel(plan, terms, fine_in_ref, coarse_in_ref, got_ref, kf_ref, kf_low_ref, k1_ref, k1_low_ref,
                  fine_ref, coarse_ref):
    rows, window = plan.fine_rows, plan.window_rows
    blocks, near = side_by_side(got_ref, 0, rows, 2), side_by_side(got_ref, 2 * rows, window, 3)
    fine, coarse = gather_part(plan, terms, blocks, near, (kf_ref, kf_low_ref), (k1_ref, k1_low_ref), 4, 3,
                               (fine_in_ref, coarse_in_ref))
    for term in range(terms):
        fine_ref[term] = fine[term]
    coarse_ref[...] = coarse


def far_kernel(plan, terms, fine_in_ref, coarse_in_ref, sent_ref, got_ref, kf_ref, kf_low_ref, k1_ref, k1_low_ref,
               zf_ref, zf_low_ref, z1_ref, z1_low_ref, zc_ref, kc_ref, table_ref, out_ref):
    rows, window, half = plan.fine_rows, plan.window_rows, plan.half
    blocks, near = side_by_side(got_ref, 0, rows, 2), side_by_side(got_ref, 2 * rows, window, 6)
    fine, coarse = gather_part(plan, terms, blocks, near, (kf_ref, kf_low_ref), (k1_ref, k1_low_ref), 6, 6,
                               (fine_in_ref, coarse_in_ref))
    at = 2 * rows + 6 * window
    top = jnp.concatenate([sent_ref[at : at + plan.top_rows], got_ref[at : at + plan.top_rows]], axis=1)
    top = dot_split(split(zc_ref[...]), split(top))
    level_one = dot_turned(split(kc_ref[...]), split(top))
    total = None
    for term in range(terms):
        piece = split(coarse[term * plan.out_cells : (term + 1) * plan.out_cells])
        level_one = level_one + dot_split(piece, (z1_ref[term], z1_low_ref[term]))
        value = dot_split(split(fine[term]), (zf_ref[term], zf_low_ref[term]))
        total = value if total is None else total + value
    table = exact_tables(plan, table_ref)
    back = dot_right(level_one, table("back", LANES))
    total = total + dot_left(table("back_right", 2 * LANES)[:, : plan.out_cells], back)
    for part in range(2):
        cells = total[part * LANES : (part + 1) * LANES]
        out_ref[:, part * half : (part + 1) * half, :] = cells.reshape(plan.brick[0], half, plan.brick[2])


def call(body, shapes, *operands, scalars=0, after=(), last=False, plain=False, scratch=()):
    specs = [pl.BlockSpec(memory_space=pltpu.SMEM)] * scalars
    specs += [pl.BlockSpec(memory_space=pltpu.VMEM)] * (len(operands) - scalars)
    if scratch:
        specs[-1] = pl.BlockSpec(memory_space=pl.ANY)
    specs += [pl.BlockSpec(memory_space=pl.ANY)] * len(after)

    def keep(operand, space=pltpu.VMEM):
        return pltpu.with_memory_space_constraint(operand, space)

    if plain:
        operands = tuple(keep(operand, pltpu.HBM) for operand in operands)
    kept = list(operands) if plain else [keep(operand) for operand in operands[scalars:]]
    kept = kept[scalars:] if plain else kept
    kept += [keep(operand) for operand in after]
    kinds = [shape if isinstance(shape[-1], int) else shape[0] for shape in shapes]
    types = [F32 if isinstance(shape[-1], int) else shape[1] for shape in shapes]
    first = len(operands)

    def run(*refs):
        body(*refs[:first], *refs[first + len(after) :])

    return pl.pallas_call(
        run,
        out_shape=[
            jax.ShapeDtypeStruct(kind, kept_as) if last else pltpu.VMEM(kind, kept_as)
            for kind, kept_as in zip(kinds, types)
        ],
        in_specs=specs,
        out_specs=[pl.BlockSpec(memory_space=pltpu.VMEM)] * len(shapes),
        scratch_shapes=scratch,
        compiler_params=pltpu.CompilerParams(vmem_limit_bytes=8 << 20),
    )(*operands[:scalars], *kept)


def pair(value, axis, bits):
    count = lax.axis_size(axis)
    return lax.ppermute(value, axis, [(i, i ^ bits) for i in range(count)])


def local_short(plan, charges, exponents, amplitudes, top_x, top_y, top_z):
    where = jnp.stack([lax.axis_index(axis) for axis in ("gx", "gy", "gz")]).astype(jnp.int32)
    terms = exponents.shape[1]
    bx, by, bz = plan.brick
    rows, window = plan.fine_rows, plan.window_rows
    bind = functools.partial

    own, sent_z = call(
        bind(start_kernel, plan),
        [(2, bz, LANES), (4 * plan.rim + plan.top_rows // 2, LANES)],
        charges,
        *np_split(plan.top_left),
        *np_split(np.stack(plan.top_right)),
        plain=True,
    )
    got_z = pair(sent_z, "gz", 1)
    table = plan.constants((top_x, top_y, top_z))
    table, params = call(
        bind(setup_kernel, plan, terms),
        [table.shape, (6 * terms + 3 * 16, LANES)],
        exponents,
        amplitudes,
        top_x,
        top_y,
        top_z,
        jnp.asarray(table),
        scalars=2,
        after=(sent_z,),
        plain=True,
        scratch=[pltpu.SemaphoreType.DMA],
    )
    fine, sent_a = call(
        bind(spread_kernel, plan),
        [(2, rows, LANES), (plan.message, LANES)],
        where,
        own,
        sent_z,
        got_z,
        table,
        scalars=1,
    )
    got_a = pair(sent_a, "gx", 1)
    kf = ((terms, 2 * LANES, 8 * LANES), BF16)
    *kf, zf, zf_low = call(
        bind(fine_weights_kernel, plan, terms),
        [kf, kf, ((terms, rows, LANES), BF16), ((terms, rows, LANES), BF16)],
        where,
        params,
        table,
        scalars=1,
        after=(sent_a,),
    )
    (sent_b,) = call(
        bind(pass_kernel, plan), [(plan.message, LANES)], where, fine, sent_a, got_a, scalars=1, after=(zf,)
    )
    got_b = pair(sent_b, "gx", 3)
    k1 = ((terms * plan.out_cells, 12 * LANES), BF16)
    *k1, z1, z1_low, zc, kc = call(
        bind(coarse_weights_kernel, plan, terms),
        [
            k1,
            k1,
            ((terms, window, LANES), BF16),
            ((terms, window, LANES), BF16),
            (LANES, plan.top_rows),
            (plan.out_cells, 2 * LANES),
        ],
        where,
        params,
        table,
        scalars=1,
        after=(sent_b,),
    )
    size = 2 * rows + 3 * window + plan.top_rows
    cells, sent_c = call(
        bind(stack_kernel, plan),
        [(2, 2 * rows, LANES), (size, LANES)],
        where,
        fine,
        sent_a,
        sent_b,
        got_a,
        got_b,
        scalars=1,
        after=(z1,),
    )
    got_c = pair(sent_c, "gy", 3)
    sums = [(terms, 2 * LANES, rows), (terms * plan.out_cells, window)]
    near = call(bind(near_kernel, plan, terms), sums, cells, sent_c, *kf, *k1)
    (sent_d,) = call(
        bind(share_kernel, plan),
        [(size + 3 * window, LANES)],
        where,
        cells,
        sent_c,
        got_c,
        scalars=1,
        after=(near[1],),
    )
    got_d = pair(sent_d, "gy", 1)
    middle = call(bind(middle_kernel, plan, terms), sums, *near, got_c, *kf, *k1, after=(sent_d,))
    (out,) = call(
        bind(far_kernel, plan, terms),
        [(bx, by, bz)],
        *middle,
        sent_d,
        got_d,
        *kf,
        *k1,
        zf,
        zf_low,
        z1,
        z1_low,
        zc,
        kc,
        table,
        last=True,
    )
    return out


def np_split(table):
    high = table.astype(BF16)
    return jnp.asarray(high), jnp.asarray((table - high.astype(np.float32)).astype(BF16))


def local(*arguments):
    counts = tuple(lax.axis_size(axis) for axis in ("gx", "gy", "gz"))
    brick = arguments[0].shape
    if fits(brick, counts, arguments[3:]):
        return local_short(Plan(brick, counts), *arguments)
    return local_any(*arguments)


def solution(mesh):
    in_specs = (P("gx", "gy", "gz"), P(), P(), P(), P(), P())
    out_specs = P("gx", "gy", "gz")
    return jax.shard_map(local, mesh=mesh, in_specs=in_specs, out_specs=out_specs, check_vma=False)
```

```python
import functools

import jax
import jax.numpy as jnp
import numpy as np
from jax import lax
from jax.experimental import pallas as pl
from jax.experimental.pallas import tpu as pltpu
from jax.sharding import PartitionSpec as P

REACH = 8


HIGHEST = lax.Precision.HIGHEST


def with_halo(cells, sides, width):
    for axis, dim in sides:
        count = lax.axis_size(axis)
        head = lax.slice_in_dim(cells, 0, width, axis=dim)
        tail = lax.slice_in_dim(cells, cells.shape[dim] - width, cells.shape[dim], axis=dim)
        cells = jnp.concatenate(
            [
                lax.ppermute(tail, axis, [(i, (i + 1) % count) for i in range(count)]),
                cells,
                lax.ppermute(head, axis, [((i + 1) % count, i) for i in range(count)]),
            ],
            axis=dim,
        )
    return cells


def gauss_taps(exponents):
    offsets = jnp.arange(-REACH, REACH + 1).astype(jnp.float32)
    weights = jnp.exp(-exponents[..., None] * offsets * offsets)
    return weights / jnp.sum(weights, axis=-1, keepdims=True)


def spline(offsets):
    inner_weight = jnp.where((offsets == 1) | (offsets == 2), 0.75, 0.0)
    return jnp.where((offsets == 0) | (offsets == 3), 0.25, inner_weight).astype(jnp.float32)


def band_gauss(tap_table, length):
    rows = jnp.arange(length + 2 * REACH)[:, None]
    cols = jnp.arange(length)[None, :]
    offsets = rows - cols
    onehot = (offsets[:, :, None] == jnp.arange(2 * REACH + 1)[None, None, :]).astype(jnp.float32)
    return jnp.einsum("gk,pok->gpo", tap_table, onehot, precision=HIGHEST)


def band_restrict(length):
    rows = jnp.arange(length + 2)[:, None]
    cols = jnp.arange(length // 2)[None, :]
    return spline(rows - 2 * cols)


def band_prolong(length):
    rows = jnp.arange(length + 2)[:, None]
    cols = jnp.arange(2 * length)[None, :]
    return spline(cols - 2 * rows + 3)


def apply_three(field, band_x, band_y, band_z):
    field = jnp.einsum("xyz,zc->xyc", field, band_z, precision=HIGHEST)
    field = jnp.einsum("xyz,yb->xbz", field, band_y, precision=HIGHEST)
    return jnp.einsum("xyz,xa->ayz", field, band_x, precision=HIGHEST)


def rim_cells(field):
    return with_halo(field, (("gx", 0), ("gy", 1), ("gz", 2)), 1)


def restrict_local(padded):
    sizes = padded.shape
    return apply_three(
        padded,
        band_restrict(sizes[0] - 2),
        band_restrict(sizes[1] - 2),
        band_restrict(sizes[2] - 2),
    )


def prolong_local(field):
    sizes = field.shape
    return apply_three(
        rim_cells(field), band_prolong(sizes[0]), band_prolong(sizes[1]), band_prolong(sizes[2])
    )


def prolong_from_whole(whole_grid, brick):
    padded = jnp.pad(whole_grid, 1, mode="wrap")
    starts = (
        lax.axis_index("gx") * brick[0],
        lax.axis_index("gy") * brick[1],
        lax.axis_index("gz") * brick[2],
    )
    piece_cells = lax.dynamic_slice(padded, starts, (brick[0] + 2, brick[1] + 2, brick[2] + 2))
    return apply_three(
        piece_cells, band_prolong(brick[0]), band_prolong(brick[1]), band_prolong(brick[2])
    )


def assemble(gathered, brick):
    count_x = lax.axis_size("gx")
    count_y = lax.axis_size("gy")
    count_z = lax.axis_size("gz")
    blocks = gathered.reshape(count_x, count_y, count_z, brick[0], brick[1], brick[2])
    blocks = jnp.transpose(blocks, (0, 3, 1, 4, 2, 5))
    return blocks.reshape(count_x * brick[0], count_y * brick[1], count_z * brick[2])


def top_level(field, top_x, top_y, top_z):
    field = jnp.einsum("ia,abc->ibc", top_x, field, precision=HIGHEST)
    field = jnp.einsum("jb,ibc->ijc", top_y, field, precision=HIGHEST)
    return jnp.einsum("kc,ijc->ijk", top_z, field, precision=HIGHEST)


def gauss_and_restrict(field, tap_table, weights):
    size_x, size_y, size_z = field.shape
    band_z = band_gauss(tap_table, size_z)
    band_y = band_gauss(tap_table, size_y)
    band_x = band_gauss(tap_table, size_x) * weights[:, None, None]
    padded = with_halo(field, (("gx", 0), ("gy", 1), ("gz", 2)), REACH)
    along_z = jnp.einsum("xyp,gpo->xygo", padded, band_z, precision=HIGHEST)
    along_y = jnp.einsum("xpgz,gpw->xgwz", along_z, band_y, precision=HIGHEST)
    result = jnp.einsum("pgwz,gpv->vwz", along_y, band_x, precision=HIGHEST)
    inner_cells = padded[
        REACH - 1 : size_x + REACH + 1,
        REACH - 1 : size_y + REACH + 1,
        REACH - 1 : size_z + REACH + 1,
    ]
    coarse = restrict_local(inner_cells)
    return (result, coarse)


def local_any(charges, exponents, amplitudes, top_x, top_y, top_z):
    tap_table = gauss_taps(exponents)
    term_zero, level_one = gauss_and_restrict(charges, tap_table[0], amplitudes[0])
    term_one, level_two = gauss_and_restrict(level_one, tap_table[1], amplitudes[1])
    level_three = restrict_local(rim_cells(level_two))
    level_four = restrict_local(rim_cells(level_three))
    brick_four = level_four.shape
    gathered = lax.all_gather(level_four.reshape(1, -1), ("gx", "gy", "gz"), axis=0, tiled=True)
    phi_four = top_level(assemble(gathered, brick_four), top_x, top_y, top_z)
    phi_three = prolong_from_whole(phi_four, brick_four)
    phi_two = prolong_local(phi_three)
    phi_one = term_one + prolong_local(phi_two)
    return term_zero + prolong_local(phi_one)


F32 = jnp.float32
BF16 = jnp.bfloat16
LANES = 128
FAR = 1.0e9
GAUSSIAN_RIM = REACH + 1


def up8(count):
    return -(-count // 8) * 8


def restrict_weights(fine, coarse):
    offsets = np.asarray(fine)[None, :] - 2 * np.asarray(coarse)[:, None] + 1
    inner = np.where((offsets == 1) | (offsets == 2), 0.75, 0.0)
    return np.where((offsets == 0) | (offsets == 3), 0.25, inner).astype(np.float32)


def reach_four(length):
    total, cells = np.eye(length, dtype=np.float32), np.arange(length)
    for level in range(1, 5):
        coarse = np.arange(-1, length // 2**level + 1)
        total = restrict_weights(cells, coarse) @ total
        cells = coarse
    return total


def prolong_three_whole(count):
    total = np.eye(count, dtype=np.float32)
    for level in range(3):
        size = count * 2**level
        step = np.zeros((2 * size, size), np.float32)
        for cell in range(size):
            for offset, weight in ((-1, 0.25), (0, 0.75), (1, 0.75), (2, 0.25)):
                step[(2 * cell + offset) % (2 * size), cell] += weight
        total = step @ total
    return total


def padded(table, rows, cols):
    out = np.zeros((rows, cols), np.float32)
    out[: table.shape[0], : table.shape[1]] = table
    return out


class Plan:
    def __init__(self, brick, counts):
        self.brick, self.counts = brick, counts
        bx, by, bz = brick
        self.half = by // 2
        self.rim = up8(2 * GAUSSIAN_RIM + 1)
        self.fine_rows = bz + 2 * REACH
        self.cx, self.cy = bx // 2 + 2, by // 2 + 2
        self.window = bz // 2 + 2 * GAUSSIAN_RIM
        self.window_rows = up8(self.window)
        self.out_z = bz // 2 + 2
        self.out_rows = up8(self.out_z)
        self.top_rows = 2 * up8(bz // 16 + 2)
        self.top_z = bz // 16 + 2
        self.top_x, self.top_y = bx // 16 + 2, by // 16 + 2
        self.group = 16
        x_of, y_of = self.own_cells()
        rz = reach_four(bz)
        self.top_left = padded(rz, self.top_rows // 2, bz)
        rx, ry = reach_four(bx), reach_four(by)
        self.top_right, self.rest_right = [], []
        sx = restrict_weights(np.arange(bx), np.arange(-1, bx // 2 + 1))
        sy = restrict_weights(np.arange(by), np.arange(-1, by // 2 + 1))
        for part in range(2):
            y = y_of + part * self.half
            table = rx[:, x_of][:, None, :] * ry[:, y][None, :, :]
            self.top_right.append(padded(table.reshape(-1, LANES).T, LANES, LANES))
            table = sx[:, x_of][:, None, :] * sy[:, y][None, :, :]
            self.rest_right.append(padded(table.reshape(-1, LANES).T, LANES, LANES))
        z_in = np.concatenate([np.arange(bz), bz + np.arange(self.rim), np.arange(-self.rim, 0)])
        z_out = np.arange(-GAUSSIAN_RIM, bz // 2 + GAUSSIAN_RIM)
        self.rest_left = padded(restrict_weights(z_in, z_out), self.window_rows, z_in.size)
        spread = restrict_weights(np.arange(bz), np.arange(-1, bz // 2 + 1)).T
        self.back_left = padded(spread.T, LANES, bz)
        cols = []
        for part in range(2):
            y = y_of + part * self.half
            table = sx[:, x_of][:, None, :] * sy[:, y][None, :, :]
            cols.append(padded(table.reshape(-1, LANES), LANES, LANES))
        self.out_cells = -(-self.cx * self.cy // 16) * 16
        self.back_right = np.concatenate(cols, axis=1).T[:, : self.out_cells]
        self.message = self.fine_rows + self.window_rows + self.top_rows

    def constants(self, kernels):
        rest = self.rest_left
        fine_cells, fine_dz = self.fine_tables()
        coarse_cells, out_cells, coarse_dz = self.coarse_tables()
        spread_x, pick_x, spread_y, pick_y, spread_z, pick_z, lift_x, lift_y = self.top_tables(kernels)
        named = {
            "rest_left": rest[:, :LANES],
            "rest_far": rest[:, LANES:],
            "rest_right": np.concatenate(self.rest_right),
            "fine_cells": fine_cells,
            "fine_dz": fine_dz,
            "coarse_cells": coarse_cells,
            "out_cells": out_cells.reshape(-1, LANES),
            "coarse_dz": coarse_dz,
            "back": self.back_left,
            "back_right": self.back_right,
            "spread_x": spread_x.reshape(-1, 16),
            "pick_x": pick_x.transpose(0, 2, 1, 3).reshape(-1, LANES),
            "spread_y": spread_y.reshape(-1, 16),
            "pick_y": pick_y.transpose(0, 2, 1, 3).reshape(-1, LANES),
            "spread_z": spread_z.reshape(-1, 16),
            "pick_z": pick_z.reshape(-1, self.top_rows),
            "lift_x": lift_x,
            "lift_y": lift_y,
        }
        at, starts, pieces = 0, {}, []
        for name, table in named.items():
            rows = -(-table.shape[0] // 16) * 16
            starts[name] = at
            pieces.append(padded(table, rows, LANES))
            at += rows
        self.starts = starts
        return np.concatenate(pieces)

    def fine_tables(self):
        bx, by, bz = self.brick
        x_of, y_of = self.own_cells()
        strip, x_far = np.arange(LANES) // (LANES // 2), x_of % (LANES // 2 // self.half)
        right, left = bx + x_far, x_far - REACH
        cells = np.stack([x_of, y_of, np.where(strip == 0, right, left), np.where(strip == 0, left, right)])
        z_in = np.concatenate([np.arange(bz), np.arange(-REACH, 0), bz + np.arange(REACH)])
        distance = z_in[:, None] - np.arange(bz)[None, :]
        squared = np.where(np.abs(distance) <= REACH, distance * distance, FAR)
        return padded(cells, 8, LANES), squared.astype(np.float32)

    def coarse_tables(self):
        bx, by, bz = (size // 2 for size in self.brick)
        lane = np.arange(LANES)
        cell, count = lane // self.cy, self.cx * self.cy
        own = cell - 1
        extra = cell >= self.cx
        far_right = np.where(extra, 3 * bx - 1 + cell - self.cx, bx + own)
        far_left = np.where(extra, -2 * bx - 1 + cell - self.cx, own - bx)
        cells = [own, own, own + bx, own - bx, far_left, far_right, lane % self.cy - 1]
        cells += [np.where(lane < count, 0.0, FAR), np.where(cell < self.cx + 2, 0.0, FAR)]
        row = np.arange(self.out_cells)[:, None] + np.zeros((1, LANES))
        outs = np.stack([row // self.cy - 1, row % self.cy - 1, np.where(row < count, 0.0, FAR)])
        z_in, z_out = np.arange(self.window_rows) - GAUSSIAN_RIM, np.arange(LANES) - 1
        distance = z_in[:, None] - z_out[None, :]
        near = (np.abs(distance) <= REACH) & (np.arange(LANES) < self.out_z)[None, :]
        near = near & (np.arange(self.window_rows) < self.window)[:, None]
        squared = np.where(near, distance * distance, FAR)
        return padded(np.stack(cells), 16, LANES), outs.astype(np.float32), squared.astype(np.float32)

    def top_tables(self, kernels):
        four = [size // 16 for size in self.brick]
        lane = np.arange(2 * LANES)
        group, cell, partner = (lane % LANES) // self.group, lane % self.group, lane // LANES
        used = cell < self.top_x * self.top_y
        tables = []
        for axis in range(3):
            count, size = kernels[axis].shape[0], self.brick[axis] // 2
            whole = prolong_three_whole(count)
            outs = (self.cx, self.cy, self.out_z)[axis]
            spread, pick = [], []
            for place in range(self.counts[axis]):
                index = (place * size - 1 + np.arange(outs)) % (8 * count)
                spread.append(padded(whole[index], 16 if axis < 2 else LANES, 16))
                if axis == 0:
                    cells = (place ^ (group % 2) ^ (3 * ((group // 2) % 2))) * four[0] + cell // self.top_y - 1
                    valid = used
                elif axis == 1:
                    cells = (place ^ partner ^ (3 * (group // 4))) * four[1] + cell % self.top_y - 1
                    valid = used
                else:
                    row = np.arange(self.top_rows)
                    side, at = row // (self.top_rows // 2), row % (self.top_rows // 2)
                    cells = (place ^ side) * four[2] + at - 1
                    valid = at < self.top_z
                hot = (np.arange(count)[:, None] == (cells % count)[None, :]) & valid[None, :]
                hot = padded(hot, 16, cells.size)
                pick.append(hot if axis == 2 else hot.reshape(16, 2, LANES))
            tables += [np.stack(spread), np.stack(pick)]
        out = np.arange(self.out_cells)
        tables.append((out[:, None] // self.cy == np.arange(16)[None, :]).astype(np.float32))
        tables.append((out[:, None] % self.cy == np.arange(16)[None, :]).astype(np.float32))
        return tables

    def own_cells(self):
        lane = np.arange(LANES)
        return lane // self.half, lane % self.half


def fits(brick, counts, tops):
    bx, by, bz = brick
    return (
        counts == (4, 4, 2)
        and bx * (by // 2) == LANES
        and by % 16 == 0
        and bx % 16 == 0
        and bz == LANES
        and bx // 2 == REACH
        and by // 2 == REACH
        and (bx // 2 + 4) * (by // 2 + 2) <= LANES
        and (bx // 16 + 2) * (by // 16 + 2) <= 16
        and max(top.shape[0] for top in tops) <= 16
    )


def split(value):
    high = value.astype(BF16)
    return high, (value - high.astype(F32)).astype(BF16)


def dot(left, right):
    return jnp.dot(left, right, preferred_element_type=F32)


def dot_left(exact, value):
    high, low = split(value)
    return dot(exact, high) + dot(exact, low)


def dot_right(value, exact):
    high, low = split(value)
    return dot(high, exact) + dot(low, exact)


def dot_split(left, right):
    return dot(left[0], right[0]) + dot(left[1], right[0]) + dot(left[0], right[1])


def exact_tables(plan, ref):
    def read(name, rows, at=0):
        start = plan.starts[name] + at * rows
        return ref[start : start + rows].astype(BF16)

    return read


def lanes_of(rows):
    return lax.broadcasted_iota(jnp.int32, (rows, LANES), 1)


def halves(first, second):
    low = lanes_of(first.shape[0]) < LANES // 2
    return (
        jnp.where(low, first, pltpu.roll(second, LANES // 2, 1)),
        jnp.where(low, pltpu.roll(first, LANES // 2, 1), second),
    )


def start_kernel(plan, charges_ref, table_ref, own_ref, out_ref):
    bx, by, bz = plan.brick
    rim, half = plan.rim, plan.half
    top, size = None, plan.top_rows // 2
    left = split(table_ref[:size])
    for part in range(2):
        cells = charges_ref[:, part * half : (part + 1) * half, :].reshape(LANES, bz).T
        own_ref[part] = cells
        out_ref[2 * rim * part : 2 * rim * part + rim] = cells[:rim]
        out_ref[2 * rim * part + rim : 2 * rim * (part + 1)] = cells[bz - rim :]
        right = split(table_ref[size + LANES * part : size + LANES * (part + 1)])
        rows = dot_split(split(dot_split(left, split(cells))), right)
        top = rows if top is None else top + rows
    out_ref[4 * rim :] = top


def setup_kernel(plan, terms, exponents_ref, amplitudes_ref, tops_x_ref, tops_y_ref, tops_z_ref, table_ref, kept_ref,
                 params_ref, semaphore):
    copy = pltpu.make_async_copy(table_ref, kept_ref, semaphore)
    copy.start()
    offsets = lax.broadcasted_iota(jnp.int32, (1, LANES), 1).astype(F32) - REACH
    squared = jnp.where(offsets <= REACH, offsets * offsets, FAR)
    for level in range(2):
        for term in range(terms):
            exponent = exponents_ref[level, term]
            scale = 1.0 / jnp.sum(jnp.exp(squared * -exponent), axis=1, keepdims=True)
            scale = jnp.broadcast_to(scale, (1, LANES))
            row = 3 * terms * level + term
            params_ref[row : row + 1] = jnp.zeros((1, LANES), F32) + exponent
            row = row + terms
            params_ref[row : row + 1] = scale * scale * amplitudes_ref[level, term]
            row = row + terms
            params_ref[row : row + 1] = scale
    params_ref[6 * terms :] = jnp.zeros((3 * 16, LANES), F32)
    for axis, source in enumerate((tops_x_ref, tops_y_ref, tops_z_ref)):
        at, count = 6 * terms + 16 * axis, source.shape[0]
        params_ref[at : at + count, :count] = source[...]
    copy.wait()


def spread_kernel(plan, place_ref, own_ref, sent_ref, got_ref, table_ref, fine_ref, out_ref, side_x_ref,
                  side_y_ref):
    bx, by, bz = plan.brick
    rim, rows = plan.rim, plan.fine_rows
    table = exact_tables(plan, table_ref)
    coarse = None
    for part in range(2):
        cells = own_ref[part]
        far = got_ref[2 * rim * part : 2 * rim * (part + 1)]
        fine_ref[part, :bz] = cells
        fine_ref[part, bz : bz + REACH] = far[2 * rim - REACH :]
        fine_ref[part, bz + REACH :] = far[:REACH]
        summed = dot_left(table("rest_left", plan.window_rows), cells)
        summed = summed + dot_left(table("rest_far", plan.window_rows)[:, : 2 * rim], far)
        summed = dot_right(summed, table("rest_right", LANES, part))
        coarse = summed if coarse is None else coarse + summed
    low, high = halves(fine_ref[0], fine_ref[1])
    even = place_ref[0] % 2 == 0
    out_ref[:rows] = jnp.where(even, high, low)
    side_x_ref[...] = jnp.where(even, low, high)
    side_y_ref[:rows] = jnp.where(place_ref[1] % 2 == 0, fine_ref[0], fine_ref[1])
    side_y_ref[rows:] = coarse
    out_ref[rows : rows + plan.window_rows] = coarse
    top = rows + plan.window_rows
    out_ref[top : top + plan.top_rows // 2] = sent_ref[4 * rim :]
    out_ref[top + plan.top_rows // 2 :] = got_ref[4 * rim :]


def pass_kernel(plan, place_ref, sent_ref, got_ref, out_ref):
    rows = plan.fine_rows
    even = place_ref[0] % 2 == 0
    own = sent_ref[rows : rows + plan.window_rows]
    far = got_ref[rows : rows + plan.window_rows]
    lane = lanes_of(plan.window_rows)
    edge, all_lanes = 2 * plan.cy, plan.cx * plan.cy
    last = all_lanes - edge
    right = own + jnp.where((lane >= last) & (lane < all_lanes), pltpu.roll(far, last, 1), 0.0)
    right = right + jnp.where((lane >= all_lanes) & (lane < all_lanes + edge), pltpu.roll(far, edge, 1), 0.0)
    left = own + jnp.where(lane < edge, pltpu.roll(far, LANES - last, 1), 0.0)
    left = left + jnp.where((lane >= all_lanes) & (lane < all_lanes + edge), pltpu.roll(far, all_lanes, 1), 0.0)
    out_ref[: plan.window_rows] = jnp.where(even, right, left)
    top = rows + plan.window_rows
    out_ref[plan.window_rows :] = sent_ref[top:] + pltpu.roll(got_ref[top:], plan.group, 1)


def stack_kernel(plan, place_ref, fine_ref, sent_ref, first_ref, side_ref, second_ref, cells_ref, out_ref):
    rows, window = plan.fine_rows, plan.window_rows
    low, high = halves(first_ref[:rows], side_ref[...])
    for part, other in ((0, low), (1, high)):
        cells_ref[part, :rows] = fine_ref[part]
        cells_ref[part, rows:] = other
    out_ref[:rows] = jnp.where(place_ref[1] % 2 == 0, low, high)
    out_ref[rows : rows + window] = first_ref[rows : rows + window]
    out_ref[rows + window : rows + 2 * window] = second_ref[:window]
    out_ref[rows + 2 * window :] = sent_ref[window:] + pltpu.roll(second_ref[window:], 2 * plan.group, 1)


def share_kernel(plan, place_ref, cells_ref, own_ref, sent_ref, side_ref, got_ref, out_ref):
    rows, window = plan.fine_rows, plan.window_rows
    even = place_ref[1] % 2 == 0
    out_ref[: 2 * rows] = jnp.where(even, cells_ref[1], cells_ref[0])
    at = 2 * rows
    for source, start, count in ((own_ref, rows, 1), (sent_ref, rows, 2), (side_ref, rows, 1), (got_ref, rows, 2)):
        out_ref[at : at + count * window] = source[start : start + count * window]
        at = at + count * window
    start = rows + 2 * window
    out_ref[at:] = sent_ref[start:] + pltpu.roll(got_ref[start:], 4 * plan.group, 1)


def dot_turned(left, right):
    def product(first, second):
        return lax.dot_general(first, second, (((1,), (1,)), ((), ())), preferred_element_type=F32)

    return product(left[0], right[0]) + product(left[1], right[0]) + product(left[0], right[1])


def fine_weights_kernel(plan, terms, place_ref, params_ref, table_ref, kf_ref, kf_low_ref, zf_ref, zf_low_ref):
    bx, by, bz = plan.brick
    cells_ref = table_ref.at[pl.ds(plan.starts["fine_cells"], 8)]
    dz_ref = table_ref.at[pl.ds(plan.starts["fine_dz"], plan.fine_rows)]
    half = plan.half
    even_x, even_y = place_ref[0] % 2 == 0, place_ref[1] % 2 == 0
    own_x, own_y = cells_ref[0:1], cells_ref[1:2]
    far_x = jnp.where(even_x, cells_ref[2:3], cells_ref[3:4])
    x_out = lax.broadcasted_iota(jnp.int32, (bx, LANES), 0).astype(F32)
    y_out = lax.broadcasted_iota(jnp.int32, (half, LANES), 0).astype(F32)
    y_low, y_high = F32(-half), F32(by)
    y_far = jnp.where(even_y, y_low, y_high), jnp.where(even_y, y_high, y_low)

    def decay(exponent, distance):
        return jnp.where(jnp.abs(distance) <= REACH, jnp.exp(-exponent * distance * distance), 0.0)

    for term in range(terms):
        exponent = params_ref[term : term + 1]
        scale = params_ref[terms + term : terms + term + 1]
        along_x = [decay(exponent, x_in - x_out)[:, None, :] for x_in in (own_x, far_x)]
        for group in range(4):
            y_in = own_y + (F32(group * half) if group < 2 else y_far[group - 2])
            for part in range(2):
                along_y = decay(exponent, y_in - (y_out + part * half)) * scale
                for block in range(2):
                    high, low = split((along_x[block] * along_y[None]).reshape(bx * half, LANES))
                    rows, cols = pl.ds(part * LANES, LANES), pl.ds((2 * group + block) * LANES, LANES)
                    kf_ref[term, rows, cols] = high
                    kf_low_ref[term, rows, cols] = low
        zf_ref[term], zf_low_ref[term] = split(
            jnp.exp(-exponent * dz_ref[...]) * params_ref[2 * terms + term : 2 * terms + term + 1]
        )


def coarse_weights_kernel(plan, terms, place_ref, params_ref, table_ref, k1_ref, k1_low_ref, z1_ref, z1_low_ref,
                          zc_ref, kc_ref):
    cells_ref = table_ref.at[pl.ds(plan.starts["coarse_cells"], 16)]
    at, count = plan.starts["out_cells"], plan.out_cells
    out_cells_ref = [table_ref[at + count * part : at + count * (part + 1)] for part in range(3)]
    dz_ref = table_ref.at[pl.ds(plan.starts["coarse_dz"], plan.window_rows)]
    zc_ref[...], kc_ref[...] = top_weights(plan, terms, place_ref, params_ref, table_ref)
    bx, by = plan.brick[0] // 2, plan.brick[1] // 2
    even_x, even_y = place_ref[0] % 2 == 0, place_ref[1] % 2 == 0
    base = 3 * terms

    def squared(distance, count):
        distance = distance - count * jnp.floor((distance + count // 2) * (1.0 / count))
        return jnp.where(jnp.abs(distance) <= REACH, distance * distance, FAR)

    x_out, y_out = out_cells_ref[0], out_cells_ref[1]
    squares_x = []
    for slot in range(3):
        x_in = jnp.where(even_x, cells_ref[2 * slot : 2 * slot + 1], cells_ref[2 * slot + 1 : 2 * slot + 2])
        used = cells_ref[7:8] if slot < 2 else cells_ref[8:9]
        squares_x.append(squared(x_in - x_out, bx * plan.counts[0]) + used)
    toward = jnp.where(even_y, F32(by), F32(-by))
    for group, offset in enumerate((F32(0), -toward, toward, F32(2 * by))):
        square_y = squared(cells_ref[6:7] + offset - y_out, by * plan.counts[1]) + out_cells_ref[2]
        for slot in range(3):
            total = squares_x[slot] + square_y
            cols = pl.ds((3 * group + slot) * LANES, LANES)
            for term in range(terms):
                exponent = params_ref[base + term : base + term + 1]
                scale = params_ref[base + terms + term : base + terms + term + 1]
                high, low = split(jnp.exp(-exponent * total) * scale)
                rows = pl.ds(term * plan.out_cells, plan.out_cells)
                k1_ref[rows, cols] = high
                k1_low_ref[rows, cols] = low
    for term in range(terms):
        exponent = params_ref[base + term : base + term + 1]
        scale = params_ref[base + 2 * terms + term : base + 2 * terms + term + 1]
        z1_ref[term], z1_low_ref[term] = split(jnp.exp(-exponent * dz_ref[...]) * scale)


def top_weights(plan, terms, place_ref, params_ref, table_ref):
    def chain(*factors):
        value = factors[0]
        for factor in factors[1:]:
            value = dot_split(split(value), split(factor))
        return value

    def read(name, rows, at=0):
        return table_ref[pl.ds(pl.multiple_of(plan.starts[name] + at * rows, 8), rows)]

    size = 16
    along = []
    for axis, (spread, pick) in enumerate((("spread_x", "pick_x"), ("spread_y", "pick_y"))):
        top = params_ref[6 * terms + size * axis : 6 * terms + size * (axis + 1)]
        picked = read(pick, 2 * size, place_ref[axis])
        picked = jnp.concatenate([picked[:size], picked[size:]], axis=1)
        value = chain(read(spread, size, place_ref[axis])[:, :size], top)[:, :size]
        along.append(chain(value, picked))
    top = params_ref[6 * terms + 2 * size : 6 * terms + 3 * size]
    value = chain(read("spread_z", LANES, place_ref[2])[:, :size], top)[:, :size]
    left = chain(value, read("pick_z", size, place_ref[2])[:, : plan.top_rows])
    lift_x, lift_y = (read(name, plan.out_cells)[:, :size] for name in ("lift_x", "lift_y"))
    return left, chain(lift_x, along[0]) * chain(lift_y, along[1])


def side_by_side(source, start, rows, count):
    return jnp.concatenate([source[start + rows * at : start + rows * (at + 1)] for at in range(count)], axis=1)


def gather_part(plan, terms, blocks, near, kf_refs, k1_refs, fine_at, coarse_at, before):
    cells, near = split(blocks), split(near)
    fine_cols = pl.ds(fine_at * LANES, blocks.shape[1])
    fine = []
    for term in range(terms):
        value = dot_turned((kf_refs[0][term, :, fine_cols], kf_refs[1][term, :, fine_cols]), cells)
        fine.append(value if before is None else before[0][term] + value)
    cols = pl.ds(coarse_at * LANES, near[0].shape[1])
    coarse = dot_turned((k1_refs[0][:, cols], k1_refs[1][:, cols]), near)
    return fine, coarse if before is None else before[1][...] + coarse


def near_kernel(plan, terms, cells_ref, own_ref, first_ref, second_ref, kf_ref, kf_low_ref, k1_ref, k1_low_ref, fine_ref, coarse_ref):
    rows, window = plan.fine_rows, plan.window_rows
    blocks = [cells_ref[part, at : at + rows] for part in range(2) for at in (0, rows)]
    near = [own_ref[rows : rows + window], first_ref[rows : rows + window], second_ref[:window]]
    near = jnp.concatenate(near, axis=1)
    fine, coarse = gather_part(plan, terms, jnp.concatenate(blocks, axis=1), near, (kf_ref, kf_low_ref),
                               (k1_ref, k1_low_ref), 0, 0, None)
    for term in range(terms):
        fine_ref[term] = fine[term]
    coarse_ref[...] = coarse


def middle_kernel(plan, terms, fine_in_ref, coarse_in_ref, side_ref, got_ref, kf_ref, kf_low_ref, k1_ref, k1_low_ref,
                  fine_ref, coarse_ref):
    rows, window = plan.fine_rows, plan.window_rows
    blocks = jnp.concatenate([side_ref[:rows], got_ref[:rows]], axis=1)
    near = jnp.concatenate([side_ref[rows:], side_by_side(got_ref, rows, window, 2)], axis=1)
    fine, coarse = gather_part(plan, terms, blocks, near, (kf_ref, kf_low_ref), (k1_ref, k1_low_ref), 4, 3,
                               (fine_in_ref, coarse_in_ref))
    for term in range(terms):
        fine_ref[term] = fine[term]
    coarse_ref[...] = coarse


def far_kernel(plan, terms, fine_in_ref, coarse_in_ref, sent_ref, got_ref, kf_ref, kf_low_ref, k1_ref, k1_low_ref,
               zf_ref, zf_low_ref, z1_ref, z1_low_ref, zc_ref, kc_ref, table_ref, out_ref):
    rows, window, half = plan.fine_rows, plan.window_rows, plan.half
    blocks, near = side_by_side(got_ref, 0, rows, 2), side_by_side(got_ref, 2 * rows, window, 6)
    fine, coarse = gather_part(plan, terms, blocks, near, (kf_ref, kf_low_ref), (k1_ref, k1_low_ref), 6, 6,
                               (fine_in_ref, coarse_in_ref))
    at = 2 * rows + 6 * window
    top = jnp.concatenate([sent_ref[at : at + plan.top_rows], got_ref[at : at + plan.top_rows]], axis=1)
    top = dot_split(split(zc_ref[...]), split(top))
    level_one = dot_turned(split(kc_ref[...]), split(top))
    total = None
    for term in range(terms):
        piece = split(coarse[term * plan.out_cells : (term + 1) * plan.out_cells])
        level_one = level_one + dot_split(piece, (z1_ref[term], z1_low_ref[term]))
        value = dot_split(split(fine[term]), (zf_ref[term], zf_low_ref[term]))
        total = value if total is None else total + value
    table = exact_tables(plan, table_ref)
    back = dot_right(level_one, table("back", LANES))
    total = total + dot_left(table("back_right", 2 * LANES)[:, : plan.out_cells], back)
    for part in range(2):
        cells = total[part * LANES : (part + 1) * LANES]
        out_ref[:, part * half : (part + 1) * half, :] = cells.reshape(plan.brick[0], half, plan.brick[2])


def call(body, shapes, *operands, scalars=0, after=(), last=False, plain=False, scratch=()):
    specs = [pl.BlockSpec(memory_space=pltpu.SMEM)] * scalars
    specs += [pl.BlockSpec(memory_space=pltpu.VMEM)] * (len(operands) - scalars)
    if scratch:
        specs[-1] = pl.BlockSpec(memory_space=pl.ANY)
    specs += [pl.BlockSpec(memory_space=pl.ANY)] * len(after)

    def keep(operand, space=pltpu.VMEM):
        return pltpu.with_memory_space_constraint(operand, space)

    if plain:
        operands = tuple(keep(operand, pltpu.HBM) for operand in operands)
    kept = list(operands) if plain else [keep(operand) for operand in operands[scalars:]]
    kept = kept[scalars:] if plain else kept
    kept += [keep(operand) for operand in after]
    kinds = [shape if isinstance(shape[-1], int) else shape[0] for shape in shapes]
    types = [F32 if isinstance(shape[-1], int) else shape[1] for shape in shapes]
    first = len(operands)

    def run(*refs):
        body(*refs[:first], *refs[first + len(after) :])

    return pl.pallas_call(
        run,
        out_shape=[
            jax.ShapeDtypeStruct(kind, kept_as) if last else pltpu.VMEM(kind, kept_as)
            for kind, kept_as in zip(kinds, types)
        ],
        in_specs=specs,
        out_specs=[pl.BlockSpec(memory_space=pltpu.VMEM)] * len(shapes),
        scratch_shapes=scratch,
        compiler_params=pltpu.CompilerParams(vmem_limit_bytes=8 << 20),
    )(*operands[:scalars], *kept)


def pair(value, axis, bits):
    count = lax.axis_size(axis)
    return lax.ppermute(value, axis, [(i, i ^ bits) for i in range(count)])


def local_short(plan, charges, exponents, amplitudes, top_x, top_y, top_z):
    where = jnp.stack([lax.axis_index(axis) for axis in ("gx", "gy", "gz")]).astype(jnp.int32)
    terms = exponents.shape[1]
    bx, by, bz = plan.brick
    rows, window = plan.fine_rows, plan.window_rows
    bind = functools.partial

    own, sent_z = call(
        bind(start_kernel, plan),
        [(2, bz, LANES), (4 * plan.rim + plan.top_rows // 2, LANES)],
        charges,
        jnp.asarray(np.concatenate([plan.top_left, *plan.top_right])),
        plain=True,
    )
    got_z = pair(sent_z, "gz", 1)
    table = plan.constants((top_x, top_y, top_z))
    table, params = call(
        bind(setup_kernel, plan, terms),
        [table.shape, (6 * terms + 3 * 16, LANES)],
        exponents,
        amplitudes,
        top_x,
        top_y,
        top_z,
        jnp.asarray(table),
        scalars=2,
        after=(sent_z,),
        plain=True,
        scratch=[pltpu.SemaphoreType.DMA],
    )
    fine, sent_a, side_x, side_y = call(
        bind(spread_kernel, plan),
        [(2, rows, LANES), (plan.message, LANES), (rows, LANES), (rows + window, LANES)],
        where,
        own,
        sent_z,
        got_z,
        table,
        scalars=1,
    )
    got_a = pair(sent_a, "gx", 1)
    got_x = pair(side_x, "gx", 3)
    got_y = pair(side_y, "gy", 3)
    (sent_b,) = call(
        bind(pass_kernel, plan), [(plan.message - rows, LANES)], where, sent_a, got_a, scalars=1
    )
    got_b = pair(sent_b, "gx", 3)
    k1 = ((terms * plan.out_cells, 12 * LANES), BF16)
    *k1, z1, z1_low, zc, kc = call(
        bind(coarse_weights_kernel, plan, terms),
        [
            k1,
            k1,
            ((terms, window, LANES), BF16),
            ((terms, window, LANES), BF16),
            (LANES, plan.top_rows),
            (plan.out_cells, 2 * LANES),
        ],
        where,
        params,
        table,
        scalars=1,
        after=(sent_b,),
    )
    size = rows + 2 * window + plan.top_rows
    cells, sent_c = call(
        bind(stack_kernel, plan),
        [(2, 2 * rows, LANES), (size, LANES)],
        where,
        fine,
        sent_b,
        got_a,
        got_x,
        got_b,
        scalars=1,
        after=(z1, got_y),
    )
    got_c = pair(sent_c, "gy", 3)
    kf = ((terms, 2 * LANES, 8 * LANES), BF16)
    *kf, zf, zf_low = call(
        bind(fine_weights_kernel, plan, terms),
        [kf, kf, ((terms, rows, LANES), BF16), ((terms, rows, LANES), BF16)],
        where,
        params,
        table,
        scalars=1,
        after=(sent_c,),
    )
    sums = [(terms, 2 * LANES, rows), (terms * plan.out_cells, window)]
    near = call(bind(near_kernel, plan, terms), sums, cells, sent_a, got_a, got_b, *kf, *k1, after=(sent_c,))
    (sent_d,) = call(
        bind(share_kernel, plan),
        [(2 * rows + 6 * window + plan.top_rows, LANES)],
        where,
        cells,
        sent_a,
        sent_c,
        got_y,
        got_c,
        scalars=1,
        after=(near[1],),
    )
    got_d = pair(sent_d, "gy", 1)
    middle = call(bind(middle_kernel, plan, terms), sums, *near, got_y, got_c, *kf, *k1, after=(sent_d,))
    (out,) = call(
        bind(far_kernel, plan, terms),
        [(bx, by, bz)],
        *middle,
        sent_d,
        got_d,
        *kf,
        *k1,
        zf,
        zf_low,
        z1,
        z1_low,
        zc,
        kc,
        table,
        last=True,
    )
    return out


def local(*arguments):
    counts = tuple(lax.axis_size(axis) for axis in ("gx", "gy", "gz"))
    brick = arguments[0].shape
    if fits(brick, counts, arguments[3:]):
        return local_short(Plan(brick, counts), *arguments)
    return local_any(*arguments)


def solution(mesh):
    in_specs = (P("gx", "gy", "gz"), P(), P(), P(), P(), P())
    out_specs = P("gx", "gy", "gz")
    return jax.shard_map(local, mesh=mesh, in_specs=in_specs, out_specs=out_specs, check_vma=False)
```

```python
import functools

import jax
import jax.numpy as jnp
import numpy as np
from jax import lax
from jax.experimental import pallas as pl
from jax.experimental.pallas import tpu as pltpu
from jax.sharding import PartitionSpec as P


REACH = 8


HIGHEST = lax.Precision.HIGHEST


def with_halo(cells, sides, width):
    for axis, dim in sides:
        count = lax.axis_size(axis)
        head = lax.slice_in_dim(cells, 0, width, axis=dim)
        tail = lax.slice_in_dim(cells, cells.shape[dim] - width, cells.shape[dim], axis=dim)
        cells = jnp.concatenate(
            [
                lax.ppermute(tail, axis, [(i, (i + 1) % count) for i in range(count)]),
                cells,
                lax.ppermute(head, axis, [((i + 1) % count, i) for i in range(count)]),
            ],
            axis=dim,
        )
    return cells


def gauss_taps(exponents):
    offsets = jnp.arange(-REACH, REACH + 1).astype(jnp.float32)
    weights = jnp.exp(-exponents[..., None] * offsets * offsets)
    return weights / jnp.sum(weights, axis=-1, keepdims=True)


def spline(offsets):
    inner_weight = jnp.where((offsets == 1) | (offsets == 2), 0.75, 0.0)
    return jnp.where((offsets == 0) | (offsets == 3), 0.25, inner_weight).astype(jnp.float32)


def band_gauss(tap_table, length):
    rows = jnp.arange(length + 2 * REACH)[:, None]
    cols = jnp.arange(length)[None, :]
    offsets = rows - cols
    onehot = (offsets[:, :, None] == jnp.arange(2 * REACH + 1)[None, None, :]).astype(jnp.float32)
    return jnp.einsum("gk,pok->gpo", tap_table, onehot, precision=HIGHEST)


def band_restrict(length):
    rows = jnp.arange(length + 2)[:, None]
    cols = jnp.arange(length // 2)[None, :]
    return spline(rows - 2 * cols)


def band_prolong(length):
    rows = jnp.arange(length + 2)[:, None]
    cols = jnp.arange(2 * length)[None, :]
    return spline(cols - 2 * rows + 3)


def apply_three(field, band_x, band_y, band_z):
    field = jnp.einsum("xyz,zc->xyc", field, band_z, precision=HIGHEST)
    field = jnp.einsum("xyz,yb->xbz", field, band_y, precision=HIGHEST)
    return jnp.einsum("xyz,xa->ayz", field, band_x, precision=HIGHEST)


def rim_cells(field):
    return with_halo(field, (("gx", 0), ("gy", 1), ("gz", 2)), 1)


def restrict_local(padded):
    sizes = padded.shape
    return apply_three(
        padded,
        band_restrict(sizes[0] - 2),
        band_restrict(sizes[1] - 2),
        band_restrict(sizes[2] - 2),
    )


def prolong_local(field):
    sizes = field.shape
    return apply_three(
        rim_cells(field), band_prolong(sizes[0]), band_prolong(sizes[1]), band_prolong(sizes[2])
    )


def prolong_from_whole(whole_grid, brick):
    padded = jnp.pad(whole_grid, 1, mode="wrap")
    starts = (
        lax.axis_index("gx") * brick[0],
        lax.axis_index("gy") * brick[1],
        lax.axis_index("gz") * brick[2],
    )
    piece_cells = lax.dynamic_slice(padded, starts, (brick[0] + 2, brick[1] + 2, brick[2] + 2))
    return apply_three(
        piece_cells, band_prolong(brick[0]), band_prolong(brick[1]), band_prolong(brick[2])
    )


def assemble(gathered, brick):
    count_x = lax.axis_size("gx")
    count_y = lax.axis_size("gy")
    count_z = lax.axis_size("gz")
    blocks = gathered.reshape(count_x, count_y, count_z, brick[0], brick[1], brick[2])
    blocks = jnp.transpose(blocks, (0, 3, 1, 4, 2, 5))
    return blocks.reshape(count_x * brick[0], count_y * brick[1], count_z * brick[2])


def top_level(field, top_x, top_y, top_z):
    field = jnp.einsum("ia,abc->ibc", top_x, field, precision=HIGHEST)
    field = jnp.einsum("jb,ibc->ijc", top_y, field, precision=HIGHEST)
    return jnp.einsum("kc,ijc->ijk", top_z, field, precision=HIGHEST)


def gauss_and_restrict(field, tap_table, weights):
    size_x, size_y, size_z = field.shape
    band_z = band_gauss(tap_table, size_z)
    band_y = band_gauss(tap_table, size_y)
    band_x = band_gauss(tap_table, size_x) * weights[:, None, None]
    padded = with_halo(field, (("gx", 0), ("gy", 1), ("gz", 2)), REACH)
    along_z = jnp.einsum("xyp,gpo->xygo", padded, band_z, precision=HIGHEST)
    along_y = jnp.einsum("xpgz,gpw->xgwz", along_z, band_y, precision=HIGHEST)
    result = jnp.einsum("pgwz,gpv->vwz", along_y, band_x, precision=HIGHEST)
    inner_cells = padded[
        REACH - 1 : size_x + REACH + 1,
        REACH - 1 : size_y + REACH + 1,
        REACH - 1 : size_z + REACH + 1,
    ]
    coarse = restrict_local(inner_cells)
    return (result, coarse)


def local_any(charges, exponents, amplitudes, top_x, top_y, top_z):
    tap_table = gauss_taps(exponents)
    term_zero, level_one = gauss_and_restrict(charges, tap_table[0], amplitudes[0])
    term_one, level_two = gauss_and_restrict(level_one, tap_table[1], amplitudes[1])
    level_three = restrict_local(rim_cells(level_two))
    level_four = restrict_local(rim_cells(level_three))
    brick_four = level_four.shape
    gathered = lax.all_gather(level_four.reshape(1, -1), ("gx", "gy", "gz"), axis=0, tiled=True)
    phi_four = top_level(assemble(gathered, brick_four), top_x, top_y, top_z)
    phi_three = prolong_from_whole(phi_four, brick_four)
    phi_two = prolong_local(phi_three)
    phi_one = term_one + prolong_local(phi_two)
    return term_zero + prolong_local(phi_one)


F32 = jnp.float32
BF16 = jnp.bfloat16
LANES = 128
FAR = 1.0e9
GAUSSIAN_RIM = REACH + 1


def up8(count):
    return -(-count // 8) * 8


def restrict_weights(fine, coarse):
    offsets = np.asarray(fine)[None, :] - 2 * np.asarray(coarse)[:, None] + 1
    inner = np.where((offsets == 1) | (offsets == 2), 0.75, 0.0)
    return np.where((offsets == 0) | (offsets == 3), 0.25, inner).astype(np.float32)


def reach_four(length):
    total, cells = np.eye(length, dtype=np.float32), np.arange(length)
    for level in range(1, 5):
        coarse = np.arange(-1, length // 2**level + 1)
        total = restrict_weights(cells, coarse) @ total
        cells = coarse
    return total


def prolong_three_whole(count):
    total = np.eye(count, dtype=np.float32)
    for level in range(3):
        size = count * 2**level
        step = np.zeros((2 * size, size), np.float32)
        for cell in range(size):
            for offset, weight in ((-1, 0.25), (0, 0.75), (1, 0.75), (2, 0.25)):
                step[(2 * cell + offset) % (2 * size), cell] += weight
        total = step @ total
    return total


def padded(table, rows, cols):
    out = np.zeros((rows, cols), np.float32)
    out[: table.shape[0], : table.shape[1]] = table
    return out


class Plan:
    def __init__(self, brick, counts):
        self.brick, self.counts = brick, counts
        bx, by, bz = brick
        self.half = by // 2
        self.rim = up8(2 * GAUSSIAN_RIM + 1)
        self.fine_rows = bz + 2 * REACH
        self.cx, self.cy = bx // 2 + 2, by // 2 + 2
        self.window = bz // 2 + 2 * GAUSSIAN_RIM
        self.window_rows = up8(self.window)
        self.out_z = bz // 2 + 2
        self.top_rows = 2 * up8(bz // 16 + 2)
        self.top_z = bz // 16 + 2
        self.top_x, self.top_y = bx // 16 + 2, by // 16 + 2
        self.group = 16
        x_of, y_of = self.own_cells()
        rz = reach_four(bz)
        self.top_left = padded(rz, self.top_rows // 2, bz)
        rx, ry = reach_four(bx), reach_four(by)
        self.top_right, self.rest_right = [], []
        sx = restrict_weights(np.arange(bx), np.arange(-1, bx // 2 + 1))
        sy = restrict_weights(np.arange(by), np.arange(-1, by // 2 + 1))
        for part in range(2):
            y = y_of + part * self.half
            table = rx[:, x_of][:, None, :] * ry[:, y][None, :, :]
            self.top_right.append(padded(table.reshape(-1, LANES).T, LANES, LANES))
            table = sx[:, x_of][:, None, :] * sy[:, y][None, :, :]
            self.rest_right.append(padded(table.reshape(-1, LANES).T, LANES, LANES))
        z_in = np.concatenate([np.arange(bz), bz + np.arange(self.rim), np.arange(-self.rim, 0)])
        z_out = np.arange(-GAUSSIAN_RIM, bz // 2 + GAUSSIAN_RIM)
        self.rest_left = padded(restrict_weights(z_in, z_out), self.window_rows, z_in.size)
        spread = restrict_weights(np.arange(bz), np.arange(-1, bz // 2 + 1)).T
        self.back_left = padded(spread.T, LANES, bz)
        cols = []
        for part in range(2):
            y = y_of + part * self.half
            table = sx[:, x_of][:, None, :] * sy[:, y][None, :, :]
            cols.append(padded(table.reshape(-1, LANES), LANES, LANES))
        self.out_cells = -(-self.cx * self.cy // 16) * 16
        self.back_right = np.concatenate(cols, axis=1).T[:, : self.out_cells]
        self.message = self.fine_rows + self.window_rows + self.top_rows

    def constants(self, kernels):
        rest = self.rest_left
        fine_cells, fine_dz = self.fine_tables()
        coarse_cells, out_cells, coarse_dz = self.coarse_tables()
        spread_x, pick_x, spread_y, pick_y, spread_z, pick_z, lift_x, lift_y = self.top_tables(kernels)
        named = {
            "rest_left": rest[:, :LANES],
            "rest_far": rest[:, LANES:],
            "rest_right": np.concatenate(self.rest_right),
            "fine_cells": fine_cells,
            "fine_dz": fine_dz,
            "coarse_cells": coarse_cells,
            "out_cells": out_cells.reshape(-1, LANES),
            "coarse_dz": coarse_dz,
            "back": self.back_left,
            "back_right": self.back_right,
            "spread_x": spread_x.reshape(-1, 16),
            "pick_x": pick_x[:, :, 0].reshape(-1, LANES),
            "spread_y": spread_y.reshape(-1, 16),
            "pick_y": pick_y[:, :, 0].reshape(-1, LANES),
            "pick_pair": pick_y[:, :, 1].reshape(-1, LANES),
            "spread_z": spread_z.reshape(-1, 16),
            "pick_z": pick_z.reshape(-1, self.top_rows),
            "lift_x": lift_x,
            "lift_y": lift_y,
        }
        at, starts, pieces = 0, {}, []
        for name, table in named.items():
            rows = -(-table.shape[0] // 16) * 16
            starts[name] = at
            pieces.append(padded(table, rows, LANES))
            at += rows
        self.starts = starts
        return np.concatenate(pieces)

    def fine_tables(self):
        bx, _, bz = self.brick
        x_of, y_of = self.own_cells()
        strip, x_far = np.arange(LANES) // (LANES // 2), x_of % (LANES // 2 // self.half)
        right, left = bx + x_far, x_far - REACH
        cells = np.stack([x_of, y_of, np.where(strip == 0, right, left), np.where(strip == 0, left, right)])
        z_in = np.concatenate([np.arange(bz), np.arange(-REACH, 0), bz + np.arange(REACH)])
        distance = z_in[:, None] - np.arange(bz)[None, :]
        squared = np.where(np.abs(distance) <= REACH, distance * distance, FAR)
        return padded(cells, 8, LANES), squared.astype(np.float32)

    def coarse_tables(self):
        bx, _, _ = (size // 2 for size in self.brick)
        lane = np.arange(LANES)
        cell, count = lane // self.cy, self.cx * self.cy
        own = cell - 1
        extra = cell >= self.cx
        far_right = np.where(extra, 3 * bx - 1 + cell - self.cx, bx + own)
        far_left = np.where(extra, -2 * bx - 1 + cell - self.cx, own - bx)
        cells = [own, own, own + bx, own - bx, far_left, far_right, lane % self.cy - 1]
        cells += [np.where(lane < count, 0.0, FAR), np.where(cell < self.cx + 2, 0.0, FAR)]
        row = np.arange(self.out_cells)[:, None] + np.zeros((1, LANES))
        outs = np.stack([row // self.cy - 1, row % self.cy - 1, np.where(row < count, 0.0, FAR)])
        z_in, z_out = np.arange(self.window_rows) - GAUSSIAN_RIM, np.arange(LANES) - 1
        distance = z_in[:, None] - z_out[None, :]
        near = (np.abs(distance) <= REACH) & (np.arange(LANES) < self.out_z)[None, :]
        near = near & (np.arange(self.window_rows) < self.window)[:, None]
        squared = np.where(near, distance * distance, FAR)
        return padded(np.stack(cells), 16, LANES), outs.astype(np.float32), squared.astype(np.float32)

    def top_tables(self, kernels):
        four = [size // 16 for size in self.brick]
        lane = np.arange(2 * LANES)
        group, cell, partner = (lane % LANES) // self.group, lane % self.group, lane // LANES
        used = cell < self.top_x * self.top_y
        tables = []
        for axis in range(3):
            count, size = kernels[axis].shape[0], self.brick[axis] // 2
            whole = prolong_three_whole(count)
            outs = (self.cx, self.cy, self.out_z)[axis]
            spread, pick = [], []
            for place in range(self.counts[axis]):
                index = (place * size - 1 + np.arange(outs)) % (8 * count)
                spread.append(padded(whole[index], 16 if axis < 2 else LANES, 16))
                if axis == 0:
                    cells = (place ^ (group % 4)) * four[0] + cell // self.top_y - 1
                    valid = used
                elif axis == 1:
                    cells = (place ^ partner ^ (3 * (group // 4))) * four[1] + cell % self.top_y - 1
                    valid = used
                else:
                    row = np.arange(self.top_rows)
                    side, at = row // (self.top_rows // 2), row % (self.top_rows // 2)
                    cells = (place ^ side) * four[2] + at - 1
                    valid = at < self.top_z
                hot = (np.arange(count)[:, None] == (cells % count)[None, :]) & valid[None, :]
                hot = padded(hot, 16, cells.size)
                pick.append(hot if axis == 2 else hot.reshape(16, 2, LANES))
            tables += [np.stack(spread), np.stack(pick)]
        out = np.arange(self.out_cells)
        tables.append((out[:, None] // self.cy == np.arange(16)[None, :]).astype(np.float32))
        tables.append((out[:, None] % self.cy == np.arange(16)[None, :]).astype(np.float32))
        return tables

    def own_cells(self):
        lane = np.arange(LANES)
        return lane // self.half, lane % self.half


def fits(brick, counts, tops):
    bx, by, bz = brick
    return (
        counts == (4, 4, 2)
        and bx * (by // 2) == LANES
        and by % 16 == 0
        and bx % 16 == 0
        and bz == LANES
        and bx // 2 == REACH
        and by // 2 == REACH
        and (bx // 2 + 4) * (by // 2 + 2) <= LANES
        and (bx // 16 + 2) * (by // 16 + 2) <= 16
        and max(top.shape[0] for top in tops) <= 16
    )


def split(value):
    high = value.astype(BF16)
    return high, (value - high.astype(F32)).astype(BF16)


def dot(left, right):
    return jnp.dot(left, right, preferred_element_type=F32)


def dot_left(exact, value):
    high, low = split(value)
    return dot(exact, high) + dot(exact, low)


def dot_right(value, exact):
    high, low = split(value)
    return dot(high, exact) + dot(low, exact)


def dot_split(left, right):
    return dot(left[0], right[0]) + dot(left[1], right[0]) + dot(left[0], right[1])


def pick(flags_ref, axis, even, odd):
    return jnp.where(jnp.broadcast_to(flags_ref[axis : axis + 1], even.shape) < 0.5, even, odd)


def exact_tables(plan, ref):
    def read(name, rows, at=0):
        start = plan.starts[name] + at * rows
        return ref[start : start + rows].astype(BF16)

    return read


def lanes_of(rows):
    return lax.broadcasted_iota(jnp.int32, (rows, LANES), 1)


def halves(first, second):
    low = lanes_of(first.shape[0]) < LANES // 2
    return (
        jnp.where(low, first, pltpu.roll(second, LANES // 2, 1)),
        jnp.where(low, pltpu.roll(first, LANES // 2, 1), second),
    )


def start_kernel(plan, charges_ref, table_ref, own_ref, out_ref):
    _, _, bz = plan.brick
    rim, half = plan.rim, plan.half
    top, size = None, plan.top_rows // 2
    left = split(table_ref[:size])
    for part in range(2):
        cells = charges_ref[:, part * half : (part + 1) * half, :].reshape(LANES, bz).T
        own_ref[part] = cells
        out_ref[2 * rim * part : 2 * rim * part + rim] = cells[:rim]
        out_ref[2 * rim * part + rim : 2 * rim * (part + 1)] = cells[bz - rim :]
        right = split(table_ref[size + LANES * part : size + LANES * (part + 1)])
        rows = dot_split(split(dot_split(left, split(cells))), right)
        top = rows if top is None else top + rows
    out_ref[4 * rim :] = top


def setup_kernel(count, *refs):
    copies = [pltpu.make_async_copy(refs[at], refs[count + at], refs[2 * count].at[at]) for at in range(count)]
    for copy in copies:
        copy.start()
    for copy in copies:
        copy.wait()


def spread_kernel(plan, flags_ref, own_ref, sent_ref, got_ref, table_ref, fine_ref, out_ref, side_x_ref,
                  side_y_ref):
    _, _, bz = plan.brick
    rim, rows = plan.rim, plan.fine_rows
    table = exact_tables(plan, table_ref)
    coarse = None
    for part in range(2):
        cells = own_ref[part]
        far = got_ref[2 * rim * part : 2 * rim * (part + 1)]
        fine_ref[part, :bz] = cells
        fine_ref[part, bz : bz + REACH] = far[2 * rim - REACH :]
        fine_ref[part, bz + REACH :] = far[:REACH]
        summed = dot_left(table("rest_left", plan.window_rows), cells)
        summed = summed + dot_left(table("rest_far", plan.window_rows)[:, : 2 * rim], far)
        summed = dot_right(summed, table("rest_right", LANES, part))
        coarse = summed if coarse is None else coarse + summed
    low, high = halves(fine_ref[0], fine_ref[1])
    out_ref[:rows] = pick(flags_ref, 0, high, low)
    side_x_ref[...] = pick(flags_ref, 0, low, high)
    side_y_ref[:rows] = pick(flags_ref, 1, fine_ref[0], fine_ref[1])
    side_y_ref[rows:] = coarse
    out_ref[rows : rows + plan.window_rows] = coarse
    top = rows + plan.window_rows
    out_ref[top : top + plan.top_rows // 2] = sent_ref[4 * rim :]
    out_ref[top + plan.top_rows // 2 :] = got_ref[4 * rim :]


def half_of(plan, flags_ref, strip_ref):
    rows = plan.fine_rows
    low, high = halves(strip_ref[: rows // 2], strip_ref[rows // 2 : rows])
    return pick(flags_ref, 1, low, high)


def pass_kernel(plan, flags_ref, sent_ref, got_ref, out_ref, side_ref):
    rows = plan.fine_rows
    own = sent_ref[rows : rows + plan.window_rows]
    far = got_ref[rows : rows + plan.window_rows]
    lane = lanes_of(plan.window_rows)
    edge, count = 2 * plan.cy, plan.cx * plan.cy
    last = count - edge
    beyond = (lane >= count) & (lane < count + edge)
    left = far + jnp.where(lane < edge, pltpu.roll(own, LANES - last, 1), 0.0)
    left = left + jnp.where(beyond, pltpu.roll(own, count, 1), 0.0)
    right = far + jnp.where((lane >= last) & (lane < count), pltpu.roll(own, last, 1), 0.0)
    right = right + jnp.where(beyond, pltpu.roll(own, edge, 1), 0.0)
    out_ref[: plan.window_rows] = pick(flags_ref, 0, left, right)
    top = rows + plan.window_rows
    out_ref[plan.window_rows :] = sent_ref[top:] + pltpu.roll(got_ref[top:], plan.group, 1)
    side_ref[: rows // 2] = half_of(plan, flags_ref, got_ref)
    side_ref[rows // 2 :] = far


def stack_kernel(plan, flags_ref, fine_ref, sent_ref, first_ref, side_ref, second_ref, cells_ref, out_ref):
    rows, window = plan.fine_rows, plan.window_rows
    low, high = halves(first_ref[:rows], side_ref[...])
    for part, other in ((0, low), (1, high)):
        cells_ref[part, :rows] = fine_ref[part]
        cells_ref[part, rows:] = other
    out_ref[: rows // 2] = half_of(plan, flags_ref, side_ref)
    out_ref[rows // 2 : rows // 2 + window] = second_ref[:window]
    out_ref[rows // 2 + window :] = sent_ref[window:] + pltpu.roll(second_ref[window:], 2 * plan.group, 1)


def dot_turned(left, right):
    def product(first, second):
        return lax.dot_general(first, second, (((1,), (1,)), ((), ())), preferred_element_type=F32)

    return product(left[0], right[0]) + product(left[1], right[0]) + product(left[0], right[1])


def fine_weights_kernel(plan, terms, flags_ref, params_ref, table_ref, kf_ref, kf_low_ref, zf_ref, zf_low_ref):
    bx, by, _ = plan.brick
    cells_ref = table_ref.at[pl.ds(plan.starts["fine_cells"], 8)]
    dz_ref = table_ref.at[pl.ds(plan.starts["fine_dz"], plan.fine_rows)]
    half = plan.half
    own_x, own_y = cells_ref[0:1], cells_ref[1:2]
    far_x = pick(flags_ref, 0, cells_ref[2:3], cells_ref[3:4])
    x_out = lax.broadcasted_iota(jnp.int32, (bx, LANES), 0).astype(F32)
    y_out = lax.broadcasted_iota(jnp.int32, (half, LANES), 0).astype(F32)
    y_far = jnp.full((1, LANES), -half, F32)
    y_far = pick(flags_ref, 1, y_far, y_far + half + by)

    def decay(exponent, distance):
        return jnp.where(jnp.abs(distance) <= REACH, jnp.exp(-exponent * distance * distance), 0.0)

    for term in range(terms):
        exponent = params_ref[term : term + 1]
        scale = params_ref[terms + term : terms + term + 1]
        along_x = [decay(exponent, x_in - x_out)[:, None, :] for x_in in (own_x, far_x)]
        for group in range(4):
            y_in = own_y + (F32(group * half) if group < 2 else y_far)
            for part in range(2):
                along_y = decay(exponent, y_in - (y_out + part * half)) * scale
                for block in range(2):
                    high, low = split((along_x[block] * along_y[None]).reshape(bx * half, LANES))
                    rows, cols = pl.ds(part * LANES, LANES), pl.ds((2 * group + block) * LANES, LANES)
                    kf_ref[term, rows, cols] = high
                    kf_low_ref[term, rows, cols] = low
        zf_ref[term], zf_low_ref[term] = split(
            jnp.exp(-exponent * dz_ref[...]) * params_ref[2 * terms + term : 2 * terms + term + 1]
        )


def set_params(terms, exponents_ref, amplitudes_ref, tops, params_ref):
    offsets = lax.broadcasted_iota(jnp.int32, (1, LANES), 1).astype(F32) - REACH
    squared = jnp.where(offsets <= REACH, offsets * offsets, FAR)
    for level in range(2):
        for term in range(terms):
            at = slice(level, level + 1), slice(term, term + 1)
            exponent = exponents_ref[at]
            scale = 1.0 / jnp.sum(jnp.exp(-exponent * squared), axis=1, keepdims=True)
            row = 3 * terms * level + term
            for value in (exponent, scale * scale * amplitudes_ref[at], scale):
                params_ref[row : row + 1] = jnp.broadcast_to(value, (1, LANES))
                row = row + terms
    params_ref[6 * terms :] = jnp.zeros((3 * 16, LANES), F32)
    for axis, source in enumerate(tops):
        at, count = 6 * terms + 16 * axis, source.shape[0]
        params_ref[at : at + count, :count] = source[...]


def coarse_weights_kernel(plan, terms, place_ref, table_ref, exponents_ref, amplitudes_ref, top_x_ref, top_y_ref,
                          top_z_ref, params_ref, k1_ref, k1_low_ref, z1_ref, z1_low_ref, zc_ref, kc_ref):
    set_params(terms, exponents_ref, amplitudes_ref, (top_x_ref, top_y_ref, top_z_ref), params_ref)
    cells_ref = table_ref.at[pl.ds(plan.starts["coarse_cells"], 16)]
    at, count = plan.starts["out_cells"], plan.out_cells
    out_cells_ref = [table_ref[at + count * part : at + count * (part + 1)] for part in range(3)]
    dz_ref = table_ref.at[pl.ds(plan.starts["coarse_dz"], plan.window_rows)]
    zc_ref[...], kc_ref[...] = top_weights(plan, terms, place_ref, params_ref, table_ref)
    bx, by = plan.brick[0] // 2, plan.brick[1] // 2
    even_x, even_y = place_ref[0] % 2 == 0, place_ref[1] % 2 == 0
    base = 3 * terms

    def squared(distance, count):
        distance = distance - count * jnp.floor((distance + count // 2) * (1.0 / count))
        return jnp.where(jnp.abs(distance) <= REACH, distance * distance, FAR)

    x_out, y_out = out_cells_ref[0], out_cells_ref[1]
    squares_x = []
    for slot in range(3):
        x_in = jnp.where(even_x, cells_ref[2 * slot : 2 * slot + 1], cells_ref[2 * slot + 1 : 2 * slot + 2])
        used = cells_ref[7:8] if slot < 2 else cells_ref[8:9]
        squares_x.append(squared(x_in - x_out, bx * plan.counts[0]) + used)
    toward = jnp.where(even_y, F32(by), F32(-by))
    for group, offset in enumerate((F32(0), -toward, -toward, F32(2 * by))):
        square_y = squared(cells_ref[6:7] + offset - y_out, by * plan.counts[1]) + out_cells_ref[2]
        for slot in range(3):
            total = squares_x[slot] + square_y
            cols = pl.ds((3 * group + slot) * LANES, LANES)
            for term in range(terms):
                exponent = params_ref[base + term : base + term + 1]
                scale = params_ref[base + terms + term : base + terms + term + 1]
                high, low = split(jnp.exp(-exponent * total) * scale)
                rows = pl.ds(term * plan.out_cells, plan.out_cells)
                k1_ref[rows, cols] = high
                k1_low_ref[rows, cols] = low
    for term in range(terms):
        exponent = params_ref[base + term : base + term + 1]
        scale = params_ref[base + 2 * terms + term : base + 2 * terms + term + 1]
        z1_ref[term], z1_low_ref[term] = split(jnp.exp(-exponent * dz_ref[...]) * scale)


def top_weights(plan, terms, place_ref, params_ref, table_ref):
    def chain(*factors):
        value = factors[0]
        for factor in factors[1:]:
            value = dot_split(split(value), split(factor))
        return value

    def read(name, rows, at=0):
        return table_ref[pl.ds(pl.multiple_of(plan.starts[name] + at * rows, 8), rows)]

    size = 16

    def along(axis, spread, pick, place):
        top = params_ref[6 * terms + size * axis : 6 * terms + size * (axis + 1)]
        value = chain(read(spread, size, place)[:, :size], top)[:, :size]
        return chain(value, read(pick, size, place))

    along_x = along(0, "spread_x", "pick_x", place_ref[0])
    lift_x, lift_y = (read(name, plan.out_cells)[:, :size] for name in ("lift_x", "lift_y"))
    along_x = chain(lift_x, along_x)
    right = []
    for partner in range(2):
        place = place_ref[1] + partner * (1 - 2 * (place_ref[1] % 2))
        along_y = along(1, "spread_y", ("pick_y", "pick_pair")[partner], place)
        right.append(along_x * chain(lift_y, along_y))
    top = params_ref[6 * terms + 2 * size : 6 * terms + 3 * size]
    value = chain(read("spread_z", LANES, place_ref[2])[:, :size], top)[:, :size]
    left = chain(value, read("pick_z", size, place_ref[2])[:, : plan.top_rows])
    return left, jnp.concatenate(right, axis=1)


def sum_fine(terms, blocks, refs, at):
    cells, cols = split(blocks), pl.ds(at * LANES, blocks.shape[1])
    return [dot_turned((refs[0][term, :, cols], refs[1][term, :, cols]), cells) for term in range(terms)]


def sum_coarse(blocks, refs, at):
    cols = pl.ds(at * LANES, blocks.shape[1])
    return dot_turned((refs[0][:, cols], refs[1][:, cols]), split(blocks))


def fine_potential(fine, refs):
    total = None
    for term, value in enumerate(fine):
        value = dot_split(split(value), (refs[0][term], refs[1][term]))
        total = value if total is None else total + value
    return total


def coarse_potential(plan, terms, coarse, refs, top, kernel, table_ref):
    level_one = dot_turned(split(kernel), split(top))
    for term in range(terms):
        piece = split(coarse[term * plan.out_cells : (term + 1) * plan.out_cells])
        level_one = level_one + dot_split(piece, (refs[0][term], refs[1][term]))
    table = exact_tables(plan, table_ref)
    back = dot_right(level_one, table("back", LANES))
    return dot_left(table("back_right", 2 * LANES)[:, : plan.out_cells], back)


def near_kernel(plan, terms, flags_ref, cells_ref, own_ref, first_ref, second_ref, kf_ref, kf_low_ref, k1_ref,
                k1_low_ref, zf_ref, zf_low_ref, fine_ref, coarse_ref, give_fine_ref, give_coarse_ref):
    rows, window = plan.fine_rows, plan.window_rows
    kf, k1 = (kf_ref, kf_low_ref), (k1_ref, k1_low_ref)
    groups = [jnp.concatenate([cells_ref[part, :rows], cells_ref[part, rows:]], axis=1) for part in range(2)]
    near = [own_ref[rows : rows + window], first_ref[rows : rows + window], second_ref[:window]]
    near = jnp.concatenate(near, axis=1)
    other = [pick(flags_ref, 1, cells_ref[1, at : at + rows], cells_ref[0, at : at + rows]) for at in (0, rows)]
    other = jnp.concatenate(other, axis=1)
    give_fine_ref[...] = fine_potential(sum_fine(terms, other, kf, 6), (zf_ref, zf_low_ref))
    give_coarse_ref[...] = sum_coarse(near, k1, 6)
    for term, value in enumerate(sum_fine(terms, jnp.concatenate(groups, axis=1), kf, 0)):
        fine_ref[term] = value
    coarse_ref[...] = sum_coarse(near, k1, 0)


def top_charges(plan, sent_ref, got_ref, zc_ref):
    start = plan.fine_rows // 2 + plan.window_rows
    top = sent_ref[start:] + pltpu.roll(got_ref[start:], 4 * plan.group, 1)
    return dot_split(split(zc_ref[...]), split(top))


def arrived(plan, side_ref, strip_ref, got_ref):
    rows = plan.fine_rows
    pieces = [side_ref[rows:], strip_ref[rows // 2 :], got_ref[rows // 2 : rows // 2 + plan.window_rows]]
    return jnp.concatenate(pieces, axis=1)


def give_kernel(plan, terms, fine_ref, coarse_ref, side_ref, strip_ref, sent_ref, got_ref, k1_ref, k1_low_ref,
                z1_ref, z1_low_ref, zc_ref, kc_ref, table_ref, out_ref):
    coarse = coarse_ref[...] + sum_coarse(arrived(plan, side_ref, strip_ref, got_ref), (k1_ref, k1_low_ref), 9)
    top = top_charges(plan, sent_ref, got_ref, zc_ref)
    out_ref[...] = fine_ref[...] + coarse_potential(
        plan, terms, coarse, (z1_ref, z1_low_ref), top, kc_ref[:, LANES:], table_ref
    )


def keep_kernel(plan, terms, fine_ref, coarse_ref, side_ref, strip_ref, sent_ref, got_ref, kf_ref, kf_low_ref,
                k1_ref, k1_low_ref, zf_ref, zf_low_ref, z1_ref, z1_low_ref, zc_ref, kc_ref, table_ref, out_ref):
    rows = plan.fine_rows
    strips = jnp.concatenate(halves(strip_ref[: rows // 2], got_ref[: rows // 2]), axis=0)
    blocks = jnp.concatenate([side_ref[:rows], strips], axis=1)
    fine = sum_fine(terms, blocks, (kf_ref, kf_low_ref), 4)
    fine = [fine_ref[term] + value for term, value in enumerate(fine)]
    coarse = coarse_ref[...] + sum_coarse(arrived(plan, side_ref, strip_ref, got_ref), (k1_ref, k1_low_ref), 3)
    top = top_charges(plan, sent_ref, got_ref, zc_ref)
    out_ref[...] = fine_potential(fine, (zf_ref, zf_low_ref)) + coarse_potential(
        plan, terms, coarse, (z1_ref, z1_low_ref), top, kc_ref[:, :LANES], table_ref
    )


def add_kernel(plan, own_ref, got_ref, out_ref):
    half = plan.half
    for part in range(2):
        rows = pl.ds(part * LANES, LANES)
        cells = own_ref[rows] + got_ref[rows]
        out_ref[:, part * half : (part + 1) * half, :] = cells.reshape(plan.brick[0], half, plan.brick[2])


def call(body, shapes, *operands, scalars=0, after=(), last=False, plain=False, copies=0):
    specs = [pl.BlockSpec(memory_space=pltpu.SMEM)] * scalars
    specs += [pl.BlockSpec(memory_space=pltpu.VMEM)] * (len(operands) - scalars)
    if copies:
        specs = [pl.BlockSpec(memory_space=pl.ANY)] * len(operands)
    specs += [pl.BlockSpec(memory_space=pl.ANY)] * len(after)

    def keep(operand, space=pltpu.VMEM):
        return pltpu.with_memory_space_constraint(operand, space)

    if plain:
        operands = tuple(keep(operand, pltpu.HBM) for operand in operands)
    kept = list(operands) if plain else [keep(operand) for operand in operands[scalars:]]
    kept = kept[scalars:] if plain else kept
    kept += [keep(operand) for operand in after]
    kinds = [shape if isinstance(shape[-1], int) else shape[0] for shape in shapes]
    types = [F32 if isinstance(shape[-1], int) else shape[1] for shape in shapes]
    first = len(operands)

    def run(*refs):
        body(*refs[:first], *refs[first + len(after) :])

    return pl.pallas_call(
        run,
        out_shape=[
            jax.ShapeDtypeStruct(kind, kept_as) if last else pltpu.VMEM(kind, kept_as)
            for kind, kept_as in zip(kinds, types)
        ],
        in_specs=specs,
        out_specs=[pl.BlockSpec(memory_space=pltpu.VMEM)] * len(shapes),
        scratch_shapes=[pltpu.SemaphoreType.DMA((copies,))] if copies else (),
        compiler_params=pltpu.CompilerParams(vmem_limit_bytes=8 << 20),
    )(*(operands[:scalars] if plain else [keep(operand, pltpu.SMEM) for operand in operands[:scalars]]), *kept)


def pair(value, axis, bits):
    count = lax.axis_size(axis)
    return lax.ppermute(value, axis, [(i, i ^ bits) for i in range(count)])


def local_short(plan, charges, exponents, amplitudes, top_x, top_y, top_z):
    where = jnp.stack([lax.axis_index(axis) for axis in ("gx", "gy", "gz")]).astype(jnp.int32)
    flags = jnp.broadcast_to((where % 2).astype(F32)[:, None], (3, LANES))
    terms = exponents.shape[1]
    bx, by, bz = plan.brick
    rows, window = plan.fine_rows, plan.window_rows
    bind = functools.partial

    own, sent_z = call(
        bind(start_kernel, plan),
        [(2, bz, LANES), (4 * plan.rim + plan.top_rows // 2, LANES)],
        charges,
        jnp.asarray(np.concatenate([plan.top_left, *plan.top_right])),
        plain=True,
    )
    got_z = pair(sent_z, "gz", 1)
    held = (jnp.asarray(plan.constants((top_x, top_y, top_z))), exponents, amplitudes, top_x, top_y, top_z)
    table, *small = call(
        bind(setup_kernel, len(held)),
        [array.shape for array in held],
        *held,
        after=(sent_z,),
        plain=True,
        copies=len(held),
    )
    fine, sent_a, side_x, side_y = call(
        bind(spread_kernel, plan),
        [(2, rows, LANES), (plan.message, LANES), (rows, LANES), (rows + window, LANES)],
        flags,
        own,
        sent_z,
        got_z,
        table,
    )
    got_a = pair(sent_a, "gx", 1)
    got_x = pair(side_x, "gx", 3)
    got_y = pair(side_y, "gy", 3)
    sent_b, side_b = call(
        bind(pass_kernel, plan),
        [(plan.message - rows, LANES), (rows // 2 + window, LANES)],
        flags,
        sent_a,
        got_a,
    )
    got_b = pair(sent_b, "gx", 2)
    got_s = pair(side_b, "gy", 3)
    k1 = ((terms * plan.out_cells, 12 * LANES), BF16)
    params, *k1, z1, z1_low, zc, kc = call(
        bind(coarse_weights_kernel, plan, terms),
        [
            (6 * terms + 3 * 16, LANES),
            k1,
            k1,
            ((terms, window, LANES), BF16),
            ((terms, window, LANES), BF16),
            (LANES, plan.top_rows),
            (plan.out_cells, 2 * LANES),
        ],
        where,
        table,
        *small,
        scalars=1,
        after=(sent_b,),
    )
    size = rows // 2 + window + plan.top_rows
    cells, sent_c = call(
        bind(stack_kernel, plan),
        [(2, 2 * rows, LANES), (size, LANES)],
        flags,
        fine,
        sent_b,
        got_a,
        got_x,
        got_b,
        after=(z1, got_y, got_s),
    )
    got_c = pair(sent_c, "gy", 3)
    kf = ((terms, 2 * LANES, 8 * LANES), BF16)
    *kf, zf, zf_low = call(
        bind(fine_weights_kernel, plan, terms),
        [kf, kf, ((terms, rows, LANES), BF16), ((terms, rows, LANES), BF16)],
        flags,
        params,
        table,
        after=(sent_c,),
    )
    give = (2 * LANES, bz)
    fine_sum, coarse_sum, give_fine, give_coarse = call(
        bind(near_kernel, plan, terms),
        [(terms, 2 * LANES, rows), (terms * plan.out_cells, window), give, (terms * plan.out_cells, window)],
        flags,
        cells,
        sent_a,
        got_a,
        got_b,
        *kf,
        *k1,
        zf,
        zf_low,
        after=(sent_c,),
    )
    ends = (z1, z1_low, zc, kc, table)
    (sent_d,) = call(
        bind(give_kernel, plan, terms), [give], give_fine, give_coarse, got_y, got_s, sent_c, got_c, *k1, *ends
    )
    got_d = pair(sent_d, "gy", 1)
    (kept,) = call(
        bind(keep_kernel, plan, terms),
        [give],
        fine_sum,
        coarse_sum,
        got_y,
        got_s,
        sent_c,
        got_c,
        *kf,
        *k1,
        zf,
        zf_low,
        *ends,
        after=(sent_d,),
    )
    (out,) = call(bind(add_kernel, plan), [(bx, by, bz)], kept, got_d, last=True)
    return out


def local(*arguments):
    counts = tuple(lax.axis_size(axis) for axis in ("gx", "gy", "gz"))
    brick = arguments[0].shape
    if fits(brick, counts, arguments[3:]):
        return local_short(Plan(brick, counts), *arguments)
    return local_any(*arguments)


def solution(mesh):
    in_specs = (P("gx", "gy", "gz"), P(), P(), P(), P(), P())
    out_specs = P("gx", "gy", "gz")
    return jax.shard_map(local, mesh=mesh, in_specs=in_specs, out_specs=out_specs, check_vma=False)
```

```python
import functools

import jax
import jax.numpy as jnp
import numpy as np
from jax import lax
from jax.experimental import pallas as pl
from jax.experimental.pallas import tpu as pltpu
from jax.sharding import PartitionSpec as P


REACH = 8


HIGHEST = lax.Precision.HIGHEST


def with_halo(cells, sides, width):
    for axis, dim in sides:
        count = lax.axis_size(axis)
        head = lax.slice_in_dim(cells, 0, width, axis=dim)
        tail = lax.slice_in_dim(cells, cells.shape[dim] - width, cells.shape[dim], axis=dim)
        cells = jnp.concatenate(
            [
                lax.ppermute(tail, axis, [(i, (i + 1) % count) for i in range(count)]),
                cells,
                lax.ppermute(head, axis, [((i + 1) % count, i) for i in range(count)]),
            ],
            axis=dim,
        )
    return cells


def gauss_taps(exponents):
    offsets = jnp.arange(-REACH, REACH + 1).astype(jnp.float32)
    weights = jnp.exp(-exponents[..., None] * offsets * offsets)
    return weights / jnp.sum(weights, axis=-1, keepdims=True)


def spline(offsets):
    inner_weight = jnp.where((offsets == 1) | (offsets == 2), 0.75, 0.0)
    return jnp.where((offsets == 0) | (offsets == 3), 0.25, inner_weight).astype(jnp.float32)


def band_gauss(tap_table, length):
    rows = jnp.arange(length + 2 * REACH)[:, None]
    cols = jnp.arange(length)[None, :]
    offsets = rows - cols
    onehot = (offsets[:, :, None] == jnp.arange(2 * REACH + 1)[None, None, :]).astype(jnp.float32)
    return jnp.einsum("gk,pok->gpo", tap_table, onehot, precision=HIGHEST)


def band_restrict(length):
    rows = jnp.arange(length + 2)[:, None]
    cols = jnp.arange(length // 2)[None, :]
    return spline(rows - 2 * cols)


def band_prolong(length):
    rows = jnp.arange(length + 2)[:, None]
    cols = jnp.arange(2 * length)[None, :]
    return spline(cols - 2 * rows + 3)


def apply_three(field, band_x, band_y, band_z):
    field = jnp.einsum("xyz,zc->xyc", field, band_z, precision=HIGHEST)
    field = jnp.einsum("xyz,yb->xbz", field, band_y, precision=HIGHEST)
    return jnp.einsum("xyz,xa->ayz", field, band_x, precision=HIGHEST)


def rim_cells(field):
    return with_halo(field, (("gx", 0), ("gy", 1), ("gz", 2)), 1)


def restrict_local(padded):
    sizes = padded.shape
    return apply_three(
        padded,
        band_restrict(sizes[0] - 2),
        band_restrict(sizes[1] - 2),
        band_restrict(sizes[2] - 2),
    )


def prolong_local(field):
    sizes = field.shape
    return apply_three(
        rim_cells(field), band_prolong(sizes[0]), band_prolong(sizes[1]), band_prolong(sizes[2])
    )


def prolong_from_whole(whole_grid, brick):
    padded = jnp.pad(whole_grid, 1, mode="wrap")
    starts = (
        lax.axis_index("gx") * brick[0],
        lax.axis_index("gy") * brick[1],
        lax.axis_index("gz") * brick[2],
    )
    piece_cells = lax.dynamic_slice(padded, starts, (brick[0] + 2, brick[1] + 2, brick[2] + 2))
    return apply_three(
        piece_cells, band_prolong(brick[0]), band_prolong(brick[1]), band_prolong(brick[2])
    )


def assemble(gathered, brick):
    count_x = lax.axis_size("gx")
    count_y = lax.axis_size("gy")
    count_z = lax.axis_size("gz")
    blocks = gathered.reshape(count_x, count_y, count_z, brick[0], brick[1], brick[2])
    blocks = jnp.transpose(blocks, (0, 3, 1, 4, 2, 5))
    return blocks.reshape(count_x * brick[0], count_y * brick[1], count_z * brick[2])


def top_level(field, top_x, top_y, top_z):
    field = jnp.einsum("ia,abc->ibc", top_x, field, precision=HIGHEST)
    field = jnp.einsum("jb,ibc->ijc", top_y, field, precision=HIGHEST)
    return jnp.einsum("kc,ijc->ijk", top_z, field, precision=HIGHEST)


def gauss_and_restrict(field, tap_table, weights):
    size_x, size_y, size_z = field.shape
    band_z = band_gauss(tap_table, size_z)
    band_y = band_gauss(tap_table, size_y)
    band_x = band_gauss(tap_table, size_x) * weights[:, None, None]
    padded = with_halo(field, (("gx", 0), ("gy", 1), ("gz", 2)), REACH)
    along_z = jnp.einsum("xyp,gpo->xygo", padded, band_z, precision=HIGHEST)
    along_y = jnp.einsum("xpgz,gpw->xgwz", along_z, band_y, precision=HIGHEST)
    result = jnp.einsum("pgwz,gpv->vwz", along_y, band_x, precision=HIGHEST)
    inner_cells = padded[
        REACH - 1 : size_x + REACH + 1,
        REACH - 1 : size_y + REACH + 1,
        REACH - 1 : size_z + REACH + 1,
    ]
    coarse = restrict_local(inner_cells)
    return (result, coarse)


def local_any(charges, exponents, amplitudes, top_x, top_y, top_z):
    tap_table = gauss_taps(exponents)
    term_zero, level_one = gauss_and_restrict(charges, tap_table[0], amplitudes[0])
    term_one, level_two = gauss_and_restrict(level_one, tap_table[1], amplitudes[1])
    level_three = restrict_local(rim_cells(level_two))
    level_four = restrict_local(rim_cells(level_three))
    brick_four = level_four.shape
    gathered = lax.all_gather(level_four.reshape(1, -1), ("gx", "gy", "gz"), axis=0, tiled=True)
    phi_four = top_level(assemble(gathered, brick_four), top_x, top_y, top_z)
    phi_three = prolong_from_whole(phi_four, brick_four)
    phi_two = prolong_local(phi_three)
    phi_one = term_one + prolong_local(phi_two)
    return term_zero + prolong_local(phi_one)


F32 = jnp.float32
BF16 = jnp.bfloat16
LANES = 128
FAR = 1.0e9
GAUSSIAN_RIM = REACH + 1


def up8(count):
    return -(-count // 8) * 8


def restrict_weights(fine, coarse):
    offsets = np.asarray(fine)[None, :] - 2 * np.asarray(coarse)[:, None] + 1
    inner = np.where((offsets == 1) | (offsets == 2), 0.75, 0.0)
    return np.where((offsets == 0) | (offsets == 3), 0.25, inner).astype(np.float32)


def reach_four(length):
    total, cells = np.eye(length, dtype=np.float32), np.arange(length)
    for level in range(1, 5):
        coarse = np.arange(-1, length // 2**level + 1)
        total = restrict_weights(cells, coarse) @ total
        cells = coarse
    return total


def prolong_three_whole(count):
    total = np.eye(count, dtype=np.float32)
    for level in range(3):
        size = count * 2**level
        step = np.zeros((2 * size, size), np.float32)
        for cell in range(size):
            for offset, weight in ((-1, 0.25), (0, 0.75), (1, 0.75), (2, 0.25)):
                step[(2 * cell + offset) % (2 * size), cell] += weight
        total = step @ total
    return total


def padded(table, rows, cols):
    out = np.zeros((rows, cols), np.float32)
    out[: table.shape[0], : table.shape[1]] = table
    return out


class Plan:
    def __init__(self, brick, counts):
        self.brick, self.counts = brick, counts
        bx, by, bz = brick
        self.half = by // 2
        self.rim = up8(2 * GAUSSIAN_RIM + 1)
        self.fine_rows = bz + 2 * REACH
        self.cx, self.cy = bx // 2 + 2, by // 2 + 2
        self.window = bz // 2 + 2 * GAUSSIAN_RIM
        self.window_rows = up8(self.window)
        self.out_z = bz // 2 + 2
        self.top_rows = 2 * up8(bz // 16 + 2)
        self.top_z = bz // 16 + 2
        self.top_x, self.top_y = bx // 16 + 2, by // 16 + 2
        self.group = 16
        x_of, y_of = self.own_cells()
        rz = reach_four(bz)
        self.top_left = padded(rz, self.top_rows // 2, bz)
        rx, ry = reach_four(bx), reach_four(by)
        self.top_right, self.rest_right = [], []
        sx = restrict_weights(np.arange(bx), np.arange(-1, bx // 2 + 1))
        sy = restrict_weights(np.arange(by), np.arange(-1, by // 2 + 1))
        for part in range(2):
            y = y_of + part * self.half
            table = rx[:, x_of][:, None, :] * ry[:, y][None, :, :]
            self.top_right.append(padded(table.reshape(-1, LANES).T, LANES, LANES))
            table = sx[:, x_of][:, None, :] * sy[:, y][None, :, :]
            self.rest_right.append(padded(table.reshape(-1, LANES).T, LANES, LANES))
        z_in = np.concatenate([np.arange(bz), bz + np.arange(self.rim), np.arange(-self.rim, 0)])
        z_out = np.arange(-GAUSSIAN_RIM, bz // 2 + GAUSSIAN_RIM)
        self.rest_left = padded(restrict_weights(z_in, z_out), self.window_rows, z_in.size)
        spread = restrict_weights(np.arange(bz), np.arange(-1, bz // 2 + 1)).T
        self.back_left = padded(spread.T, LANES, bz)
        cols = []
        for part in range(2):
            y = y_of + part * self.half
            table = sx[:, x_of][:, None, :] * sy[:, y][None, :, :]
            cols.append(padded(table.reshape(-1, LANES), LANES, LANES))
        self.out_cells = -(-self.cx * self.cy // 16) * 16
        self.back_right = np.concatenate(cols, axis=1).T[:, : self.out_cells]
        self.message = self.fine_rows + self.window_rows + self.top_rows

    def constants(self, kernels):
        rest = self.rest_left
        fine_cells, fine_dz = self.fine_tables()
        coarse_cells, out_cells, coarse_dz = self.coarse_tables()
        spread_x, pick_x, spread_y, pick_y, spread_z, pick_z, lift_x, lift_y = self.top_tables(kernels)
        named = {
            "rest_left": rest[:, :LANES],
            "rest_far": rest[:, LANES:],
            "rest_right": np.concatenate(self.rest_right),
            "fine_cells": fine_cells,
            "fine_dz": fine_dz,
            "coarse_cells": coarse_cells,
            "out_cells": out_cells.reshape(-1, LANES),
            "coarse_dz": coarse_dz,
            "back": self.back_left,
            "back_right": self.back_right,
            "spread_x": spread_x.reshape(-1, 16),
            "pick_x": pick_x[:, :, 0].reshape(-1, LANES),
            "spread_y": spread_y.reshape(-1, 16),
            "pick_y": pick_y[:, :, 0].reshape(-1, LANES),
            "pick_pair": pick_y[:, :, 1].reshape(-1, LANES),
            "spread_z": spread_z.reshape(-1, 16),
            "pick_z": pick_z.reshape(-1, self.top_rows),
            "lift_x": lift_x,
            "lift_y": lift_y,
        }
        at, starts, pieces = 0, {}, []
        for name, table in named.items():
            rows = -(-table.shape[0] // 16) * 16
            starts[name] = at
            pieces.append(padded(table, rows, LANES))
            at += rows
        self.starts = starts
        return np.concatenate(pieces)

    def fine_tables(self):
        bx, _, bz = self.brick
        x_of, y_of = self.own_cells()
        strip, x_far = np.arange(LANES) // (LANES // 2), x_of % (LANES // 2 // self.half)
        right, left = bx + x_far, x_far - REACH
        cells = np.stack([x_of, y_of, np.where(strip == 0, right, left), np.where(strip == 0, left, right)])
        z_in = np.concatenate([np.arange(bz), np.arange(-REACH, 0), bz + np.arange(REACH)])
        distance = z_in[:, None] - np.arange(bz)[None, :]
        squared = np.where(np.abs(distance) <= REACH, distance * distance, FAR)
        return padded(cells, 8, LANES), squared.astype(np.float32)

    def coarse_tables(self):
        bx, _, _ = (size // 2 for size in self.brick)
        lane = np.arange(LANES)
        cell, count = lane // self.cy, self.cx * self.cy
        own = cell - 1
        extra = cell >= self.cx
        far_right = np.where(extra, 3 * bx - 1 + cell - self.cx, bx + own)
        far_left = np.where(extra, -2 * bx - 1 + cell - self.cx, own - bx)
        cells = [own, own, own + bx, own - bx, far_left, far_right, lane % self.cy - 1]
        cells += [np.where(lane < count, 0.0, FAR), np.where(cell < self.cx + 2, 0.0, FAR)]
        row = np.arange(self.out_cells)[:, None] + np.zeros((1, LANES))
        outs = np.stack([row // self.cy - 1, row % self.cy - 1, np.where(row < count, 0.0, FAR)])
        z_in, z_out = np.arange(self.window_rows) - GAUSSIAN_RIM, np.arange(LANES) - 1
        distance = z_in[:, None] - z_out[None, :]
        near = (np.abs(distance) <= REACH) & (np.arange(LANES) < self.out_z)[None, :]
        near = near & (np.arange(self.window_rows) < self.window)[:, None]
        squared = np.where(near, distance * distance, FAR)
        return padded(np.stack(cells), 16, LANES), outs.astype(np.float32), squared.astype(np.float32)

    def top_tables(self, kernels):
        four = [size // 16 for size in self.brick]
        lane = np.arange(2 * LANES)
        group, cell, partner = (lane % LANES) // self.group, lane % self.group, lane // LANES
        used = cell < self.top_x * self.top_y
        tables = []
        for axis in range(3):
            count, size = kernels[axis].shape[0], self.brick[axis] // 2
            whole = prolong_three_whole(count)
            outs = (self.cx, self.cy, self.out_z)[axis]
            spread, pick = [], []
            for place in range(self.counts[axis]):
                index = (place * size - 1 + np.arange(outs)) % (8 * count)
                spread.append(padded(whole[index], 16 if axis < 2 else LANES, 16))
                if axis == 0:
                    cells = (place ^ (group % 4)) * four[0] + cell // self.top_y - 1
                    valid = used
                elif axis == 1:
                    cells = (place ^ partner ^ (3 * (group // 4))) * four[1] + cell % self.top_y - 1
                    valid = used
                else:
                    row = np.arange(self.top_rows)
                    side, at = row // (self.top_rows // 2), row % (self.top_rows // 2)
                    cells = (place ^ side) * four[2] + at - 1
                    valid = at < self.top_z
                hot = (np.arange(count)[:, None] == (cells % count)[None, :]) & valid[None, :]
                hot = padded(hot, 16, cells.size)
                pick.append(hot if axis == 2 else hot.reshape(16, 2, LANES))
            tables += [np.stack(spread), np.stack(pick)]
        out = np.arange(self.out_cells)
        tables.append((out[:, None] // self.cy == np.arange(16)[None, :]).astype(np.float32))
        tables.append((out[:, None] % self.cy == np.arange(16)[None, :]).astype(np.float32))
        return tables

    def own_cells(self):
        lane = np.arange(LANES)
        return lane // self.half, lane % self.half


def fits(brick, counts, tops):
    bx, by, bz = brick
    return (
        counts == (4, 4, 2)
        and bx * (by // 2) == LANES
        and by % 16 == 0
        and bx % 16 == 0
        and bz == LANES
        and bx // 2 == REACH
        and by // 2 == REACH
        and (bx // 2 + 4) * (by // 2 + 2) <= LANES
        and (bx // 16 + 2) * (by // 16 + 2) <= 16
        and max(top.shape[0] for top in tops) <= 16
    )


def split(value):
    high = value.astype(BF16)
    return high, (value - high.astype(F32)).astype(BF16)


def dot(left, right):
    return jnp.dot(left, right, preferred_element_type=F32)


def dot_left(exact, value):
    high, low = split(value)
    return dot(exact, high) + dot(exact, low)


def dot_right(value, exact):
    high, low = split(value)
    return dot(high, exact) + dot(low, exact)


def dot_split(left, right):
    return dot(left[0], right[0]) + dot(left[1], right[0]) + dot(left[0], right[1])


def pick(flags_ref, axis, even, odd):
    return jnp.where(jnp.broadcast_to(flags_ref[axis : axis + 1], even.shape) < 0.5, even, odd)


def exact_tables(plan, ref):
    def read(name, rows, at=0):
        start = plan.starts[name] + at * rows
        return ref[start : start + rows].astype(BF16)

    return read


def lanes_of(rows):
    return lax.broadcasted_iota(jnp.int32, (rows, LANES), 1)


def halves(first, second):
    low = lanes_of(first.shape[0]) < LANES // 2
    return (
        jnp.where(low, first, pltpu.roll(second, LANES // 2, 1)),
        jnp.where(low, pltpu.roll(first, LANES // 2, 1), second),
    )


def start_kernel(plan, charges_ref, table_ref, own_ref, out_ref):
    _, _, bz = plan.brick
    rim, half = plan.rim, plan.half
    top, size = None, plan.top_rows // 2
    left = split(table_ref[:size])
    for part in range(2):
        cells = charges_ref[:, part * half : (part + 1) * half, :].reshape(LANES, bz).T
        own_ref[part] = cells
        out_ref[2 * rim * part : 2 * rim * part + rim] = cells[:rim]
        out_ref[2 * rim * part + rim : 2 * rim * (part + 1)] = cells[bz - rim :]
        right = split(table_ref[size + LANES * part : size + LANES * (part + 1)])
        rows = dot_split(split(dot_split(left, split(cells))), right)
        top = rows if top is None else top + rows
    out_ref[4 * rim :] = top


def setup_kernel(count, *refs):
    copies = [pltpu.make_async_copy(refs[at], refs[count + at], refs[2 * count].at[at]) for at in range(count)]
    for copy in copies:
        copy.start()
    for copy in copies:
        copy.wait()


def spread_kernel(plan, flags_ref, own_ref, sent_ref, got_ref, table_ref, fine_ref, out_ref, side_x_ref,
                  side_y_ref):
    _, _, bz = plan.brick
    rim, rows = plan.rim, plan.fine_rows
    table = exact_tables(plan, table_ref)
    coarse = None
    for part in range(2):
        cells = own_ref[part]
        far = got_ref[2 * rim * part : 2 * rim * (part + 1)]
        fine_ref[part, :bz] = cells
        fine_ref[part, bz : bz + REACH] = far[2 * rim - REACH :]
        fine_ref[part, bz + REACH :] = far[:REACH]
        summed = dot_left(table("rest_left", plan.window_rows), cells)
        summed = summed + dot_left(table("rest_far", plan.window_rows)[:, : 2 * rim], far)
        summed = dot_right(summed, table("rest_right", LANES, part))
        coarse = summed if coarse is None else coarse + summed
    low, high = halves(fine_ref[0], fine_ref[1])
    out_ref[:rows] = pick(flags_ref, 0, high, low)
    side_x_ref[...] = pick(flags_ref, 0, low, high)
    side_y_ref[:rows] = pick(flags_ref, 1, fine_ref[0], fine_ref[1])
    side_y_ref[rows:] = coarse
    out_ref[rows : rows + plan.window_rows] = coarse
    top = rows + plan.window_rows
    out_ref[top : top + plan.top_rows // 2] = sent_ref[4 * rim :]
    out_ref[top + plan.top_rows // 2 :] = got_ref[4 * rim :]


def half_of(plan, flags_ref, strip_ref):
    rows = plan.fine_rows
    low, high = halves(strip_ref[: rows // 2], strip_ref[rows // 2 : rows])
    return pick(flags_ref, 1, low, high)


def pass_kernel(plan, flags_ref, sent_ref, got_ref, out_ref, side_ref):
    rows = plan.fine_rows
    own = sent_ref[rows : rows + plan.window_rows]
    far = got_ref[rows : rows + plan.window_rows]
    lane = lanes_of(plan.window_rows)
    edge, count = 2 * plan.cy, plan.cx * plan.cy
    last = count - edge
    beyond = (lane >= count) & (lane < count + edge)
    left = far + jnp.where(lane < edge, pltpu.roll(own, LANES - last, 1), 0.0)
    left = left + jnp.where(beyond, pltpu.roll(own, count, 1), 0.0)
    right = far + jnp.where((lane >= last) & (lane < count), pltpu.roll(own, last, 1), 0.0)
    right = right + jnp.where(beyond, pltpu.roll(own, edge, 1), 0.0)
    out_ref[: plan.window_rows] = pick(flags_ref, 0, left, right)
    top = rows + plan.window_rows
    out_ref[plan.window_rows :] = sent_ref[top:] + pltpu.roll(got_ref[top:], plan.group, 1)
    side_ref[: rows // 2] = half_of(plan, flags_ref, got_ref)
    side_ref[rows // 2 :] = far


def stack_kernel(plan, flags_ref, fine_ref, sent_ref, first_ref, side_ref, second_ref, cells_ref, out_ref):
    rows, window = plan.fine_rows, plan.window_rows
    low, high = halves(first_ref[:rows], side_ref[...])
    for part, other in ((0, low), (1, high)):
        cells_ref[part, :rows] = fine_ref[part]
        cells_ref[part, rows:] = other
    out_ref[: rows // 2] = half_of(plan, flags_ref, side_ref)
    out_ref[rows // 2 : rows // 2 + window] = second_ref[:window]
    out_ref[rows // 2 + window :] = sent_ref[window:] + pltpu.roll(second_ref[window:], 2 * plan.group, 1)


def turned(left, right):
    return lax.dot_general(left, right, (((1,), (1,)), ((), ())), preferred_element_type=F32)


def dot_turned(left, right):
    return turned(left[0], right[0]) + turned(left[1], right[0]) + turned(left[0], right[1])


def fine_weights_kernel(plan, terms, flags_ref, params_ref, table_ref, kf_ref, kf_low_ref, zf_ref, zf_low_ref):
    bx, by, _ = plan.brick
    cells_ref = table_ref.at[pl.ds(plan.starts["fine_cells"], 8)]
    dz_ref = table_ref.at[pl.ds(plan.starts["fine_dz"], plan.fine_rows)]
    half = plan.half
    own_x, own_y = cells_ref[0:1], cells_ref[1:2]
    far_x = pick(flags_ref, 0, cells_ref[2:3], cells_ref[3:4])
    x_out = lax.broadcasted_iota(jnp.int32, (bx, LANES), 0).astype(F32)
    y_out = lax.broadcasted_iota(jnp.int32, (half, LANES), 0).astype(F32)
    y_far = jnp.full((1, LANES), -half, F32)
    y_far = pick(flags_ref, 1, y_far, y_far + half + by)

    def decay(exponent, distance):
        return jnp.where(jnp.abs(distance) <= REACH, jnp.exp(-exponent * distance * distance), 0.0)

    for term in range(terms):
        exponent = params_ref[term : term + 1]
        scale = params_ref[terms + term : terms + term + 1]
        along_x = [decay(exponent, x_in - x_out)[:, None, :] for x_in in (own_x, far_x)]
        for group in range(3):
            y_in = own_y + (F32(group * half) if group < 2 else y_far)
            for part in range(2):
                along_y = decay(exponent, y_in - (y_out + part * half)) * scale
                for block in range(2):
                    high, low = split((along_x[block] * along_y[None]).reshape(bx * half, LANES))
                    rows, cols = pl.ds(part * LANES, LANES), pl.ds((2 * group + block) * LANES, LANES)
                    kf_ref[term, rows, cols] = high
                    kf_low_ref[term, rows, cols] = low
        zf_ref[term], zf_low_ref[term] = split(
            jnp.exp(-exponent * dz_ref[...]) * params_ref[2 * terms + term : 2 * terms + term + 1]
        )


def set_params(terms, exponents_ref, amplitudes_ref, tops, params_ref):
    offsets = lax.broadcasted_iota(jnp.int32, (1, LANES), 1).astype(F32) - REACH
    squared = jnp.where(offsets <= REACH, offsets * offsets, FAR)
    for level in range(2):
        for term in range(terms):
            at = slice(level, level + 1), slice(term, term + 1)
            exponent = exponents_ref[at]
            scale = 1.0 / jnp.sum(jnp.exp(-exponent * squared), axis=1, keepdims=True)
            row = 3 * terms * level + term
            for value in (exponent, scale * scale * amplitudes_ref[at], scale):
                params_ref[row : row + 1] = jnp.broadcast_to(value, (1, LANES))
                row = row + terms
    params_ref[6 * terms :] = jnp.zeros((3 * 16, LANES), F32)
    for axis, source in enumerate(tops):
        at, count = 6 * terms + 16 * axis, source.shape[0]
        params_ref[at : at + count, :count] = source[...]


def coarse_weights_kernel(plan, terms, place_ref, table_ref, exponents_ref, amplitudes_ref, top_x_ref, top_y_ref,
                          top_z_ref, params_ref, k1_ref, k1_low_ref, z1_ref, z1_low_ref, zc_ref, kc_ref):
    set_params(terms, exponents_ref, amplitudes_ref, (top_x_ref, top_y_ref, top_z_ref), params_ref)
    cells_ref = table_ref.at[pl.ds(plan.starts["coarse_cells"], 16)]
    at, count = plan.starts["out_cells"], plan.out_cells
    out_cells_ref = [table_ref[at + count * part : at + count * (part + 1)] for part in range(3)]
    dz_ref = table_ref.at[pl.ds(plan.starts["coarse_dz"], plan.window_rows)]
    zc_ref[...], kc_ref[...] = top_weights(plan, terms, place_ref, params_ref, table_ref)
    bx, by = plan.brick[0] // 2, plan.brick[1] // 2
    even_x, even_y = place_ref[0] % 2 == 0, place_ref[1] % 2 == 0
    base = 3 * terms

    def squared(distance, count):
        distance = distance - count * jnp.floor((distance + count // 2) * (1.0 / count))
        return jnp.where(jnp.abs(distance) <= REACH, distance * distance, FAR)

    x_out, y_out = out_cells_ref[0], out_cells_ref[1]
    squares_x = []
    for slot in range(3):
        x_in = jnp.where(even_x, cells_ref[2 * slot : 2 * slot + 1], cells_ref[2 * slot + 1 : 2 * slot + 2])
        used = cells_ref[7:8] if slot < 2 else cells_ref[8:9]
        squares_x.append(squared(x_in - x_out, bx * plan.counts[0]) + used)
    toward = jnp.where(even_y, F32(by), F32(-by))
    for group, offset in enumerate((F32(0), -toward, F32(2 * by))):
        square_y = squared(cells_ref[6:7] + offset - y_out, by * plan.counts[1]) + out_cells_ref[2]
        for slot in range(3):
            total = squares_x[slot] + square_y
            cols = pl.ds((3 * group + slot) * LANES, LANES)
            for term in range(terms):
                exponent = params_ref[base + term : base + term + 1]
                scale = params_ref[base + terms + term : base + terms + term + 1]
                high, low = split(jnp.exp(-exponent * total) * scale)
                rows = pl.ds(term * plan.out_cells, plan.out_cells)
                k1_ref[rows, cols] = high
                k1_low_ref[rows, cols] = low
    for term in range(terms):
        exponent = params_ref[base + term : base + term + 1]
        scale = params_ref[base + 2 * terms + term : base + 2 * terms + term + 1]
        z1_ref[term], z1_low_ref[term] = split(jnp.exp(-exponent * dz_ref[...]) * scale)


def top_weights(plan, terms, place_ref, params_ref, table_ref):
    def chain(*factors):
        value = factors[0]
        for factor in factors[1:]:
            value = dot_split(split(value), split(factor))
        return value

    def read(name, rows, at=0):
        return table_ref[pl.ds(pl.multiple_of(plan.starts[name] + at * rows, 8), rows)]

    size = 16

    def along(axis, spread, pick, place):
        top = params_ref[6 * terms + size * axis : 6 * terms + size * (axis + 1)]
        value = chain(read(spread, size, place)[:, :size], top)[:, :size]
        return chain(value, read(pick, size, place))

    along_x = along(0, "spread_x", "pick_x", place_ref[0])
    lift_x, lift_y = (read(name, plan.out_cells)[:, :size] for name in ("lift_x", "lift_y"))
    along_x = chain(lift_x, along_x)
    right = []
    for partner in range(2):
        place = place_ref[1] + partner * (1 - 2 * (place_ref[1] % 2))
        along_y = along(1, "spread_y", ("pick_y", "pick_pair")[partner], place)
        right.append(along_x * chain(lift_y, along_y))
    top = params_ref[6 * terms + 2 * size : 6 * terms + 3 * size]
    value = chain(read("spread_z", LANES, place_ref[2])[:, :size], top)[:, :size]
    left = chain(value, read("pick_z", size, place_ref[2])[:, : plan.top_rows])
    return left, jnp.concatenate(right, axis=1)


def sum_fine(terms, blocks, refs, at):
    cells, cols = split(blocks), pl.ds(at * LANES, blocks.shape[1])
    return [dot_turned((refs[0][term, :, cols], refs[1][term, :, cols]), cells) for term in range(terms)]


def sum_coarse(blocks, refs, at):
    cols, count = pl.ds(at * LANES, blocks.shape[1]), blocks.shape[0]
    high = blocks.astype(BF16)
    exact = high.astype(F32)
    gap = jnp.zeros((LANES - count, blocks.shape[1]), F32)
    both = jnp.concatenate([exact, gap, blocks - exact], axis=0).astype(BF16)
    sums = turned(refs[0][:, cols], both)
    return sums[:, :count] + sums[:, LANES : LANES + count] + turned(refs[1][:, cols], high)


def fine_potential(fine, refs):
    total = None
    for term, value in enumerate(fine):
        value = dot_split(split(value), (refs[0][term], refs[1][term]))
        total = value if total is None else total + value
    return total


def coarse_potential(plan, terms, coarse, refs, top, kernel, table_ref):
    level_one = dot_turned(split(kernel), split(top))
    for term in range(terms):
        piece = split(coarse[term * plan.out_cells : (term + 1) * plan.out_cells])
        level_one = level_one + dot_split(piece, (refs[0][term], refs[1][term]))
    table = exact_tables(plan, table_ref)
    back = dot_right(level_one, table("back", LANES))
    return dot_left(table("back_right", 2 * LANES)[:, : plan.out_cells], back)


def near_kernel(plan, terms, flags_ref, cells_ref, own_ref, first_ref, second_ref, kf_ref, kf_low_ref, k1_ref,
                k1_low_ref, zf_ref, zf_low_ref, fine_ref, coarse_ref, give_fine_ref, give_coarse_ref):
    rows, window = plan.fine_rows, plan.window_rows
    kf, k1 = (kf_ref, kf_low_ref), (k1_ref, k1_low_ref)
    groups = [jnp.concatenate([cells_ref[part, :rows], cells_ref[part, rows:]], axis=1) for part in range(2)]
    near = [own_ref[rows : rows + window], first_ref[rows : rows + window], second_ref[:window]]
    near = jnp.concatenate(near, axis=1)
    other = [pick(flags_ref, 1, cells_ref[1, at : at + rows], cells_ref[0, at : at + rows]) for at in (0, rows)]
    other = jnp.concatenate(other, axis=1)
    give_fine_ref[...] = fine_potential(sum_fine(terms, other, kf, 4), (zf_ref, zf_low_ref))
    give_coarse_ref[...] = sum_coarse(near, k1, 3)
    for term, value in enumerate(sum_fine(terms, jnp.concatenate(groups, axis=1), kf, 0)):
        fine_ref[term] = value
    coarse_ref[...] = sum_coarse(near, k1, 0)


def top_charges(plan, sent_ref, got_ref, zc_ref):
    start = plan.fine_rows // 2 + plan.window_rows
    top = sent_ref[start:] + pltpu.roll(got_ref[start:], 4 * plan.group, 1)
    return dot_split(split(zc_ref[...]), split(top))


def arrived(plan, side_ref, strip_ref, got_ref):
    rows = plan.fine_rows
    pieces = [side_ref[rows:], strip_ref[rows // 2 :], got_ref[rows // 2 : rows // 2 + plan.window_rows]]
    return jnp.concatenate(pieces, axis=1)


def give_kernel(plan, terms, fine_ref, coarse_ref, side_ref, strip_ref, sent_ref, got_ref, k1_ref, k1_low_ref,
                z1_ref, z1_low_ref, zc_ref, kc_ref, table_ref, out_ref):
    coarse = coarse_ref[...] + sum_coarse(arrived(plan, side_ref, strip_ref, got_ref), (k1_ref, k1_low_ref), 6)
    top = top_charges(plan, sent_ref, got_ref, zc_ref)
    out_ref[...] = fine_ref[...] + coarse_potential(
        plan, terms, coarse, (z1_ref, z1_low_ref), top, kc_ref[:, LANES:], table_ref
    )


def keep_kernel(plan, terms, fine_ref, coarse_ref, side_ref, strip_ref, sent_ref, got_ref, kf_ref, kf_low_ref,
                k1_ref, k1_low_ref, zf_ref, zf_low_ref, z1_ref, z1_low_ref, zc_ref, kc_ref, table_ref, out_ref):
    rows = plan.fine_rows
    strips = jnp.concatenate(halves(strip_ref[: rows // 2], got_ref[: rows // 2]), axis=0)
    blocks = jnp.concatenate([side_ref[:rows], strips], axis=1)
    fine = sum_fine(terms, blocks, (kf_ref, kf_low_ref), 4)
    fine = [fine_ref[term] + value for term, value in enumerate(fine)]
    coarse = coarse_ref[...] + sum_coarse(arrived(plan, side_ref, strip_ref, got_ref), (k1_ref, k1_low_ref), 3)
    top = top_charges(plan, sent_ref, got_ref, zc_ref)
    out_ref[...] = fine_potential(fine, (zf_ref, zf_low_ref)) + coarse_potential(
        plan, terms, coarse, (z1_ref, z1_low_ref), top, kc_ref[:, :LANES], table_ref
    )


def add_kernel(plan, own_ref, got_ref, out_ref):
    half = plan.half
    for part in range(2):
        rows = pl.ds(part * LANES, LANES)
        cells = own_ref[rows] + got_ref[rows]
        out_ref[:, part * half : (part + 1) * half, :] = cells.reshape(plan.brick[0], half, plan.brick[2])


def call(body, shapes, *operands, scalars=0, after=(), last=False, plain=False, copies=0):
    specs = [pl.BlockSpec(memory_space=pltpu.SMEM)] * scalars
    specs += [pl.BlockSpec(memory_space=pltpu.VMEM)] * (len(operands) - scalars)
    if copies:
        specs = [pl.BlockSpec(memory_space=pl.ANY)] * len(operands)
    specs += [pl.BlockSpec(memory_space=pl.ANY)] * len(after)

    def keep(operand, space=pltpu.VMEM):
        return pltpu.with_memory_space_constraint(operand, space)

    if plain:
        operands = tuple(keep(operand, pltpu.HBM) for operand in operands)
    kept = list(operands) if plain else [keep(operand) for operand in operands[scalars:]]
    kept = kept[scalars:] if plain else kept
    kept += [keep(operand) for operand in after]
    kinds = [shape if isinstance(shape[-1], int) else shape[0] for shape in shapes]
    types = [F32 if isinstance(shape[-1], int) else shape[1] for shape in shapes]
    first = len(operands)

    def run(*refs):
        body(*refs[:first], *refs[first + len(after) :])

    return pl.pallas_call(
        run,
        out_shape=[
            jax.ShapeDtypeStruct(kind, kept_as) if last else pltpu.VMEM(kind, kept_as)
            for kind, kept_as in zip(kinds, types)
        ],
        in_specs=specs,
        out_specs=[pl.BlockSpec(memory_space=pltpu.VMEM)] * len(shapes),
        scratch_shapes=[pltpu.SemaphoreType.DMA((copies,))] if copies else (),
        compiler_params=pltpu.CompilerParams(vmem_limit_bytes=8 << 20),
    )(*(operands[:scalars] if plain else [keep(operand, pltpu.SMEM) for operand in operands[:scalars]]), *kept)


def pair(value, axis, bits):
    count = lax.axis_size(axis)
    return lax.ppermute(value, axis, [(i, i ^ bits) for i in range(count)])


def local_short(plan, charges, exponents, amplitudes, top_x, top_y, top_z):
    where = jnp.stack([lax.axis_index(axis) for axis in ("gx", "gy", "gz")]).astype(jnp.int32)
    flags = jnp.broadcast_to((where % 2).astype(F32)[:, None], (3, LANES))
    terms = exponents.shape[1]
    bx, by, bz = plan.brick
    rows, window = plan.fine_rows, plan.window_rows
    bind = functools.partial

    own, sent_z = call(
        bind(start_kernel, plan),
        [(2, bz, LANES), (4 * plan.rim + plan.top_rows // 2, LANES)],
        charges,
        jnp.asarray(np.concatenate([plan.top_left, *plan.top_right])),
        plain=True,
    )
    got_z = pair(sent_z, "gz", 1)
    held = (jnp.asarray(plan.constants((top_x, top_y, top_z))), exponents, amplitudes, top_x, top_y, top_z)
    table, *small = call(
        bind(setup_kernel, len(held)),
        [array.shape for array in held],
        *held,
        after=(sent_z,),
        plain=True,
        copies=len(held),
    )
    fine, sent_a, side_x, side_y = call(
        bind(spread_kernel, plan),
        [(2, rows, LANES), (plan.message, LANES), (rows, LANES), (rows + window, LANES)],
        flags,
        own,
        sent_z,
        got_z,
        table,
    )
    got_a = pair(sent_a, "gx", 1)
    got_x = pair(side_x, "gx", 3)
    got_y = pair(side_y, "gy", 3)
    sent_b, side_b = call(
        bind(pass_kernel, plan),
        [(plan.message - rows, LANES), (rows // 2 + window, LANES)],
        flags,
        sent_a,
        got_a,
    )
    got_b = pair(sent_b, "gx", 2)
    got_s = pair(side_b, "gy", 3)
    k1 = ((terms * plan.out_cells, 9 * LANES), BF16)
    params, *k1, z1, z1_low, zc, kc = call(
        bind(coarse_weights_kernel, plan, terms),
        [
            (6 * terms + 3 * 16, LANES),
            k1,
            k1,
            ((terms, window, LANES), BF16),
            ((terms, window, LANES), BF16),
            (LANES, plan.top_rows),
            (plan.out_cells, 2 * LANES),
        ],
        where,
        table,
        *small,
        scalars=1,
        after=(sent_b,),
    )
    size = rows // 2 + window + plan.top_rows
    cells, sent_c = call(
        bind(stack_kernel, plan),
        [(2, 2 * rows, LANES), (size, LANES)],
        flags,
        fine,
        sent_b,
        got_a,
        got_x,
        got_b,
        after=(z1, got_y, got_s),
    )
    got_c = pair(sent_c, "gy", 3)
    kf = ((terms, 2 * LANES, 6 * LANES), BF16)
    *kf, zf, zf_low = call(
        bind(fine_weights_kernel, plan, terms),
        [kf, kf, ((terms, rows, LANES), BF16), ((terms, rows, LANES), BF16)],
        flags,
        params,
        table,
        after=(sent_c,),
    )
    give = (2 * LANES, bz)
    fine_sum, coarse_sum, give_fine, give_coarse = call(
        bind(near_kernel, plan, terms),
        [(terms, 2 * LANES, rows), (terms * plan.out_cells, window), give, (terms * plan.out_cells, window)],
        flags,
        cells,
        sent_a,
        got_a,
        got_b,
        *kf,
        *k1,
        zf,
        zf_low,
        after=(sent_c,),
    )
    ends = (z1, z1_low, zc, kc, table)
    (sent_d,) = call(
        bind(give_kernel, plan, terms), [give], give_fine, give_coarse, got_y, got_s, sent_c, got_c, *k1, *ends
    )
    got_d = pair(sent_d, "gy", 1)
    (kept,) = call(
        bind(keep_kernel, plan, terms),
        [give],
        fine_sum,
        coarse_sum,
        got_y,
        got_s,
        sent_c,
        got_c,
        *kf,
        *k1,
        zf,
        zf_low,
        *ends,
        after=(sent_d,),
    )
    (out,) = call(bind(add_kernel, plan), [(bx, by, bz)], kept, got_d, last=True)
    return out


def local(*arguments):
    counts = tuple(lax.axis_size(axis) for axis in ("gx", "gy", "gz"))
    brick = arguments[0].shape
    if fits(brick, counts, arguments[3:]):
        return local_short(Plan(brick, counts), *arguments)
    return local_any(*arguments)


def solution(mesh):
    in_specs = (P("gx", "gy", "gz"), P(), P(), P(), P(), P())
    out_specs = P("gx", "gy", "gz")
    return jax.shard_map(local, mesh=mesh, in_specs=in_specs, out_specs=out_specs, check_vma=False)
```

```python
import functools

import jax
import jax.numpy as jnp
import numpy as np
from jax import lax
from jax.experimental import pallas as pl
from jax.experimental.pallas import tpu as pltpu
from jax.sharding import PartitionSpec as P


REACH = 8


HIGHEST = lax.Precision.HIGHEST


def with_halo(cells, sides, width):
    for axis, dim in sides:
        count = lax.axis_size(axis)
        head = lax.slice_in_dim(cells, 0, width, axis=dim)
        tail = lax.slice_in_dim(cells, cells.shape[dim] - width, cells.shape[dim], axis=dim)
        cells = jnp.concatenate(
            [
                lax.ppermute(tail, axis, [(i, (i + 1) % count) for i in range(count)]),
                cells,
                lax.ppermute(head, axis, [((i + 1) % count, i) for i in range(count)]),
            ],
            axis=dim,
        )
    return cells


def gauss_taps(exponents):
    offsets = jnp.arange(-REACH, REACH + 1).astype(jnp.float32)
    weights = jnp.exp(-exponents[..., None] * offsets * offsets)
    return weights / jnp.sum(weights, axis=-1, keepdims=True)


def spline(offsets):
    inner_weight = jnp.where((offsets == 1) | (offsets == 2), 0.75, 0.0)
    return jnp.where((offsets == 0) | (offsets == 3), 0.25, inner_weight).astype(jnp.float32)


def band_gauss(tap_table, length):
    rows = jnp.arange(length + 2 * REACH)[:, None]
    cols = jnp.arange(length)[None, :]
    offsets = rows - cols
    onehot = (offsets[:, :, None] == jnp.arange(2 * REACH + 1)[None, None, :]).astype(jnp.float32)
    return jnp.einsum("gk,pok->gpo", tap_table, onehot, precision=HIGHEST)


def band_restrict(length):
    rows = jnp.arange(length + 2)[:, None]
    cols = jnp.arange(length // 2)[None, :]
    return spline(rows - 2 * cols)


def band_prolong(length):
    rows = jnp.arange(length + 2)[:, None]
    cols = jnp.arange(2 * length)[None, :]
    return spline(cols - 2 * rows + 3)


def apply_three(field, band_x, band_y, band_z):
    field = jnp.einsum("xyz,zc->xyc", field, band_z, precision=HIGHEST)
    field = jnp.einsum("xyz,yb->xbz", field, band_y, precision=HIGHEST)
    return jnp.einsum("xyz,xa->ayz", field, band_x, precision=HIGHEST)


def rim_cells(field):
    return with_halo(field, (("gx", 0), ("gy", 1), ("gz", 2)), 1)


def restrict_local(padded):
    sizes = padded.shape
    return apply_three(
        padded,
        band_restrict(sizes[0] - 2),
        band_restrict(sizes[1] - 2),
        band_restrict(sizes[2] - 2),
    )


def prolong_local(field):
    sizes = field.shape
    return apply_three(
        rim_cells(field), band_prolong(sizes[0]), band_prolong(sizes[1]), band_prolong(sizes[2])
    )


def prolong_from_whole(whole_grid, brick):
    padded = jnp.pad(whole_grid, 1, mode="wrap")
    starts = (
        lax.axis_index("gx") * brick[0],
        lax.axis_index("gy") * brick[1],
        lax.axis_index("gz") * brick[2],
    )
    piece_cells = lax.dynamic_slice(padded, starts, (brick[0] + 2, brick[1] + 2, brick[2] + 2))
    return apply_three(
        piece_cells, band_prolong(brick[0]), band_prolong(brick[1]), band_prolong(brick[2])
    )


def assemble(gathered, brick):
    count_x = lax.axis_size("gx")
    count_y = lax.axis_size("gy")
    count_z = lax.axis_size("gz")
    blocks = gathered.reshape(count_x, count_y, count_z, brick[0], brick[1], brick[2])
    blocks = jnp.transpose(blocks, (0, 3, 1, 4, 2, 5))
    return blocks.reshape(count_x * brick[0], count_y * brick[1], count_z * brick[2])


def top_level(field, top_x, top_y, top_z):
    field = jnp.einsum("ia,abc->ibc", top_x, field, precision=HIGHEST)
    field = jnp.einsum("jb,ibc->ijc", top_y, field, precision=HIGHEST)
    return jnp.einsum("kc,ijc->ijk", top_z, field, precision=HIGHEST)


def gauss_and_restrict(field, tap_table, weights):
    size_x, size_y, size_z = field.shape
    band_z = band_gauss(tap_table, size_z)
    band_y = band_gauss(tap_table, size_y)
    band_x = band_gauss(tap_table, size_x) * weights[:, None, None]
    padded = with_halo(field, (("gx", 0), ("gy", 1), ("gz", 2)), REACH)
    along_z = jnp.einsum("xyp,gpo->xygo", padded, band_z, precision=HIGHEST)
    along_y = jnp.einsum("xpgz,gpw->xgwz", along_z, band_y, precision=HIGHEST)
    result = jnp.einsum("pgwz,gpv->vwz", along_y, band_x, precision=HIGHEST)
    inner_cells = padded[
        REACH - 1 : size_x + REACH + 1,
        REACH - 1 : size_y + REACH + 1,
        REACH - 1 : size_z + REACH + 1,
    ]
    coarse = restrict_local(inner_cells)
    return (result, coarse)


def local_any(charges, exponents, amplitudes, top_x, top_y, top_z):
    tap_table = gauss_taps(exponents)
    term_zero, level_one = gauss_and_restrict(charges, tap_table[0], amplitudes[0])
    term_one, level_two = gauss_and_restrict(level_one, tap_table[1], amplitudes[1])
    level_three = restrict_local(rim_cells(level_two))
    level_four = restrict_local(rim_cells(level_three))
    brick_four = level_four.shape
    gathered = lax.all_gather(level_four.reshape(1, -1), ("gx", "gy", "gz"), axis=0, tiled=True)
    phi_four = top_level(assemble(gathered, brick_four), top_x, top_y, top_z)
    phi_three = prolong_from_whole(phi_four, brick_four)
    phi_two = prolong_local(phi_three)
    phi_one = term_one + prolong_local(phi_two)
    return term_zero + prolong_local(phi_one)


F32 = jnp.float32
BF16 = jnp.bfloat16
LANES = 128
FAR = 1.0e9
GAUSSIAN_RIM = REACH + 1


def up8(count):
    return -(-count // 8) * 8


def restrict_weights(fine, coarse):
    offsets = np.asarray(fine)[None, :] - 2 * np.asarray(coarse)[:, None] + 1
    inner = np.where((offsets == 1) | (offsets == 2), 0.75, 0.0)
    return np.where((offsets == 0) | (offsets == 3), 0.25, inner).astype(np.float32)


def reach_four(length):
    total, cells = np.eye(length, dtype=np.float32), np.arange(length)
    for level in range(1, 5):
        coarse = np.arange(-1, length // 2**level + 1)
        total = restrict_weights(cells, coarse) @ total
        cells = coarse
    return total


def prolong_three_whole(count):
    total = np.eye(count, dtype=np.float32)
    for level in range(3):
        size = count * 2**level
        step = np.zeros((2 * size, size), np.float32)
        for cell in range(size):
            for offset, weight in ((-1, 0.25), (0, 0.75), (1, 0.75), (2, 0.25)):
                step[(2 * cell + offset) % (2 * size), cell] += weight
        total = step @ total
    return total


def padded(table, rows, cols):
    out = np.zeros((rows, cols), np.float32)
    out[: table.shape[0], : table.shape[1]] = table
    return out


class Plan:
    def __init__(self, brick, counts):
        self.brick, self.counts = brick, counts
        bx, by, bz = brick
        self.half = by // 2
        self.rim = up8(2 * GAUSSIAN_RIM + 1)
        self.fine_rows = bz + 2 * REACH
        self.cx, self.cy = bx // 2 + 2, by // 2 + 2
        self.window = bz // 2 + 2 * GAUSSIAN_RIM
        self.window_rows = up8(self.window)
        self.out_z = bz // 2 + 2
        self.sent_top = up8(bz // 16 + 2)
        self.top_rows = up8(2 * (bz // 16 + 2))
        self.top_z = bz // 16 + 2
        self.top_x, self.top_y = bx // 16 + 2, by // 16 + 2
        self.group = 16
        x_of, y_of = self.own_cells()
        rz = reach_four(bz)
        self.top_left = padded(rz, self.sent_top, bz)
        rx, ry = reach_four(bx), reach_four(by)
        self.top_right, self.rest_right = [], []
        sx = restrict_weights(np.arange(bx), np.arange(-1, bx // 2 + 1))
        sy = restrict_weights(np.arange(by), np.arange(-1, by // 2 + 1))
        for part in range(2):
            y = y_of + part * self.half
            table = rx[:, x_of][:, None, :] * ry[:, y][None, :, :]
            self.top_right.append(padded(table.reshape(-1, LANES).T, LANES, LANES))
            table = sx[:, x_of][:, None, :] * sy[:, y][None, :, :]
            self.rest_right.append(padded(table.reshape(-1, LANES).T, LANES, LANES))
        z_in = np.concatenate([np.arange(bz), bz + np.arange(self.rim), np.arange(-self.rim, 0)])
        z_out = np.arange(-GAUSSIAN_RIM, bz // 2 + GAUSSIAN_RIM)
        self.rest_left = padded(restrict_weights(z_in, z_out), self.window_rows, z_in.size)
        spread = restrict_weights(np.arange(bz), np.arange(-1, bz // 2 + 1)).T
        self.back_left = padded(spread.T, LANES, bz)
        cols = []
        for part in range(2):
            y = y_of + part * self.half
            table = sx[:, x_of][:, None, :] * sy[:, y][None, :, :]
            cols.append(padded(table.reshape(-1, LANES), LANES, LANES))
        self.out_cells = -(-self.cx * self.cy // 16) * 16
        self.back_right = np.concatenate(cols, axis=1).T[:, : self.out_cells]
        self.message = self.fine_rows + self.window_rows + self.top_rows

    def constants(self, kernels):
        rest = self.rest_left
        fine_cells, fine_dz = self.fine_tables()
        coarse_cells, out_cells, coarse_dz = self.coarse_tables()
        spread_x, pick_x, spread_y, pick_y, spread_z, pick_z, lift_x, lift_y = self.top_tables(kernels)
        named = {
            "rest_left": rest[:, :LANES],
            "rest_far": rest[:, LANES:],
            "rest_right": np.concatenate(self.rest_right),
            "fine_cells": fine_cells,
            "fine_dz": fine_dz,
            "coarse_cells": coarse_cells,
            "out_cells": out_cells.reshape(-1, LANES),
            "coarse_dz": coarse_dz,
            "back": self.back_left,
            "back_turned": self.back_left.T,
            "back_right": self.back_right,
            "spread_x": spread_x.reshape(-1, 16),
            "pick_x": pick_x[:, :, 0].reshape(-1, LANES),
            "spread_y": spread_y.reshape(-1, 16),
            "pick_y": pick_y[:, :, 0].reshape(-1, LANES),
            "pick_pair": pick_y[:, :, 1].reshape(-1, LANES),
            "spread_z": spread_z.reshape(-1, 16),
            "pick_z": pick_z.reshape(-1, self.top_rows),
            "lift_x": lift_x,
            "lift_y": lift_y,
        }
        at, starts, pieces = 0, {}, []
        for name, table in named.items():
            rows = -(-table.shape[0] // 16) * 16
            starts[name] = at
            pieces.append(padded(table, rows, LANES))
            at += rows
        self.starts = starts
        return np.concatenate(pieces)

    def fine_tables(self):
        bx, _, bz = self.brick
        x_of, y_of = self.own_cells()
        strip, x_far = np.arange(LANES) // (LANES // 2), x_of % (LANES // 2 // self.half)
        right, left = bx + x_far, x_far - REACH
        cells = np.stack([x_of, y_of, np.where(strip == 0, right, left), np.where(strip == 0, left, right)])
        z_in = np.concatenate([np.arange(bz), np.arange(-REACH, 0), bz + np.arange(REACH)])
        distance = z_in[:, None] - np.arange(bz)[None, :]
        squared = np.where(np.abs(distance) <= REACH, distance * distance, FAR)
        return padded(cells, 8, LANES), squared.astype(np.float32)

    def coarse_tables(self):
        bx, _, _ = (size // 2 for size in self.brick)
        lane = np.arange(LANES)
        cell, count = lane // self.cy, self.cx * self.cy
        own = cell - 1
        extra = cell >= self.cx
        far_right = np.where(extra, 3 * bx - 1 + cell - self.cx, bx + own)
        far_left = np.where(extra, -2 * bx - 1 + cell - self.cx, own - bx)
        cells = [own, own, own + bx, own - bx, far_left, far_right, lane % self.cy - 1]
        cells += [np.where(lane < count, 0.0, FAR), np.where(cell < self.cx + 2, 0.0, FAR)]
        row = np.arange(self.out_cells)[:, None] + np.zeros((1, LANES))
        outs = np.stack([row // self.cy - 1, row % self.cy - 1, np.where(row < count, 0.0, FAR)])
        z_in, z_out = np.arange(self.window_rows) - GAUSSIAN_RIM, np.arange(LANES) - 1
        distance = z_in[:, None] - z_out[None, :]
        near = (np.abs(distance) <= REACH) & (np.arange(LANES) < self.out_z)[None, :]
        near = near & (np.arange(self.window_rows) < self.window)[:, None]
        squared = np.where(near, distance * distance, FAR)
        return padded(np.stack(cells), 16, LANES), outs.astype(np.float32), squared.astype(np.float32)

    def top_tables(self, kernels):
        four = [size // 16 for size in self.brick]
        lane = np.arange(2 * LANES)
        group, cell, partner = (lane % LANES) // self.group, lane % self.group, lane // LANES
        used = cell < self.top_x * self.top_y
        tables = []
        for axis in range(3):
            count, size = kernels[axis].shape[0], self.brick[axis] // 2
            whole = prolong_three_whole(count)
            outs = (self.cx, self.cy, self.out_z)[axis]
            spread, pick = [], []
            for place in range(self.counts[axis]):
                index = (place * size - 1 + np.arange(outs)) % (8 * count)
                spread.append(padded(whole[index], 16 if axis < 2 else LANES, 16))
                if axis == 0:
                    cells = (place ^ (group % 4)) * four[0] + cell // self.top_y - 1
                    valid = used
                elif axis == 1:
                    cells = (place ^ partner ^ (3 * (group // 4))) * four[1] + cell % self.top_y - 1
                    valid = used
                else:
                    row = np.arange(self.top_rows)
                    side, at = row // self.top_z, row % self.top_z
                    cells = (place ^ side) * four[2] + at - 1
                    valid = side < 2
                hot = (np.arange(count)[:, None] == (cells % count)[None, :]) & valid[None, :]
                hot = padded(hot, 16, cells.size)
                pick.append(hot if axis == 2 else hot.reshape(16, 2, LANES))
            tables += [np.stack(spread), np.stack(pick)]
        out = np.arange(self.out_cells)
        tables.append((out[:, None] // self.cy == np.arange(16)[None, :]).astype(np.float32))
        tables.append((out[:, None] % self.cy == np.arange(16)[None, :]).astype(np.float32))
        return tables

    def own_cells(self):
        lane = np.arange(LANES)
        return lane // self.half, lane % self.half


def fits(brick, counts, tops):
    bx, by, bz = brick
    return (
        counts == (4, 4, 2)
        and bx * (by // 2) == LANES
        and by % 16 == 0
        and bx % 16 == 0
        and bz == LANES
        and bx // 2 == REACH
        and by // 2 == REACH
        and (bx // 2 + 4) * (by // 2 + 2) <= LANES
        and (bx // 16 + 2) * (by // 16 + 2) <= 16
        and max(top.shape[0] for top in tops) <= 16
    )


def split(value):
    high = value.astype(BF16)
    return high, (value - high.astype(F32)).astype(BF16)


def dot(left, right):
    return jnp.dot(left, right, preferred_element_type=F32)


def dot_left(exact, value):
    high, low = split(value)
    return dot(exact, high) + dot(exact, low)


def dot_right(value, exact):
    high, low = split(value)
    return dot(high, exact) + dot(low, exact)


def dot_split(left, right):
    return dot(left[0], right[0]) + dot(left[1], right[0]) + dot(left[0], right[1])


def pick(flags_ref, axis, even, odd):
    return jnp.where(jnp.broadcast_to(flags_ref[axis : axis + 1], even.shape) < 0.5, even, odd)


def exact_tables(plan, ref):
    def read(name, rows, at=0):
        start = plan.starts[name] + at * rows
        return ref[start : start + rows].astype(BF16)

    return read


def lanes_of(rows):
    return lax.broadcasted_iota(jnp.int32, (rows, LANES), 1)


def halves(first, second):
    low = lanes_of(first.shape[0]) < LANES // 2
    return (
        jnp.where(low, first, pltpu.roll(second, LANES // 2, 1)),
        jnp.where(low, pltpu.roll(first, LANES // 2, 1), second),
    )


def start_kernel(plan, charges_ref, table_ref, own_ref, out_ref):
    _, _, bz = plan.brick
    rim, half = plan.rim, plan.half
    top, size = None, plan.sent_top
    left = split(table_ref[:size])
    for part in range(2):
        cells = charges_ref[:, part * half : (part + 1) * half, :].reshape(LANES, bz).T
        own_ref[part] = cells
        out_ref[2 * rim * part : 2 * rim * part + rim] = cells[:rim]
        out_ref[2 * rim * part + rim : 2 * rim * (part + 1)] = cells[bz - rim :]
        right = split(table_ref[size + LANES * part : size + LANES * (part + 1)])
        rows = dot_split(split(dot_split(left, split(cells))), right)
        top = rows if top is None else top + rows
    out_ref[4 * rim :] = top


def setup_kernel(count, *refs):
    copies = [pltpu.make_async_copy(refs[at], refs[count + at], refs[2 * count].at[at]) for at in range(count)]
    for copy in copies:
        copy.start()
    for copy in copies:
        copy.wait()


def spread_kernel(plan, flags_ref, own_ref, sent_ref, got_ref, table_ref, fine_ref, out_ref, side_x_ref,
                  side_y_ref):
    _, _, bz = plan.brick
    rim, rows = plan.rim, plan.fine_rows
    table = exact_tables(plan, table_ref)
    coarse = None
    for part in range(2):
        cells = own_ref[part]
        far = got_ref[2 * rim * part : 2 * rim * (part + 1)]
        fine_ref[part, :bz] = cells
        fine_ref[part, bz : bz + REACH] = far[2 * rim - REACH :]
        fine_ref[part, bz + REACH :] = far[:REACH]
        summed = dot_left(table("rest_left", plan.window_rows), cells)
        summed = summed + dot_left(table("rest_far", plan.window_rows)[:, : 2 * rim], far)
        summed = dot_right(summed, table("rest_right", LANES, part))
        coarse = summed if coarse is None else coarse + summed
    low, high = halves(fine_ref[0], fine_ref[1])
    out_ref[:rows] = pick(flags_ref, 0, high, low)
    side_x_ref[...] = pick(flags_ref, 0, low, high)
    side_y_ref[:rows] = pick(flags_ref, 1, fine_ref[0], fine_ref[1])
    side_y_ref[rows:] = coarse
    out_ref[rows : rows + plan.window_rows] = coarse
    top = rows + plan.window_rows
    cells = plan.top_z
    out_ref[top : top + cells] = sent_ref[4 * rim : 4 * rim + cells]
    out_ref[top + cells : top + 2 * cells] = got_ref[4 * rim : 4 * rim + cells]
    if plan.top_rows > 2 * cells:
        out_ref[top + 2 * cells :] = jnp.zeros((plan.top_rows - 2 * cells, LANES), F32)


def half_of(plan, flags_ref, strip_ref):
    rows = plan.fine_rows
    low, high = halves(strip_ref[: rows // 2], strip_ref[rows // 2 : rows])
    return pick(flags_ref, 1, low, high)


def pass_kernel(plan, flags_ref, sent_ref, got_ref, out_ref, side_ref):
    rows = plan.fine_rows
    own = sent_ref[rows : rows + plan.window_rows]
    far = got_ref[rows : rows + plan.window_rows]
    lane = lanes_of(plan.window_rows)
    edge, count = 2 * plan.cy, plan.cx * plan.cy
    last = count - edge
    beyond = (lane >= count) & (lane < count + edge)
    left = far + jnp.where(lane < edge, pltpu.roll(own, LANES - last, 1), 0.0)
    left = left + jnp.where(beyond, pltpu.roll(own, count, 1), 0.0)
    right = far + jnp.where((lane >= last) & (lane < count), pltpu.roll(own, last, 1), 0.0)
    right = right + jnp.where(beyond, pltpu.roll(own, edge, 1), 0.0)
    out_ref[: plan.window_rows] = pick(flags_ref, 0, left, right)
    top = rows + plan.window_rows
    out_ref[plan.window_rows :] = sent_ref[top:] + pltpu.roll(got_ref[top:], plan.group, 1)
    side_ref[: rows // 2] = half_of(plan, flags_ref, got_ref)
    side_ref[rows // 2 :] = far


def stack_kernel(plan, flags_ref, fine_ref, sent_ref, first_ref, side_ref, second_ref, cells_ref, out_ref):
    rows, window = plan.fine_rows, plan.window_rows
    low, high = halves(first_ref[:rows], side_ref[...])
    for part, other in ((0, low), (1, high)):
        cells_ref[part, :rows] = fine_ref[part]
        cells_ref[part, rows:] = other
    out_ref[: rows // 2] = half_of(plan, flags_ref, side_ref)
    out_ref[rows // 2 : rows // 2 + window] = second_ref[:window]
    out_ref[rows // 2 + window :] = sent_ref[window:] + pltpu.roll(second_ref[window:], 2 * plan.group, 1)


def turned(left, right):
    return lax.dot_general(left, right, (((1,), (1,)), ((), ())), preferred_element_type=F32)


def dot_turned(left, right):
    return turned(left[0], right[0]) + turned(left[1], right[0]) + turned(left[0], right[1])


def fine_weights_kernel(plan, terms, flags_ref, params_ref, table_ref, kf_ref, kf_low_ref, zf_ref, zf_low_ref):
    bx, by, _ = plan.brick
    cells_ref = table_ref.at[pl.ds(plan.starts["fine_cells"], 8)]
    dz_ref = table_ref.at[pl.ds(plan.starts["fine_dz"], plan.fine_rows)]
    half = plan.half
    own_x, own_y = cells_ref[0:1], cells_ref[1:2]
    far_x = pick(flags_ref, 0, cells_ref[2:3], cells_ref[3:4])
    x_out = lax.broadcasted_iota(jnp.int32, (bx, LANES), 0).astype(F32)
    y_out = lax.broadcasted_iota(jnp.int32, (half, LANES), 0).astype(F32)
    y_far = jnp.full((1, LANES), -half, F32)
    y_far = pick(flags_ref, 1, y_far, y_far + half + by)

    def decay(exponent, distance):
        return jnp.where(jnp.abs(distance) <= REACH, jnp.exp(-exponent * distance * distance), 0.0)

    for term in range(terms):
        exponent = params_ref[term : term + 1]
        scale = params_ref[terms + term : terms + term + 1]
        along_x = [decay(exponent, x_in - x_out)[:, None, :] for x_in in (own_x, far_x)]
        for group in range(3):
            y_in = own_y + (F32(group * half) if group < 2 else y_far)
            for part in range(2):
                along_y = decay(exponent, y_in - (y_out + part * half)) * scale
                for block in range(2):
                    high, low = split((along_x[block] * along_y[None]).reshape(bx * half, LANES))
                    rows, cols = pl.ds(part * LANES, LANES), pl.ds((2 * group + block) * LANES, LANES)
                    kf_ref[term, rows, cols] = high
                    kf_low_ref[term, rows, cols] = low
        zf_ref[term], zf_low_ref[term] = split(
            jnp.exp(-exponent * dz_ref[...]) * params_ref[2 * terms + term : 2 * terms + term + 1]
        )


def set_params(terms, exponents_ref, amplitudes_ref, tops, params_ref):
    offsets = lax.broadcasted_iota(jnp.int32, (1, LANES), 1).astype(F32) - REACH
    squared = jnp.where(offsets <= REACH, offsets * offsets, FAR)
    for level in range(2):
        for term in range(terms):
            at = slice(level, level + 1), slice(term, term + 1)
            exponent = exponents_ref[at]
            scale = 1.0 / jnp.sum(jnp.exp(-exponent * squared), axis=1, keepdims=True)
            row = 3 * terms * level + term
            for value in (exponent, scale * scale * amplitudes_ref[at], scale):
                params_ref[row : row + 1] = jnp.broadcast_to(value, (1, LANES))
                row = row + terms
    params_ref[6 * terms :] = jnp.zeros((3 * 16, LANES), F32)
    for axis, source in enumerate(tops):
        at, count = 6 * terms + 16 * axis, source.shape[0]
        params_ref[at : at + count, :count] = source[...]


def coarse_weights_kernel(plan, terms, flags_ref, table_ref, exponents_ref, amplitudes_ref, top_x_ref, top_y_ref,
                          top_z_ref, params_ref, k1_ref, k1_low_ref, z1_ref, z1_low_ref, zc_ref, kc_ref):
    set_params(terms, exponents_ref, amplitudes_ref, (top_x_ref, top_y_ref, top_z_ref), params_ref)
    cells_ref = table_ref.at[pl.ds(plan.starts["coarse_cells"], 16)]
    at, count = plan.starts["out_cells"], plan.out_cells
    out_cells_ref = [table_ref[at + count * part : at + count * (part + 1)] for part in range(3)]
    dz_ref = table_ref.at[pl.ds(plan.starts["coarse_dz"], plan.window_rows)]
    zc_ref[...], kc_ref[...] = top_weights(plan, terms, flags_ref, params_ref, table_ref)
    bx, by = plan.brick[0] // 2, plan.brick[1] // 2
    base = 3 * terms

    def squared(distance, count):
        distance = distance - count * jnp.floor((distance + count // 2) * (1.0 / count))
        return jnp.where(jnp.abs(distance) <= REACH, distance * distance, FAR)

    x_out, y_out = out_cells_ref[0], out_cells_ref[1]
    squares_x = []
    for slot in range(3):
        x_in = pick(flags_ref, 0, cells_ref[2 * slot : 2 * slot + 1], cells_ref[2 * slot + 1 : 2 * slot + 2])
        used = cells_ref[7:8] if slot < 2 else cells_ref[8:9]
        squares_x.append(squared(x_in - x_out, bx * plan.counts[0]) + used)
    toward = jnp.full((1, LANES), by, F32)
    toward = pick(flags_ref, 1, toward, -toward)
    for group, offset in enumerate((F32(0), -toward, F32(2 * by))):
        square_y = squared(cells_ref[6:7] + offset - y_out, by * plan.counts[1]) + out_cells_ref[2]
        for slot in range(3):
            total = squares_x[slot] + square_y
            cols = pl.ds((3 * group + slot) * LANES, LANES)
            for term in range(terms):
                exponent = params_ref[base + term : base + term + 1]
                scale = params_ref[base + terms + term : base + terms + term + 1]
                high, low = split(jnp.exp(-exponent * total) * scale)
                rows = pl.ds(term * plan.out_cells, plan.out_cells)
                k1_ref[rows, cols] = high
                k1_low_ref[rows, cols] = low
    for term in range(terms):
        exponent = params_ref[base + term : base + term + 1]
        scale = params_ref[base + 2 * terms + term : base + 2 * terms + term + 1]
        value = dot_right(jnp.exp(-exponent * dz_ref[...]) * scale, exact_tables(plan, table_ref)("back", LANES))
        z1_ref[term], z1_low_ref[term] = split(value)


def top_weights(plan, terms, flags_ref, params_ref, table_ref):
    def chain(*factors):
        value = factors[0]
        for factor in factors[1:]:
            value = dot_split(split(value), split(factor))
        return value

    def read(name, rows, axis=None, partner=0):
        start = plan.starts[name]
        if axis is None:
            return table_ref[start : start + rows]
        total, first = None, 3 + sum(plan.counts[:axis])
        for place in range(plan.counts[axis]):
            flag = flags_ref[first + (place ^ partner) : first + (place ^ partner) + 1]
            value = table_ref[start + rows * place : start + rows * (place + 1)] * flag
            total = value if total is None else total + value
        return total

    size = 16

    def along(axis, spread, chosen, partner=0):
        top = params_ref[6 * terms + size * axis : 6 * terms + size * (axis + 1)]
        value = chain(read(spread, size, axis, partner)[:, :size], top)[:, :size]
        return chain(value, read(chosen, size, axis, partner))

    lift_x, lift_y = (read(name, plan.out_cells)[:, :size] for name in ("lift_x", "lift_y"))
    along_x = chain(lift_x, along(0, "spread_x", "pick_x"))
    right = []
    for partner, chosen in enumerate(("pick_y", "pick_pair")):
        right.append(along_x * chain(lift_y, along(1, "spread_y", chosen, partner)))
    top = params_ref[6 * terms + 2 * size : 6 * terms + 3 * size]
    value = chain(read("spread_z", LANES, 2)[:, :size], top)[:, :size]
    left = chain(value, read("pick_z", size, 2)[:, : plan.top_rows])
    return dot_left(read("back_turned", LANES).astype(BF16), left), jnp.concatenate(right, axis=1)


def sum_fine(terms, blocks, refs, at):
    cells, cols = split(blocks), pl.ds(at * LANES, blocks.shape[1])
    return [dot_turned((refs[0][term, :, cols], refs[1][term, :, cols]), cells) for term in range(terms)]


def sum_coarse(blocks, refs, at):
    cols, count = pl.ds(at * LANES, blocks.shape[1]), blocks.shape[0]
    high = blocks.astype(BF16)
    exact = high.astype(F32)
    gap = jnp.zeros((LANES - count, blocks.shape[1]), F32)
    both = jnp.concatenate([exact, gap, blocks - exact], axis=0).astype(BF16)
    sums = turned(refs[0][:, cols], both)
    return sums[:, :count] + sums[:, LANES : LANES + count] + turned(refs[1][:, cols], high)


def fine_potential(fine, refs):
    total = None
    for term, value in enumerate(fine):
        value = dot_split(split(value), (refs[0][term], refs[1][term]))
        total = value if total is None else total + value
    return total


def coarse_potential(plan, terms, coarse, refs, top, kernel, table_ref):
    level_one = dot_turned(split(kernel), split(top))
    for term in range(terms):
        piece = split(coarse[term * plan.out_cells : (term + 1) * plan.out_cells])
        level_one = level_one + dot_split(piece, (refs[0][term], refs[1][term]))
    table = exact_tables(plan, table_ref)
    return dot_left(table("back_right", 2 * LANES)[:, : plan.out_cells], level_one)


def near_kernel(plan, terms, flags_ref, cells_ref, own_ref, first_ref, second_ref, kf_ref, kf_low_ref, k1_ref,
                k1_low_ref, zf_ref, zf_low_ref, fine_ref, coarse_ref, give_fine_ref, give_coarse_ref):
    rows, window = plan.fine_rows, plan.window_rows
    kf, k1 = (kf_ref, kf_low_ref), (k1_ref, k1_low_ref)
    groups = [jnp.concatenate([cells_ref[part, :rows], cells_ref[part, rows:]], axis=1) for part in range(2)]
    near = [own_ref[rows : rows + window], first_ref[rows : rows + window], second_ref[:window]]
    near = jnp.concatenate(near, axis=1)
    other = [pick(flags_ref, 1, cells_ref[1, at : at + rows], cells_ref[0, at : at + rows]) for at in (0, rows)]
    other = jnp.concatenate(other, axis=1)
    give_fine_ref[...] = fine_potential(sum_fine(terms, other, kf, 4), (zf_ref, zf_low_ref))
    give_coarse_ref[...] = sum_coarse(near, k1, 3)
    for term, value in enumerate(sum_fine(terms, jnp.concatenate(groups, axis=1), kf, 0)):
        fine_ref[term] = value
    coarse_ref[...] = sum_coarse(near, k1, 0)


def top_charges(plan, sent_ref, got_ref, zc_ref):
    start = plan.fine_rows // 2 + plan.window_rows
    top = sent_ref[start:] + pltpu.roll(got_ref[start:], 4 * plan.group, 1)
    return dot_split(split(zc_ref[...]), split(top))


def arrived(plan, side_ref, strip_ref, got_ref):
    rows = plan.fine_rows
    pieces = [side_ref[rows:], strip_ref[rows // 2 :], got_ref[rows // 2 : rows // 2 + plan.window_rows]]
    return jnp.concatenate(pieces, axis=1)


def give_kernel(plan, terms, fine_ref, coarse_ref, side_ref, strip_ref, sent_ref, got_ref, k1_ref, k1_low_ref,
                z1_ref, z1_low_ref, zc_ref, kc_ref, table_ref, out_ref):
    coarse = coarse_ref[...] + sum_coarse(arrived(plan, side_ref, strip_ref, got_ref), (k1_ref, k1_low_ref), 6)
    top = top_charges(plan, sent_ref, got_ref, zc_ref)
    out_ref[...] = fine_ref[...] + coarse_potential(
        plan, terms, coarse, (z1_ref, z1_low_ref), top, kc_ref[:, LANES:], table_ref
    )


def keep_kernel(plan, terms, fine_ref, coarse_ref, side_ref, strip_ref, sent_ref, got_ref, kf_ref, kf_low_ref,
                k1_ref, k1_low_ref, zf_ref, zf_low_ref, z1_ref, z1_low_ref, zc_ref, kc_ref, table_ref, out_ref):
    rows = plan.fine_rows
    strips = jnp.concatenate(halves(strip_ref[: rows // 2], got_ref[: rows // 2]), axis=0)
    blocks = jnp.concatenate([side_ref[:rows], strips], axis=1)
    fine = sum_fine(terms, blocks, (kf_ref, kf_low_ref), 4)
    fine = [fine_ref[term] + value for term, value in enumerate(fine)]
    coarse = coarse_ref[...] + sum_coarse(arrived(plan, side_ref, strip_ref, got_ref), (k1_ref, k1_low_ref), 3)
    top = top_charges(plan, sent_ref, got_ref, zc_ref)
    out_ref[...] = fine_potential(fine, (zf_ref, zf_low_ref)) + coarse_potential(
        plan, terms, coarse, (z1_ref, z1_low_ref), top, kc_ref[:, :LANES], table_ref
    )


def add_kernel(plan, own_ref, got_ref, out_ref):
    half = plan.half
    for part in range(2):
        rows = pl.ds(part * LANES, LANES)
        cells = own_ref[rows] + got_ref[rows]
        out_ref[:, part * half : (part + 1) * half, :] = cells.reshape(plan.brick[0], half, plan.brick[2])


def call(body, shapes, *operands, scalars=0, after=(), last=False, plain=False, copies=0):
    specs = [pl.BlockSpec(memory_space=pltpu.SMEM)] * scalars
    specs += [pl.BlockSpec(memory_space=pltpu.VMEM)] * (len(operands) - scalars)
    if copies:
        specs = [pl.BlockSpec(memory_space=pl.ANY)] * len(operands)
    specs += [pl.BlockSpec(memory_space=pl.ANY)] * len(after)

    def keep(operand, space=pltpu.VMEM):
        return pltpu.with_memory_space_constraint(operand, space)

    if plain:
        operands = tuple(keep(operand, pltpu.HBM) for operand in operands)
    kept = list(operands) if plain else [keep(operand) for operand in operands[scalars:]]
    kept = kept[scalars:] if plain else kept
    kept += [keep(operand) for operand in after]
    kinds = [shape if isinstance(shape[-1], int) else shape[0] for shape in shapes]
    types = [F32 if isinstance(shape[-1], int) else shape[1] for shape in shapes]
    first = len(operands)

    def run(*refs):
        body(*refs[:first], *refs[first + len(after) :])

    return pl.pallas_call(
        run,
        out_shape=[
            jax.ShapeDtypeStruct(kind, kept_as) if last else pltpu.VMEM(kind, kept_as)
            for kind, kept_as in zip(kinds, types)
        ],
        in_specs=specs,
        out_specs=[pl.BlockSpec(memory_space=pltpu.VMEM)] * len(shapes),
        scratch_shapes=[pltpu.SemaphoreType.DMA((copies,))] if copies else (),
        compiler_params=pltpu.CompilerParams(vmem_limit_bytes=8 << 20),
    )(*(operands[:scalars] if plain else [keep(operand, pltpu.SMEM) for operand in operands[:scalars]]), *kept)


def pair(value, axis, bits):
    count = lax.axis_size(axis)
    return lax.ppermute(value, axis, [(i, i ^ bits) for i in range(count)])


def local_short(plan, charges, exponents, amplitudes, top_x, top_y, top_z):
    row = lax.broadcasted_iota(jnp.int32, (3 + sum(plan.counts), LANES), 0)
    flags, first = jnp.zeros(row.shape, F32), 3
    for axis, name in enumerate(("gx", "gy", "gz")):
        place = lax.axis_index(name).astype(jnp.int32)
        flags = jnp.where(row == axis, (place % 2).astype(F32), flags)
        flags = jnp.where(row == first + place, 1.0, flags)
        first = first + plan.counts[axis]
    terms = exponents.shape[1]
    bx, by, bz = plan.brick
    rows, window = plan.fine_rows, plan.window_rows
    bind = functools.partial

    own, sent_z = call(
        bind(start_kernel, plan),
        [(2, bz, LANES), (4 * plan.rim + plan.sent_top, LANES)],
        charges,
        jnp.asarray(np.concatenate([plan.top_left, *plan.top_right])),
        plain=True,
    )
    got_z = pair(sent_z, "gz", 1)
    held = (jnp.asarray(plan.constants((top_x, top_y, top_z))), exponents, amplitudes, top_x, top_y, top_z)
    table, *small = call(
        bind(setup_kernel, len(held)),
        [array.shape for array in held],
        *held,
        after=(sent_z,),
        plain=True,
        copies=len(held),
    )
    fine, sent_a, side_x, side_y = call(
        bind(spread_kernel, plan),
        [(2, rows, LANES), (plan.message, LANES), (rows, LANES), (rows + window, LANES)],
        flags,
        own,
        sent_z,
        got_z,
        table,
    )
    got_a = pair(sent_a, "gx", 1)
    got_x = pair(side_x, "gx", 3)
    got_y = pair(side_y, "gy", 3)
    sent_b, side_b = call(
        bind(pass_kernel, plan),
        [(plan.message - rows, LANES), (rows // 2 + window, LANES)],
        flags,
        sent_a,
        got_a,
    )
    got_b = pair(sent_b, "gx", 2)
    got_s = pair(side_b, "gy", 3)
    k1 = ((terms * plan.out_cells, 9 * LANES), BF16)
    params, *k1, z1, z1_low, zc, kc = call(
        bind(coarse_weights_kernel, plan, terms),
        [
            (6 * terms + 3 * 16, LANES),
            k1,
            k1,
            ((terms, window, LANES), BF16),
            ((terms, window, LANES), BF16),
            (LANES, plan.top_rows),
            (plan.out_cells, 2 * LANES),
        ],
        flags,
        table,
        *small,
        after=(sent_b,),
    )
    size = rows // 2 + window + plan.top_rows
    cells, sent_c = call(
        bind(stack_kernel, plan),
        [(2, 2 * rows, LANES), (size, LANES)],
        flags,
        fine,
        sent_b,
        got_a,
        got_x,
        got_b,
        after=(z1, got_y, got_s),
    )
    got_c = pair(sent_c, "gy", 3)
    kf = ((terms, 2 * LANES, 6 * LANES), BF16)
    *kf, zf, zf_low = call(
        bind(fine_weights_kernel, plan, terms),
        [kf, kf, ((terms, rows, LANES), BF16), ((terms, rows, LANES), BF16)],
        flags,
        params,
        table,
        after=(sent_c,),
    )
    give = (2 * LANES, bz)
    fine_sum, coarse_sum, give_fine, give_coarse = call(
        bind(near_kernel, plan, terms),
        [(terms, 2 * LANES, rows), (terms * plan.out_cells, window), give, (terms * plan.out_cells, window)],
        flags,
        cells,
        sent_a,
        got_a,
        got_b,
        *kf,
        *k1,
        zf,
        zf_low,
        after=(sent_c,),
    )
    ends = (z1, z1_low, zc, kc, table)
    (sent_d,) = call(
        bind(give_kernel, plan, terms), [give], give_fine, give_coarse, got_y, got_s, sent_c, got_c, *k1, *ends
    )
    got_d = pair(sent_d, "gy", 1)
    (kept,) = call(
        bind(keep_kernel, plan, terms),
        [give],
        fine_sum,
        coarse_sum,
        got_y,
        got_s,
        sent_c,
        got_c,
        *kf,
        *k1,
        zf,
        zf_low,
        *ends,
        after=(sent_d,),
    )
    (out,) = call(bind(add_kernel, plan), [(bx, by, bz)], kept, got_d, last=True)
    return out


def local(*arguments):
    counts = tuple(lax.axis_size(axis) for axis in ("gx", "gy", "gz"))
    brick = arguments[0].shape
    if fits(brick, counts, arguments[3:]):
        return local_short(Plan(brick, counts), *arguments)
    return local_any(*arguments)


def solution(mesh):
    in_specs = (P("gx", "gy", "gz"), P(), P(), P(), P(), P())
    out_specs = P("gx", "gy", "gz")
    return jax.shard_map(local, mesh=mesh, in_specs=in_specs, out_specs=out_specs, check_vma=False)
```

```python
import functools

import jax
import jax.numpy as jnp
import numpy as np
from jax import lax
from jax.experimental import pallas as pl
from jax.experimental.pallas import tpu as pltpu
from jax.sharding import PartitionSpec as P


REACH = 8


HIGHEST = lax.Precision.HIGHEST


def with_halo(cells, sides, width):
    for axis, dim in sides:
        count = lax.axis_size(axis)
        head = lax.slice_in_dim(cells, 0, width, axis=dim)
        tail = lax.slice_in_dim(cells, cells.shape[dim] - width, cells.shape[dim], axis=dim)
        cells = jnp.concatenate(
            [
                lax.ppermute(tail, axis, [(i, (i + 1) % count) for i in range(count)]),
                cells,
                lax.ppermute(head, axis, [((i + 1) % count, i) for i in range(count)]),
            ],
            axis=dim,
        )
    return cells


def gauss_taps(exponents):
    offsets = jnp.arange(-REACH, REACH + 1).astype(jnp.float32)
    weights = jnp.exp(-exponents[..., None] * offsets * offsets)
    return weights / jnp.sum(weights, axis=-1, keepdims=True)


def spline(offsets):
    inner_weight = jnp.where((offsets == 1) | (offsets == 2), 0.75, 0.0)
    return jnp.where((offsets == 0) | (offsets == 3), 0.25, inner_weight).astype(jnp.float32)


def band_gauss(tap_table, length):
    rows = jnp.arange(length + 2 * REACH)[:, None]
    cols = jnp.arange(length)[None, :]
    offsets = rows - cols
    onehot = (offsets[:, :, None] == jnp.arange(2 * REACH + 1)[None, None, :]).astype(jnp.float32)
    return jnp.einsum("gk,pok->gpo", tap_table, onehot, precision=HIGHEST)


def band_restrict(length):
    rows = jnp.arange(length + 2)[:, None]
    cols = jnp.arange(length // 2)[None, :]
    return spline(rows - 2 * cols)


def band_prolong(length):
    rows = jnp.arange(length + 2)[:, None]
    cols = jnp.arange(2 * length)[None, :]
    return spline(cols - 2 * rows + 3)


def apply_three(field, band_x, band_y, band_z):
    field = jnp.einsum("xyz,zc->xyc", field, band_z, precision=HIGHEST)
    field = jnp.einsum("xyz,yb->xbz", field, band_y, precision=HIGHEST)
    return jnp.einsum("xyz,xa->ayz", field, band_x, precision=HIGHEST)


def rim_cells(field):
    return with_halo(field, (("gx", 0), ("gy", 1), ("gz", 2)), 1)


def restrict_local(padded):
    sizes = padded.shape
    return apply_three(
        padded,
        band_restrict(sizes[0] - 2),
        band_restrict(sizes[1] - 2),
        band_restrict(sizes[2] - 2),
    )


def prolong_local(field):
    sizes = field.shape
    return apply_three(
        rim_cells(field), band_prolong(sizes[0]), band_prolong(sizes[1]), band_prolong(sizes[2])
    )


def prolong_from_whole(whole_grid, brick):
    padded = jnp.pad(whole_grid, 1, mode="wrap")
    starts = (
        lax.axis_index("gx") * brick[0],
        lax.axis_index("gy") * brick[1],
        lax.axis_index("gz") * brick[2],
    )
    piece_cells = lax.dynamic_slice(padded, starts, (brick[0] + 2, brick[1] + 2, brick[2] + 2))
    return apply_three(
        piece_cells, band_prolong(brick[0]), band_prolong(brick[1]), band_prolong(brick[2])
    )


def assemble(gathered, brick):
    count_x = lax.axis_size("gx")
    count_y = lax.axis_size("gy")
    count_z = lax.axis_size("gz")
    blocks = gathered.reshape(count_x, count_y, count_z, brick[0], brick[1], brick[2])
    blocks = jnp.transpose(blocks, (0, 3, 1, 4, 2, 5))
    return blocks.reshape(count_x * brick[0], count_y * brick[1], count_z * brick[2])


def top_level(field, top_x, top_y, top_z):
    field = jnp.einsum("ia,abc->ibc", top_x, field, precision=HIGHEST)
    field = jnp.einsum("jb,ibc->ijc", top_y, field, precision=HIGHEST)
    return jnp.einsum("kc,ijc->ijk", top_z, field, precision=HIGHEST)


def gauss_and_restrict(field, tap_table, weights):
    size_x, size_y, size_z = field.shape
    band_z = band_gauss(tap_table, size_z)
    band_y = band_gauss(tap_table, size_y)
    band_x = band_gauss(tap_table, size_x) * weights[:, None, None]
    padded = with_halo(field, (("gx", 0), ("gy", 1), ("gz", 2)), REACH)
    along_z = jnp.einsum("xyp,gpo->xygo", padded, band_z, precision=HIGHEST)
    along_y = jnp.einsum("xpgz,gpw->xgwz", along_z, band_y, precision=HIGHEST)
    result = jnp.einsum("pgwz,gpv->vwz", along_y, band_x, precision=HIGHEST)
    inner_cells = padded[
        REACH - 1 : size_x + REACH + 1,
        REACH - 1 : size_y + REACH + 1,
        REACH - 1 : size_z + REACH + 1,
    ]
    coarse = restrict_local(inner_cells)
    return (result, coarse)


def local_any(charges, exponents, amplitudes, top_x, top_y, top_z):
    tap_table = gauss_taps(exponents)
    term_zero, level_one = gauss_and_restrict(charges, tap_table[0], amplitudes[0])
    term_one, level_two = gauss_and_restrict(level_one, tap_table[1], amplitudes[1])
    level_three = restrict_local(rim_cells(level_two))
    level_four = restrict_local(rim_cells(level_three))
    brick_four = level_four.shape
    gathered = lax.all_gather(level_four.reshape(1, -1), ("gx", "gy", "gz"), axis=0, tiled=True)
    phi_four = top_level(assemble(gathered, brick_four), top_x, top_y, top_z)
    phi_three = prolong_from_whole(phi_four, brick_four)
    phi_two = prolong_local(phi_three)
    phi_one = term_one + prolong_local(phi_two)
    return term_zero + prolong_local(phi_one)


F32 = jnp.float32
BF16 = jnp.bfloat16
LANES = 128
FAR = 1.0e9
GAUSSIAN_RIM = REACH + 1


def up8(count):
    return -(-count // 8) * 8


def restrict_weights(fine, coarse):
    offsets = np.asarray(fine)[None, :] - 2 * np.asarray(coarse)[:, None] + 1
    inner = np.where((offsets == 1) | (offsets == 2), 0.75, 0.0)
    return np.where((offsets == 0) | (offsets == 3), 0.25, inner).astype(np.float32)


def reach_four(length):
    total, cells = np.eye(length, dtype=np.float32), np.arange(length)
    for level in range(1, 5):
        coarse = np.arange(-1, length // 2**level + 1)
        total = restrict_weights(cells, coarse) @ total
        cells = coarse
    return total


def prolong_three_whole(count):
    total = np.eye(count, dtype=np.float32)
    for level in range(3):
        size = count * 2**level
        step = np.zeros((2 * size, size), np.float32)
        for cell in range(size):
            for offset, weight in ((-1, 0.25), (0, 0.75), (1, 0.75), (2, 0.25)):
                step[(2 * cell + offset) % (2 * size), cell] += weight
        total = step @ total
    return total


def padded(table, rows, cols):
    out = np.zeros((rows, cols), np.float32)
    out[: table.shape[0], : table.shape[1]] = table
    return out


class Plan:
    def __init__(self, brick, counts):
        self.brick, self.counts = brick, counts
        bx, by, bz = brick
        self.half = by // 2
        self.rim = up8(2 * GAUSSIAN_RIM + 1)
        self.fine_rows = bz + 2 * REACH
        self.cx, self.cy = bx // 2 + 2, by // 2 + 2
        self.window = bz // 2 + 2 * GAUSSIAN_RIM
        self.window_rows = up8(self.window)
        self.out_z = bz // 2 + 2
        self.sent_top = up8(bz // 16 + 2)
        self.top_rows = up8(2 * (bz // 16 + 2))
        self.top_z = bz // 16 + 2
        self.top_x, self.top_y = bx // 16 + 2, by // 16 + 2
        self.group = 16
        x_of, y_of = self.own_cells()
        rz = reach_four(bz)
        self.top_left = padded(rz, self.sent_top, bz)
        rx, ry = reach_four(bx), reach_four(by)
        self.top_right, self.rest_right = [], []
        sx = restrict_weights(np.arange(bx), np.arange(-1, bx // 2 + 1))
        sy = restrict_weights(np.arange(by), np.arange(-1, by // 2 + 1))
        for part in range(2):
            y = y_of + part * self.half
            table = rx[:, x_of][:, None, :] * ry[:, y][None, :, :]
            self.top_right.append(padded(table.reshape(-1, LANES).T, LANES, LANES))
            table = sx[:, x_of][:, None, :] * sy[:, y][None, :, :]
            self.rest_right.append(padded(table.reshape(-1, LANES).T, LANES, LANES))
        z_in = np.concatenate([np.arange(bz), bz + np.arange(self.rim), np.arange(-self.rim, 0)])
        z_out = np.arange(-GAUSSIAN_RIM, bz // 2 + GAUSSIAN_RIM)
        self.rest_left = padded(restrict_weights(z_in, z_out), self.window_rows, z_in.size)
        spread = restrict_weights(np.arange(bz), np.arange(-1, bz // 2 + 1)).T
        self.back_left = padded(spread.T, LANES, bz)
        cols = []
        for part in range(2):
            y = y_of + part * self.half
            table = sx[:, x_of][:, None, :] * sy[:, y][None, :, :]
            cols.append(padded(table.reshape(-1, LANES), LANES, LANES))
        self.out_cells = -(-self.cx * self.cy // 16) * 16
        self.back_right = np.concatenate(cols, axis=1).T[:, : self.out_cells]
        self.message = self.fine_rows + self.window_rows + self.top_rows

    def constants(self, kernels):
        rest = self.rest_left
        fine_cells, fine_dz = self.fine_tables()
        coarse_cells, out_cells, coarse_dz = self.coarse_tables()
        spread_x, pick_x, spread_y, pick_y, spread_z, pick_z, lift_x, lift_y = self.top_tables(kernels)
        named = {
            "rest_left": rest[:, :LANES],
            "rest_far": rest[:, LANES:],
            "rest_right": np.concatenate(self.rest_right),
            "fine_cells": fine_cells,
            "fine_dz": fine_dz,
            "coarse_cells": coarse_cells,
            "out_cells": out_cells.reshape(-1, LANES),
            "coarse_dz": coarse_dz,
            "back": self.back_left,
            "back_turned": self.back_left.T,
            "back_right": self.back_right,
            "spread_x": spread_x.reshape(-1, 16),
            "pick_x": pick_x[:, :, 0].reshape(-1, LANES),
            "spread_y": spread_y.reshape(-1, 16),
            "pick_y": pick_y[:, :, 0].reshape(-1, LANES),
            "pick_pair": pick_y[:, :, 1].reshape(-1, LANES),
            "spread_z": spread_z.reshape(-1, 16),
            "pick_z": pick_z.reshape(-1, self.top_rows),
            "lift_x": lift_x,
            "lift_y": lift_y,
        }
        at, starts, pieces = 0, {}, []
        for name, table in named.items():
            rows = -(-table.shape[0] // 16) * 16
            starts[name] = at
            pieces.append(padded(table, rows, LANES))
            at += rows
        self.starts = starts
        return np.concatenate(pieces)

    def fine_tables(self):
        bx, _, bz = self.brick
        x_of, y_of = self.own_cells()
        strip, x_far = np.arange(LANES) // (LANES // 2), x_of % (LANES // 2 // self.half)
        right, left = bx + x_far, x_far - REACH
        cells = np.stack([x_of, y_of, np.where(strip == 0, right, left), np.where(strip == 0, left, right)])
        z_in = np.concatenate([np.arange(bz), np.arange(-REACH, 0), bz + np.arange(REACH)])
        distance = z_in[:, None] - np.arange(bz)[None, :]
        squared = np.where(np.abs(distance) <= REACH, distance * distance, FAR)
        return padded(cells, 8, LANES), squared.astype(np.float32)

    def coarse_tables(self):
        bx, _, _ = (size // 2 for size in self.brick)
        lane = np.arange(LANES)
        cell, count = lane // self.cy, self.cx * self.cy
        own = cell - 1
        extra = cell >= self.cx
        far_right = np.where(extra, 3 * bx - 1 + cell - self.cx, bx + own)
        far_left = np.where(extra, -2 * bx - 1 + cell - self.cx, own - bx)
        cells = [own, own, own + bx, own - bx, far_left, far_right, lane % self.cy - 1]
        cells += [np.where(lane < count, 0.0, FAR), np.where(cell < self.cx + 2, 0.0, FAR)]
        row = np.arange(self.out_cells)[:, None] + np.zeros((1, LANES))
        outs = np.stack([row // self.cy - 1, row % self.cy - 1, np.where(row < count, 0.0, FAR)])
        z_in, z_out = np.arange(self.window_rows) - GAUSSIAN_RIM, np.arange(LANES) - 1
        distance = z_in[:, None] - z_out[None, :]
        near = (np.abs(distance) <= REACH) & (np.arange(LANES) < self.out_z)[None, :]
        near = near & (np.arange(self.window_rows) < self.window)[:, None]
        squared = np.where(near, distance * distance, FAR)
        return padded(np.stack(cells), 16, LANES), outs.astype(np.float32), squared.astype(np.float32)

    def top_tables(self, kernels):
        four = [size // 16 for size in self.brick]
        lane = np.arange(2 * LANES)
        group, cell, partner = (lane % LANES) // self.group, lane % self.group, lane // LANES
        used = cell < self.top_x * self.top_y
        tables = []
        for axis in range(3):
            count, size = kernels[axis].shape[0], self.brick[axis] // 2
            whole = prolong_three_whole(count)
            outs = (self.cx, self.cy, self.out_z)[axis]
            spread, pick = [], []
            for place in range(self.counts[axis]):
                index = (place * size - 1 + np.arange(outs)) % (8 * count)
                spread.append(padded(whole[index], 16 if axis < 2 else LANES, 16))
                if axis == 0:
                    cells = (place ^ (group % 4)) * four[0] + cell // self.top_y - 1
                    valid = used
                elif axis == 1:
                    cells = (place ^ partner ^ (3 * (group // 4))) * four[1] + cell % self.top_y - 1
                    valid = used
                else:
                    row = np.arange(self.top_rows)
                    side, at = row // self.top_z, row % self.top_z
                    cells = (place ^ side) * four[2] + at - 1
                    valid = side < 2
                hot = (np.arange(count)[:, None] == (cells % count)[None, :]) & valid[None, :]
                hot = padded(hot, 16, cells.size)
                pick.append(hot if axis == 2 else hot.reshape(16, 2, LANES))
            tables += [np.stack(spread), np.stack(pick)]
        out = np.arange(self.out_cells)
        tables.append((out[:, None] // self.cy == np.arange(16)[None, :]).astype(np.float32))
        tables.append((out[:, None] % self.cy == np.arange(16)[None, :]).astype(np.float32))
        return tables

    def own_cells(self):
        lane = np.arange(LANES)
        return lane // self.half, lane % self.half


def fits(brick, counts, tops):
    bx, by, bz = brick
    return (
        counts == (4, 4, 2)
        and bx * (by // 2) == LANES
        and by % 16 == 0
        and bx % 16 == 0
        and bz == LANES
        and bx // 2 == REACH
        and by // 2 == REACH
        and (bx // 2 + 4) * (by // 2 + 2) <= LANES
        and (bx // 16 + 2) * (by // 16 + 2) <= 16
        and max(top.shape[0] for top in tops) <= 16
    )


def split(value):
    high = value.astype(BF16)
    return high, (value - high.astype(F32)).astype(BF16)


def dot(left, right):
    return jnp.dot(left, right, preferred_element_type=F32)


def dot_left(exact, value):
    high, low = split(value)
    return dot(exact, high) + dot(exact, low)


def dot_right(value, exact):
    high, low = split(value)
    return dot(high, exact) + dot(low, exact)


def dot_split(left, right):
    return dot(left[0], right[0]) + dot(left[1], right[0]) + dot(left[0], right[1])


def pick(flags_ref, axis, even, odd):
    return jnp.where(jnp.broadcast_to(flags_ref[axis : axis + 1], even.shape) < 0.5, even, odd)


def exact_tables(plan, ref):
    def read(name, rows, at=0):
        start = plan.starts[name] + at * rows
        return ref[start : start + rows].astype(BF16)

    return read


def lanes_of(rows):
    return lax.broadcasted_iota(jnp.int32, (rows, LANES), 1)


def halves(first, second):
    low = lanes_of(first.shape[0]) < LANES // 2
    return (
        jnp.where(low, first, pltpu.roll(second, LANES // 2, 1)),
        jnp.where(low, pltpu.roll(first, LANES // 2, 1), second),
    )


def start_kernel(plan, charges_ref, table_ref, own_ref, out_ref):
    _, _, bz = plan.brick
    rim, half = plan.rim, plan.half
    top, size = None, plan.sent_top
    left = split(table_ref[:size])
    for part in range(2):
        cells = charges_ref[:, part * half : (part + 1) * half, :].reshape(LANES, bz).T
        own_ref[part] = cells
        out_ref[2 * rim * part : 2 * rim * part + rim] = cells[:rim]
        out_ref[2 * rim * part + rim : 2 * rim * (part + 1)] = cells[bz - rim :]
        right = split(table_ref[size + LANES * part : size + LANES * (part + 1)])
        rows = dot_split(split(dot_split(left, split(cells))), right)
        top = rows if top is None else top + rows
    out_ref[4 * rim :] = top


def setup_kernel(count, *refs):
    copies = [pltpu.make_async_copy(refs[at], refs[count + at], refs[2 * count].at[at]) for at in range(count)]
    for copy in copies:
        copy.start()
    for copy in copies:
        copy.wait()


def spread_kernel(plan, flags_ref, own_ref, sent_ref, got_ref, table_ref, fine_ref, out_ref, side_x_ref,
                  side_y_ref):
    _, _, bz = plan.brick
    rim, rows = plan.rim, plan.fine_rows
    table = exact_tables(plan, table_ref)
    coarse = None
    for part in range(2):
        cells = own_ref[part]
        far = got_ref[2 * rim * part : 2 * rim * (part + 1)]
        fine_ref[part, :bz] = cells
        fine_ref[part, bz : bz + REACH] = far[2 * rim - REACH :]
        fine_ref[part, bz + REACH :] = far[:REACH]
        summed = dot_left(table("rest_left", plan.window_rows), cells)
        summed = summed + dot_left(table("rest_far", plan.window_rows)[:, : 2 * rim], far)
        summed = dot_right(summed, table("rest_right", LANES, part))
        coarse = summed if coarse is None else coarse + summed
    low, high = halves(fine_ref[0], fine_ref[1])
    out_ref[:rows] = pick(flags_ref, 0, high, low)
    side_x_ref[...] = pick(flags_ref, 0, low, high)
    side_y_ref[:rows] = pick(flags_ref, 1, fine_ref[0], fine_ref[1])
    side_y_ref[rows:] = coarse
    out_ref[rows : rows + plan.window_rows] = coarse
    top = rows + plan.window_rows
    cells = plan.top_z
    out_ref[top : top + cells] = sent_ref[4 * rim : 4 * rim + cells]
    out_ref[top + cells : top + 2 * cells] = got_ref[4 * rim : 4 * rim + cells]
    if plan.top_rows > 2 * cells:
        out_ref[top + 2 * cells :] = jnp.zeros((plan.top_rows - 2 * cells, LANES), F32)


def half_of(plan, flags_ref, strip_ref):
    rows = plan.fine_rows
    low, high = halves(strip_ref[: rows // 2], strip_ref[rows // 2 : rows])
    return pick(flags_ref, 1, low, high)


def pass_kernel(plan, flags_ref, sent_ref, got_ref, out_ref, side_ref):
    rows = plan.fine_rows
    own = sent_ref[rows : rows + plan.window_rows]
    far = got_ref[rows : rows + plan.window_rows]
    lane = lanes_of(plan.window_rows)
    edge, count = 2 * plan.cy, plan.cx * plan.cy
    last = count - edge
    beyond = (lane >= count) & (lane < count + edge)
    left = far + jnp.where(lane < edge, pltpu.roll(own, LANES - last, 1), 0.0)
    left = left + jnp.where(beyond, pltpu.roll(own, count, 1), 0.0)
    right = far + jnp.where((lane >= last) & (lane < count), pltpu.roll(own, last, 1), 0.0)
    right = right + jnp.where(beyond, pltpu.roll(own, edge, 1), 0.0)
    out_ref[: plan.window_rows] = pick(flags_ref, 0, left, right)
    top = rows + plan.window_rows
    out_ref[plan.window_rows :] = sent_ref[top:] + pltpu.roll(got_ref[top:], plan.group, 1)
    side_ref[: rows // 2] = half_of(plan, flags_ref, got_ref)
    side_ref[rows // 2 :] = far


def stack_kernel(plan, flags_ref, fine_ref, sent_ref, first_ref, side_ref, second_ref, cells_ref, out_ref):
    rows, window = plan.fine_rows, plan.window_rows
    low, high = halves(first_ref[:rows], side_ref[...])
    for part, other in ((0, low), (1, high)):
        cells_ref[part, :rows] = fine_ref[part]
        cells_ref[part, rows:] = other
    out_ref[: rows // 2] = half_of(plan, flags_ref, side_ref)
    out_ref[rows // 2 : rows // 2 + window] = second_ref[:window]
    out_ref[rows // 2 + window :] = sent_ref[window:] + pltpu.roll(second_ref[window:], 2 * plan.group, 1)


def turned(left, right):
    return lax.dot_general(left, right, (((1,), (1,)), ((), ())), preferred_element_type=F32)


def dot_turned(left, right):
    return turned(left[0], right[0]) + turned(left[1], right[0]) + turned(left[0], right[1])


def fine_weights_kernel(plan, terms, flags_ref, params_ref, table_ref, kf_ref, kf_low_ref, zf_ref, zf_low_ref):
    bx, by, _ = plan.brick
    cells_ref = table_ref.at[pl.ds(plan.starts["fine_cells"], 8)]
    dz_ref = table_ref.at[pl.ds(plan.starts["fine_dz"], plan.fine_rows)]
    half = plan.half
    own_x, own_y = cells_ref[0:1], cells_ref[1:2]
    far_x = pick(flags_ref, 0, cells_ref[2:3], cells_ref[3:4])
    x_out = lax.broadcasted_iota(jnp.int32, (bx, LANES), 0).astype(F32)
    y_out = lax.broadcasted_iota(jnp.int32, (half, LANES), 0).astype(F32)
    y_far = jnp.full((1, LANES), -half, F32)
    y_far = pick(flags_ref, 1, y_far, y_far + half + by)

    def decay(exponent, distance):
        return jnp.where(jnp.abs(distance) <= REACH, jnp.exp(-exponent * distance * distance), 0.0)

    for term in range(terms):
        exponent = params_ref[term : term + 1]
        scale = params_ref[terms + term : terms + term + 1]
        along_x = [decay(exponent, x_in - x_out)[:, None, :] for x_in in (own_x, far_x)]
        for group in range(3):
            y_in = own_y + (F32(group * half) if group < 2 else y_far)
            for part in range(2):
                along_y = decay(exponent, y_in - (y_out + part * half)) * scale
                for block in range(2):
                    high, low = split((along_x[block] * along_y[None]).reshape(bx * half, LANES))
                    rows, cols = pl.ds(part * LANES, LANES), pl.ds((2 * group + block) * LANES, LANES)
                    kf_ref[term, rows, cols] = high
                    kf_low_ref[term, rows, cols] = low
        zf_ref[term], zf_low_ref[term] = split(
            jnp.exp(-exponent * dz_ref[...]) * params_ref[2 * terms + term : 2 * terms + term + 1]
        )


def set_params(terms, exponents_ref, amplitudes_ref, tops, params_ref):
    offsets = lax.broadcasted_iota(jnp.int32, (1, LANES), 1).astype(F32) - REACH
    squared = jnp.where(offsets <= REACH, offsets * offsets, FAR)
    for level in range(2):
        for term in range(terms):
            at = slice(level, level + 1), slice(term, term + 1)
            exponent = exponents_ref[at]
            scale = 1.0 / jnp.sum(jnp.exp(-exponent * squared), axis=1, keepdims=True)
            row = 3 * terms * level + term
            for value in (exponent, scale * scale * amplitudes_ref[at], scale):
                params_ref[row : row + 1] = jnp.broadcast_to(value, (1, LANES))
                row = row + terms
    params_ref[6 * terms :] = jnp.zeros((3 * 16, LANES), F32)
    for axis, source in enumerate(tops):
        at, count = 6 * terms + 16 * axis, source.shape[0]
        params_ref[at : at + count, :count] = source[...]


def coarse_weights_kernel(plan, terms, flags_ref, table_ref, exponents_ref, amplitudes_ref, top_x_ref, top_y_ref,
                          top_z_ref, params_ref, k1_ref, k1_low_ref, z1_ref, z1_low_ref, zc_ref, kc_ref):
    set_params(terms, exponents_ref, amplitudes_ref, (top_x_ref, top_y_ref, top_z_ref), params_ref)
    cells_ref = table_ref.at[pl.ds(plan.starts["coarse_cells"], 16)]
    at, count = plan.starts["out_cells"], plan.out_cells
    out_cells_ref = [table_ref[at + count * part : at + count * (part + 1)] for part in range(3)]
    dz_ref = table_ref.at[pl.ds(plan.starts["coarse_dz"], plan.window_rows)]
    zc_ref[...], kc_ref[...] = top_weights(plan, terms, flags_ref, params_ref, table_ref)
    bx, by = plan.brick[0] // 2, plan.brick[1] // 2
    base = 3 * terms

    def squared(distance, count):
        distance = distance - count * jnp.floor((distance + count // 2) * (1.0 / count))
        return jnp.where(jnp.abs(distance) <= REACH, distance * distance, FAR)

    x_out, y_out = out_cells_ref[0], out_cells_ref[1]
    squares_x = []
    for slot in range(3):
        x_in = pick(flags_ref, 0, cells_ref[2 * slot : 2 * slot + 1], cells_ref[2 * slot + 1 : 2 * slot + 2])
        used = cells_ref[7:8] if slot < 2 else cells_ref[8:9]
        squares_x.append(squared(x_in - x_out, bx * plan.counts[0]) + used)
    toward = jnp.full((1, LANES), by, F32)
    toward = pick(flags_ref, 1, toward, -toward)
    for group, offset in enumerate((F32(0), -toward, F32(2 * by))):
        square_y = squared(cells_ref[6:7] + offset - y_out, by * plan.counts[1]) + out_cells_ref[2]
        for slot in range(3):
            total = squares_x[slot] + square_y
            cols = pl.ds((3 * group + slot) * LANES, LANES)
            for term in range(terms):
                exponent = params_ref[base + term : base + term + 1]
                scale = params_ref[base + terms + term : base + terms + term + 1]
                high, low = split(jnp.exp(-exponent * total) * scale)
                rows = pl.ds(term * plan.out_cells, plan.out_cells)
                k1_ref[rows, cols] = high
                k1_low_ref[rows, cols] = low
    for term in range(terms):
        exponent = params_ref[base + term : base + term + 1]
        scale = params_ref[base + 2 * terms + term : base + 2 * terms + term + 1]
        value = dot_right(jnp.exp(-exponent * dz_ref[...]) * scale, exact_tables(plan, table_ref)("back", LANES))
        z1_ref[term], z1_low_ref[term] = split(value)


def top_weights(plan, terms, flags_ref, params_ref, table_ref):
    def chain(*factors):
        value = factors[0]
        for factor in factors[1:]:
            value = dot_split(split(value), split(factor))
        return value

    def read(name, rows, axis=None, partner=0):
        start = plan.starts[name]
        if axis is None:
            return table_ref[start : start + rows]
        total, first = None, 3 + sum(plan.counts[:axis])
        for place in range(plan.counts[axis]):
            flag = flags_ref[first + (place ^ partner) : first + (place ^ partner) + 1]
            value = table_ref[start + rows * place : start + rows * (place + 1)] * flag
            total = value if total is None else total + value
        return total

    size = 16

    def along(axis, spread, chosen, partner=0):
        top = params_ref[6 * terms + size * axis : 6 * terms + size * (axis + 1)]
        value = chain(read(spread, size, axis, partner)[:, :size], top)[:, :size]
        return chain(value, read(chosen, size, axis, partner))

    lift_x, lift_y = (read(name, plan.out_cells)[:, :size] for name in ("lift_x", "lift_y"))
    along_x = chain(lift_x, along(0, "spread_x", "pick_x"))
    right = []
    for partner, chosen in enumerate(("pick_y", "pick_pair")):
        right.append(along_x * chain(lift_y, along(1, "spread_y", chosen, partner)))
    top = params_ref[6 * terms + 2 * size : 6 * terms + 3 * size]
    value = chain(read("spread_z", LANES, 2)[:, :size], top)[:, :size]
    left = chain(value, read("pick_z", size, 2)[:, : plan.top_rows])
    return dot_left(read("back_turned", LANES).astype(BF16), left), jnp.concatenate(right, axis=1)


def sum_fine(terms, blocks, refs, at):
    cells, cols = split(blocks), pl.ds(at * LANES, blocks.shape[1])
    return [dot_turned((refs[0][term, :, cols], refs[1][term, :, cols]), cells) for term in range(terms)]


def sum_coarse(blocks, refs, at):
    cols, count = pl.ds(at * LANES, blocks.shape[1]), blocks.shape[0]
    high = blocks.astype(BF16)
    exact = high.astype(F32)
    gap = jnp.zeros((LANES - count, blocks.shape[1]), F32)
    both = jnp.concatenate([exact, gap, blocks - exact], axis=0).astype(BF16)
    sums = turned(refs[0][:, cols], both)
    return sums[:, :count] + sums[:, LANES : LANES + count] + turned(refs[1][:, cols], high)


def fine_potential(fine, refs):
    total = None
    for term, value in enumerate(fine):
        value = dot_split(split(value), (refs[0][term], refs[1][term]))
        total = value if total is None else total + value
    return total


def coarse_potential(plan, terms, coarse, refs, top, kernel, table_ref):
    level_one = dot_turned(split(kernel), split(top))
    for term in range(terms):
        piece = split(coarse[term * plan.out_cells : (term + 1) * plan.out_cells])
        level_one = level_one + dot_split(piece, (refs[0][term], refs[1][term]))
    table = exact_tables(plan, table_ref)
    return dot_left(table("back_right", 2 * LANES)[:, : plan.out_cells], level_one)


def near_kernel(plan, terms, flags_ref, cells_ref, own_ref, first_ref, second_ref, side_ref, strip_ref, kf_ref,
                kf_low_ref, k1_ref, k1_low_ref, zf_ref, zf_low_ref, fine_ref, coarse_ref, give_fine_ref,
                give_coarse_ref):
    rows, window = plan.fine_rows, plan.window_rows
    kf, k1 = (kf_ref, kf_low_ref), (k1_ref, k1_low_ref)
    cells = [cells_ref[part, at : at + rows] for part in range(2) for at in (0, rows)]
    near = [own_ref[rows : rows + window], first_ref[rows : rows + window], second_ref[:window]]
    early = [side_ref[rows:], strip_ref[rows // 2 :]]
    other = [pick(flags_ref, 1, cells[2 + block], cells[block]) for block in range(2)]
    other = sum_fine(terms, jnp.concatenate(other, axis=1), kf, 4)
    give_fine_ref[...] = fine_potential(other, (zf_ref, zf_low_ref))
    give_coarse_ref[...] = sum_coarse(jnp.concatenate(near + early, axis=1), k1, 3)
    cells = jnp.concatenate(cells + [side_ref[:rows]], axis=1)
    for term, value in enumerate(sum_fine(terms, cells, kf, 0)):
        fine_ref[term] = value
    coarse_ref[...] = sum_coarse(jnp.concatenate(near + early, axis=1), k1, 0)


def top_charges(plan, sent_ref, got_ref, zc_ref):
    start = plan.fine_rows // 2 + plan.window_rows
    top = sent_ref[start:] + pltpu.roll(got_ref[start:], 4 * plan.group, 1)
    return dot_split(split(zc_ref[...]), split(top))


def last_cells(plan, got_ref):
    return got_ref[plan.fine_rows // 2 : plan.fine_rows // 2 + plan.window_rows]


def give_kernel(plan, terms, fine_ref, coarse_ref, sent_ref, got_ref, k1_ref, k1_low_ref, z1_ref, z1_low_ref,
                zc_ref, kc_ref, table_ref, out_ref):
    coarse = coarse_ref[...] + sum_coarse(last_cells(plan, got_ref), (k1_ref, k1_low_ref), 8)
    top = top_charges(plan, sent_ref, got_ref, zc_ref)
    out_ref[...] = fine_ref[...] + coarse_potential(
        plan, terms, coarse, (z1_ref, z1_low_ref), top, kc_ref[:, LANES:], table_ref
    )


def keep_kernel(plan, terms, fine_ref, coarse_ref, strip_ref, sent_ref, got_ref, kf_ref, kf_low_ref, k1_ref,
                k1_low_ref, zf_ref, zf_low_ref, z1_ref, z1_low_ref, zc_ref, kc_ref, table_ref, out_ref):
    half = plan.fine_rows // 2
    strips = jnp.concatenate(halves(strip_ref[:half], got_ref[:half]), axis=0)
    fine = sum_fine(terms, strips, (kf_ref, kf_low_ref), 5)
    fine = [fine_ref[term] + value for term, value in enumerate(fine)]
    coarse = coarse_ref[...] + sum_coarse(last_cells(plan, got_ref), (k1_ref, k1_low_ref), 5)
    top = top_charges(plan, sent_ref, got_ref, zc_ref)
    out_ref[...] = fine_potential(fine, (zf_ref, zf_low_ref)) + coarse_potential(
        plan, terms, coarse, (z1_ref, z1_low_ref), top, kc_ref[:, :LANES], table_ref
    )


def add_kernel(plan, own_ref, got_ref, out_ref):
    half = plan.half
    for part in range(2):
        rows = pl.ds(part * LANES, LANES)
        cells = own_ref[rows] + got_ref[rows]
        out_ref[:, part * half : (part + 1) * half, :] = cells.reshape(plan.brick[0], half, plan.brick[2])


def call(body, shapes, *operands, scalars=0, after=(), last=False, plain=False, copies=0):
    specs = [pl.BlockSpec(memory_space=pltpu.SMEM)] * scalars
    specs += [pl.BlockSpec(memory_space=pltpu.VMEM)] * (len(operands) - scalars)
    if copies:
        specs = [pl.BlockSpec(memory_space=pl.ANY)] * len(operands)
    specs += [pl.BlockSpec(memory_space=pl.ANY)] * len(after)

    def keep(operand, space=pltpu.VMEM):
        return pltpu.with_memory_space_constraint(operand, space)

    if plain:
        operands = tuple(keep(operand, pltpu.HBM) for operand in operands)
    kept = list(operands) if plain else [keep(operand) for operand in operands[scalars:]]
    kept = kept[scalars:] if plain else kept
    kept += [keep(operand) for operand in after]
    kinds = [shape if isinstance(shape[-1], int) else shape[0] for shape in shapes]
    types = [F32 if isinstance(shape[-1], int) else shape[1] for shape in shapes]
    first = len(operands)

    def run(*refs):
        body(*refs[:first], *refs[first + len(after) :])

    return pl.pallas_call(
        run,
        out_shape=[
            jax.ShapeDtypeStruct(kind, kept_as) if last else pltpu.VMEM(kind, kept_as)
            for kind, kept_as in zip(kinds, types)
        ],
        in_specs=specs,
        out_specs=[pl.BlockSpec(memory_space=pltpu.VMEM)] * len(shapes),
        scratch_shapes=[pltpu.SemaphoreType.DMA((copies,))] if copies else (),
        compiler_params=pltpu.CompilerParams(vmem_limit_bytes=8 << 20),
    )(*(operands[:scalars] if plain else [keep(operand, pltpu.SMEM) for operand in operands[:scalars]]), *kept)


def pair(value, axis, bits):
    count = lax.axis_size(axis)
    return lax.ppermute(value, axis, [(i, i ^ bits) for i in range(count)])


def local_short(plan, charges, exponents, amplitudes, top_x, top_y, top_z):
    row = lax.broadcasted_iota(jnp.int32, (3 + sum(plan.counts), LANES), 0)
    flags, first = jnp.zeros(row.shape, F32), 3
    for axis, name in enumerate(("gx", "gy", "gz")):
        place = lax.axis_index(name).astype(jnp.int32)
        flags = jnp.where(row == axis, (place % 2).astype(F32), flags)
        flags = jnp.where(row == first + place, 1.0, flags)
        first = first + plan.counts[axis]
    terms = exponents.shape[1]
    bx, by, bz = plan.brick
    rows, window = plan.fine_rows, plan.window_rows
    bind = functools.partial

    own, sent_z = call(
        bind(start_kernel, plan),
        [(2, bz, LANES), (4 * plan.rim + plan.sent_top, LANES)],
        charges,
        jnp.asarray(np.concatenate([plan.top_left, *plan.top_right])),
        plain=True,
    )
    got_z = pair(sent_z, "gz", 1)
    held = (jnp.asarray(plan.constants((top_x, top_y, top_z))), exponents, amplitudes, top_x, top_y, top_z)
    table, *small = call(
        bind(setup_kernel, len(held)),
        [array.shape for array in held],
        *held,
        after=(sent_z,),
        plain=True,
        copies=len(held),
    )
    fine, sent_a, side_x, side_y = call(
        bind(spread_kernel, plan),
        [(2, rows, LANES), (plan.message, LANES), (rows, LANES), (rows + window, LANES)],
        flags,
        own,
        sent_z,
        got_z,
        table,
    )
    got_a = pair(sent_a, "gx", 1)
    got_x = pair(side_x, "gx", 3)
    got_y = pair(side_y, "gy", 3)
    sent_b, side_b = call(
        bind(pass_kernel, plan),
        [(plan.message - rows, LANES), (rows // 2 + window, LANES)],
        flags,
        sent_a,
        got_a,
    )
    got_b = pair(sent_b, "gx", 2)
    got_s = pair(side_b, "gy", 3)
    k1 = ((terms * plan.out_cells, 9 * LANES), BF16)
    params, *k1, z1, z1_low, zc, kc = call(
        bind(coarse_weights_kernel, plan, terms),
        [
            (6 * terms + 3 * 16, LANES),
            k1,
            k1,
            ((terms, window, LANES), BF16),
            ((terms, window, LANES), BF16),
            (LANES, plan.top_rows),
            (plan.out_cells, 2 * LANES),
        ],
        flags,
        table,
        *small,
        after=(sent_b,),
    )
    kf = ((terms, 2 * LANES, 6 * LANES), BF16)
    *kf, zf, zf_low = call(
        bind(fine_weights_kernel, plan, terms),
        [kf, kf, ((terms, rows, LANES), BF16), ((terms, rows, LANES), BF16)],
        flags,
        params,
        table,
        after=(sent_b,),
    )
    size = rows // 2 + window + plan.top_rows
    cells, sent_c = call(
        bind(stack_kernel, plan),
        [(2, 2 * rows, LANES), (size, LANES)],
        flags,
        fine,
        sent_b,
        got_a,
        got_x,
        got_b,
        after=(z1, zf, got_y, got_s),
    )
    got_c = pair(sent_c, "gy", 3)
    give = (2 * LANES, bz)
    fine_sum, coarse_sum, give_fine, give_coarse = call(
        bind(near_kernel, plan, terms),
        [(terms, 2 * LANES, rows), (terms * plan.out_cells, window), give, (terms * plan.out_cells, window)],
        flags,
        cells,
        sent_a,
        got_a,
        got_b,
        got_y,
        got_s,
        *kf,
        *k1,
        zf,
        zf_low,
        after=(sent_c,),
    )
    ends = (z1, z1_low, zc, kc, table)
    (sent_d,) = call(
        bind(give_kernel, plan, terms), [give], give_fine, give_coarse, sent_c, got_c, *k1, *ends
    )
    got_d = pair(sent_d, "gy", 1)
    (kept,) = call(
        bind(keep_kernel, plan, terms),
        [give],
        fine_sum,
        coarse_sum,
        got_s,
        sent_c,
        got_c,
        *kf,
        *k1,
        zf,
        zf_low,
        *ends,
        after=(sent_d,),
    )
    (out,) = call(bind(add_kernel, plan), [(bx, by, bz)], kept, got_d, last=True)
    return out


def local(*arguments):
    counts = tuple(lax.axis_size(axis) for axis in ("gx", "gy", "gz"))
    brick = arguments[0].shape
    if fits(brick, counts, arguments[3:]):
        return local_short(Plan(brick, counts), *arguments)
    return local_any(*arguments)


def solution(mesh):
    in_specs = (P("gx", "gy", "gz"), P(), P(), P(), P(), P())
    out_specs = P("gx", "gy", "gz")
    return jax.shard_map(local, mesh=mesh, in_specs=in_specs, out_specs=out_specs, check_vma=False)
```
